256 devices in a mesh: seq: 16 (over x_hi, y, core), tp: 16 (over z, x_lo).
Axes of the slice: x: 4 (x_hi: 2, x_lo: 2; x = x_hi * 2 + x_lo), y: 4, z: 8, core: 2. Of those that a mesh axis runs over, the one named last changes fastest.
Arguments:
- hidden: bfloat16 [12288, 8192], P('seq', 'tp'), may hold values from -6 to 6
- cotangent: bfloat16 [12288, 8192], P('seq', 'tp'), may hold values from -0.59765625 to 0.59765625
- router_gate: bfloat16 [12288], P('seq'), may hold values from 0.25 to 1
- recursion_depth: int32 [12288], P('seq'), may hold values from 1 to 4
- live_counts: int32 [16], replicated, may hold values from 0 to 768, as said below
- out_weight: bfloat16 [8192, 8192], P(None, 'tp'), may hold values from -0.0625 to 0.0625
- adapter_down: bfloat16 [8192, 1024], P('tp', 'seq'), may hold values from -0.0625 to 0.0625
- adapter_up: bfloat16 [1024, 8192], P('seq', 'tp'), may hold values from -0.375 to 0.375
Outputs:
- hidden_grad: float32 [12288, 8192], P('seq', 'tp')
- gate_grad: float32 [12288], P('seq')
- weight_grad: float32 [8192, 8192], P('seq', 'tp')
- down_grad: float32 [1024, 8192], P('seq', 'tp')
- up_grad: float32 [1024, 8192], P('seq', 'tp')
The draws below stay inside these ranges and needn't reach their ends.
Inputs may be any that keep to these rules, and one draw needn't show every extreme that they name: `live_counts`: each entry is a multiple of 128; the entries sum to 6144; the largest entry equals 768. Rows at or past an index's count are not live.
All inputs are finite; a program needn't handle non-finite values.
Results may differ from the reference program's by a relative error of at most 0.0055.
Values may be sent and summed in bfloat16 or wider, within the bound.
A program may use at most 192 MiB of HBM per device.

```python
import jax
import jax.numpy as jnp

D = 8192
RANK = 256
NREC = 4
BLOCK = 128
BAL = 384
CAP = 768
SLOTS = 12288
N_SEQ = 16


def draw_live_counts(key, part):
    block_mean = BAL // BLOCK
    carried = jax.random.randint(jax.random.fold_in(key, 11), (N_SEQ,), 0, block_mean + 1)
    carried = carried.at[0].set(block_mean).at[N_SEQ - 1].set(0)
    in_blocks = block_mean + carried - jnp.roll(carried, 1)
    placing = jax.random.permutation(jax.random.fold_in(key, 12), N_SEQ)
    placed = jnp.zeros((N_SEQ,), jnp.int32).at[placing].set(in_blocks.astype(jnp.int32))
    return (placed * BLOCK).astype(jnp.int32)


def touch_ends(drawn, rng, low, top_value):
    longest = drawn.shape.index(max(drawn.shape))
    spots = []
    for shift in (0, 1):
        where = [jax.random.randint(jax.random.fold_in(rng, axis), (), 0, length) for axis, length in enumerate(drawn.shape)]
        where[longest] = (where[longest] + shift) % drawn.shape[longest]
        spots.append(tuple(where))
    return drawn.at[spots[0]].set(low).at[spots[1]].set(top_value)


def block_levels(rng, shape, pieces, smallest, high):
    level, own = 1.0, jax.random.fold_in(rng, 6)
    for axis_at, shards_of in pieces:
        steps = jnp.exp(jax.random.uniform(jax.random.fold_in(own, axis_at), (shards_of,), jnp.float32, smallest / len(pieces), high / len(pieces)))
        level = level * jnp.repeat(steps, shape[axis_at] // shards_of).reshape([-1 if axis == axis_at else 1 for axis in range(len(shape))])
    return level


def bell_draw(own_key, extent, scale, limit, cuts=(), held_as=jnp.bfloat16):
    array = scale * jax.random.normal(own_key, extent, jnp.float32)
    if cuts:
        array = array * block_levels(own_key, extent, cuts, -0.22, 0.18)
    return jnp.clip(array, -limit, limit).astype(held_as)


def setup_inputs(seed: int = 0) -> dict:
    key_list = jax.random.split(jax.random.key(seed), 9)
    hidden = bell_draw(key_list[0], (SLOTS, D), 1.0, 6.0, ((0, 16), (1, 16)))
    cotangent = bell_draw(key_list[1], (SLOTS, D), 0.1, 0.59765625, ((0, 16), (1, 16)))
    router_gate = jnp.clip(0.25 + 0.75 * jax.random.uniform(key_list[2], (SLOTS,), jnp.float32) ** block_levels(key_list[2], (SLOTS,), ((0, 16),), -0.2, 0.2), 0.25, 1.0).astype(jnp.bfloat16)
    recursion_depth = touch_ends(jax.random.randint(key_list[3], (SLOTS,), 1, 5), jax.random.fold_in(key_list[3], 1), 1, 4).astype(jnp.int32)
    live_counts = draw_live_counts(jax.random.fold_in(key_list[8], 71), 0)
    out_weight = bell_draw(key_list[5], (D, D), D ** -0.5, 0.0625, ((1, 16),))
    adapter_down = bell_draw(key_list[6], (D, NREC * RANK), D ** -0.5, 0.0625, ((0, 16), (1, 16)))
    adapter_up = bell_draw(key_list[7], (NREC * RANK, D), RANK ** -0.5, 0.375, ((0, 16), (1, 16)))
    return dict(hidden=hidden, cotangent=cotangent, router_gate=router_gate, recursion_depth=recursion_depth, live_counts=live_counts, out_weight=out_weight, adapter_down=adapter_down, adapter_up=adapter_up)


adapter_scale = 0.5


def reference(hidden, cotangent, router_gate, recursion_depth, live_counts, out_weight, adapter_down, adapter_up):
    total_live = N_SEQ * BAL
    finish = jnp.cumsum(live_counts).astype(jnp.int32)
    starts_at = (finish - live_counts).astype(jnp.int32)
    rank_slots = jnp.arange(total_live, dtype=jnp.int32)
    source = jnp.sum((finish[None, :] <= rank_slots[:, None]).astype(jnp.int32), axis=1).astype(jnp.int32)
    shard_ids = jnp.arange(N_SEQ, dtype=jnp.int32)
    begin_at = jnp.sum(jnp.where(source[:, None] == shard_ids[None, :], starts_at[None, :], 0), axis=1).astype(jnp.int32)
    row_index = (source * CAP + rank_slots - begin_at).astype(jnp.int32)
    rows_h = jnp.take(hidden, row_index, axis=0)
    rows_dy = jnp.take(cotangent, row_index, axis=0)
    gate_rows = jnp.take(router_gate, row_index).astype(jnp.float32)
    depths = jnp.take(recursion_depth, row_index).astype(jnp.int32)
    levels = jnp.arange(1, NREC + 1, dtype=jnp.int32)
    selector = (depths[:, None] == levels[None, :]).astype(jnp.float32)
    down_all = jnp.dot(rows_h, adapter_down, preferred_element_type=jnp.float32)
    down_proj = jnp.sum(down_all.reshape(total_live, NREC, RANK) * selector[:, :, None], axis=1)
    up_all = jnp.dot(rows_dy, adapter_up.T, preferred_element_type=jnp.float32)
    up_back = adapter_scale * jnp.sum(up_all.reshape(total_live, NREC, RANK) * selector[:, :, None], axis=1)
    wide_back = (selector[:, :, None] * up_back[:, None, :]).reshape(total_live, NREC * RANK)
    wide_down = (selector[:, :, None] * down_proj[:, None, :]).reshape(total_live, NREC * RANK)
    pre_grad = jnp.dot(rows_dy, out_weight, preferred_element_type=jnp.float32)
    pre_grad = pre_grad + jnp.dot(wide_back.astype(jnp.bfloat16), adapter_down.T, preferred_element_type=jnp.float32)
    row_grad = gate_rows[:, None] * pre_grad
    gate_row = jnp.sum(rows_h.astype(jnp.float32) * pre_grad, axis=1)
    hidden_grad = jnp.zeros((N_SEQ * CAP, D), jnp.float32).at[row_index].set(row_grad)
    gate_grad = jnp.zeros((N_SEQ * CAP,), jnp.float32).at[row_index].set(gate_row)
    gated_dy = (gate_rows[:, None] * rows_dy.astype(jnp.float32)).astype(jnp.bfloat16)
    weight_grad = jnp.dot(gated_dy.T, rows_h, preferred_element_type=jnp.float32)
    back_gated = (gate_rows[:, None] * wide_back).astype(jnp.bfloat16)
    down_grad = jnp.dot(back_gated.T, rows_h, preferred_element_type=jnp.float32)
    down_gated = (gate_rows[:, None] * adapter_scale * wide_down).astype(jnp.bfloat16)
    up_grad = jnp.dot(down_gated.T, rows_dy, preferred_element_type=jnp.float32)
    return hidden_grad, gate_grad, weight_grad, down_grad, up_grad
```

```python
import jax
import jax.numpy as jnp
from jax import lax
from jax.experimental import pallas as pl
from jax.experimental.pallas import tpu as pltpu
from jax.sharding import PartitionSpec as P

NREC = 4
BLOCK = 128
GROUP = 16
CHIPS = 8
LEVELS = 6
GROUPS = 48
ROWS = GROUPS * GROUP
RING = 8
HALF = GROUPS // 2
WIDTH = 512
RANK = 256
PART = 48
PEERS = 16
VMEM_LIMIT = 60 * 1024 * 1024

contract_rows = (((0,), (0,)), ((), ()))
contract_last = (((1,), (1,)), ((), ()))
bf16 = jnp.bfloat16
f32 = jnp.float32


def local_kernel(
    pick_ref, place_ref, alive_ref, target_ref,
    cot_ref, hid_ref, rid_ref, up_ref, down_ref, w_ref,
    hg_out, gg_out, wg_out, dg_out, ug_out,
    recv_rows, recv_rid, rows, rid, hid, gated_hid, ring, weights, pre,
    w_send, w_recv, maps, part_send, part_recv, part_sum, proj, wide,
    g_send, g_recv, x_send, x_recv, h_send, h_recv,
    gate_part, gate_recv, gate_slots, gate_back,
    in_sem, w_sem, ring_send, ring_recv, hid_sem, p_sem, wg_send, wg_recv,
    gr_sem, x_ssem, x_rsem, hr_sem, gate_sem,
):
    s = lax.axis_index("seq")
    t = lax.axis_index("tp")
    core = s % 2
    chip = s // 2
    z = t // 2
    xl = t % 2
    is_cot = core == xl
    kind = (core + xl) % 2

    def remote(src, dst, ssem, rsem, seq, tp):
        return pltpu.make_async_remote_copy(
            src_ref=src, dst_ref=dst, send_sem=ssem, recv_sem=rsem,
            device_id={"seq": seq, "tp": tp}, device_id_type=pl.DeviceIdType.MESH,
        )

    def wait_bytes(ref, sem):
        pltpu.make_async_copy(ref, ref, sem).wait()

    def load_weights(j, c):
        start = pl.multiple_of((2 * j + core) * WIDTH, WIDTH)
        pltpu.make_async_copy(w_ref.at[pl.ds(start, WIDTH)], weights.at[j], w_sem.at[j]).start()
        return c
    lax.fori_loop(0, RING, load_weights, 0)

    barrier = pltpu.get_barrier_semaphore()

    def greet_seq(i, c):
        pl.semaphore_signal(barrier, inc=1, device_id={"seq": (s + i) % 16, "tp": t},
                            device_id_type=pl.DeviceIdType.MESH)
        return c
    lax.fori_loop(1, 16, greet_seq, 0)

    def greet_tp(i, c):
        for other in range(2):
            pl.semaphore_signal(barrier, inc=1, device_id={"seq": 2 * chip + other, "tp": (t + i) % 16},
                                device_id_type=pl.DeviceIdType.MESH)
        return c
    lax.fori_loop(1, 16, greet_tp, 0)
    pl.semaphore_wait(barrier, 45)

    def give(src, dst, sem_out, sem_in, seq):
        @pl.when(seq == s)
        def _():
            pltpu.make_async_copy(src, dst, sem_in).start()

        @pl.when(seq != s)
        def _():
            remote(src, dst, sem_out, sem_in, seq, t).start()

    my_slots = pl.ds(s * LEVELS, LEVELS)

    def send_first(i, c):
        d = (chip + i) % CHIPS
        give(cot_ref.at[:, d], recv_rows.at[my_slots], in_sem.at[0], in_sem.at[1], 2 * d + xl)
        for other in range(2):
            give(rid_ref.at[:, d], recv_rid.at[my_slots], in_sem.at[2], in_sem.at[3], 2 * d + other)
        return c
    lax.fori_loop(0, CHIPS, send_first, 0)

    def send_second(i, c):
        d = (chip + i) % CHIPS
        give(hid_ref.at[:, d], recv_rows.at[my_slots], in_sem.at[0], in_sem.at[1], 2 * d + 1 - xl)
        return c
    lax.fori_loop(0, CHIPS, send_second, 0)

    def send_maps(i, c):
        d = (chip + i) % CHIPS
        give(up_ref, maps.at[s], in_sem.at[4], in_sem.at[5], 2 * d + xl)
        give(down_ref, maps.at[s], in_sem.at[4], in_sem.at[5], 2 * d + 1 - xl)
        return c
    lax.fori_loop(0, CHIPS, send_maps, 0)

    right = 2 * ((z + 1) % RING) + xl
    left = 2 * ((z + RING - 1) % RING) + xl
    across = 2 * z + 1 - xl
    partner = 2 * chip + 1 - core

    def half(h):
        return pl.ds(h * HALF, HALF)

    def to_right(src, slot, h):
        return remote(src, ring.at[slot, half(h)], ring_send.at[slot, h], ring_recv.at[slot, h], s, right)

    def to_left(src, slot, h):
        return remote(src, ring.at[slot, half(h)], ring_send.at[slot, h], ring_recv.at[slot, h], s, left)

    def to_across(h):
        return remote(ring.at[0, half(h)], ring.at[0, half(h)], ring_send.at[0, h], ring_recv.at[0, h], s, across)

    def to_partner():
        return remote(hid, hid, hid_sem.at[0], hid_sem.at[1], partner, t)

    @pl.when(is_cot)
    def _():
        wait_bytes(recv_rows, in_sem.at[1])

        def pack(g, c):
            value = recv_rows[pick_ref[g]]
            rows[g] = value
            ring[0, g] = value
            return c
        lax.fori_loop(0, GROUPS, pack, 0)
        for h in range(2):
            to_across(h).start()
            to_right(ring.at[0, half(h)], 1, h).start()
            to_left(ring.at[0, half(h)], 2, h).start()

    @pl.when(jnp.logical_not(is_cot))
    def _():
        for h in range(2):
            wait_bytes(ring.at[0, half(h)], ring_recv.at[0, h])
            to_right(ring.at[0, half(h)], 1, h).start()
            to_left(ring.at[0, half(h)], 2, h).start()
        wait_bytes(recv_rows, in_sem.at[1])

        def pack(g, c):
            value = recv_rows[pick_ref[g]]
            rows[g] = value
            hid[g] = value
            return c
        lax.fori_loop(0, GROUPS, pack, 0)
        to_partner().start()

    wait_bytes(recv_rid, in_sem.at[3])

    def pack_rid(g, c):
        rid[g] = recv_rid[pick_ref[g]]
        return c
    lax.fori_loop(0, GROUPS, pack_rid, 0)

    wait_bytes(maps, in_sem.at[5])

    def project(r, c):
        groups = pl.ds(r * GROUP, GROUP)
        x = rows[groups].reshape(RANK, WIDTH)
        y = lax.dot_general(x, maps[...].reshape(NREC * RANK, WIDTH), contract_last, preferred_element_type=f32)
        depth = rid[groups].reshape(RANK, BLOCK)[:, 64:65].astype(f32)
        total = jnp.zeros((RANK, RANK), f32)
        for d in range(NREC):
            total = total + jnp.where(depth == d + 1.0, y[:, d * RANK:(d + 1) * RANK], 0.0)
        part_send[pl.ds(r * RANK, RANK)] = total.astype(bf16)
        return c
    lax.fori_loop(0, ROWS // RANK, project, 0)

    def same_kind(t2):
        return 2 * chip + (core + xl + t2) % 2

    def send_part(i, c):
        t2 = (t + i) % PEERS
        remote(part_send.at[pl.ds(t2 * PART, PART)], part_recv.at[t], p_sem.at[0], p_sem.at[1],
               same_kind(t2), t2).start()
        return c
    lax.fori_loop(1, PEERS, send_part, 0)
    pltpu.make_async_copy(part_send.at[pl.ds(t * PART, PART)], part_recv.at[t], p_sem.at[1]).start()

    @pl.when(is_cot)
    def _():
        wait_bytes(hid, hid_sem.at[1])

    def apply_gate(g, c):
        gate = rid[g][:, 0:1].astype(f32)
        gated_hid[g] = (gate * hid[g].astype(f32)).astype(bf16)
        rows[g] = (gate * rows[g].astype(f32)).astype(bf16)
        return c
    lax.fori_loop(0, GROUPS, apply_gate, 0)
    pre[...] = jnp.zeros_like(pre)

    def step(i, c):
        @pl.when(jnp.logical_and(i % 2 == 1, i < RING - 1))
        def _():
            for h in range(2):
                wait_bytes(ring.at[i, half(h)], ring_recv.at[i, h])

                @pl.when(jnp.logical_or(i < 5, h == 0))
                def _():
                    to_right(ring.at[i, half(h)], i + 2, h).start()
                wait_bytes(ring.at[i + 1, half(h)], ring_recv.at[i + 1, h])

                @pl.when(i < 5)
                def _():
                    to_left(ring.at[i + 1, half(h)], i + 3, h).start()
                if h == 1:
                    @pl.when(i == 5)
                    def _():
                        to_left(ring.at[6, half(h)], 7, h).start()

        @pl.when(i == RING - 1)
        def _():
            for h in range(2):
                wait_bytes(ring.at[RING - 1, half(h)], ring_recv.at[RING - 1, h])

        @pl.when(i == 1)
        def _():
            wait_bytes(part_recv, p_sem.at[1])
            part_sum[...] = jnp.sum(part_recv[...].astype(f32), axis=0).astype(bf16)

            def send_sum(j, c):
                t2 = (t + j) % PEERS
                remote(part_sum, proj.at[t], p_sem.at[2], p_sem.at[3],
                       4 * chip + 1 - same_kind(t2), t2).start()
                return c
            lax.fori_loop(0, PEERS, send_sum, 0)

        @pl.when(i == 3)
        def _():
            wait_bytes(proj, p_sem.at[3])
            flat = proj[...].reshape(ROWS, RANK)
            depth = rid[...].reshape(ROWS, BLOCK)[:, 64:65].astype(f32)
            for d in range(NREC):
                wide[:, d * RANK:(d + 1) * RANK] = jnp.where(
                    depth == d + 1.0, 0.5 * flat.astype(f32), 0.0).astype(bf16)

            @pl.when(jnp.logical_not(is_cot))
            def _():
                def add_adapter(r, c):
                    groups = pl.ds(r * GROUP, GROUP)
                    term = jnp.dot(wide[pl.ds(r * RANK, RANK)], maps[...].reshape(NREC * RANK, WIDTH),
                                   preferred_element_type=f32)
                    pre[groups] = pre[groups] + term.reshape(GROUP, GROUP, WIDTH)
                    return c
                lax.fori_loop(0, ROWS // RANK, add_adapter, 0)

            for q in range(NREC):
                grad = lax.dot_general(wide[:, q * RANK:(q + 1) * RANK], rows[...].reshape(ROWS, WIDTH),
                                       contract_rows, preferred_element_type=f32)
                g_send[q * 4:(q + 1) * 4] = grad.astype(bf16).reshape(4, 64, WIDTH)

            def send_grad(j, c):
                to = (s + j) % 16
                remote(g_send.at[to], g_recv.at[kind, chip], gr_sem.at[0], gr_sem.at[1], to, t).start()
                return c
            lax.fori_loop(1, 16, send_grad, 0)
            pltpu.make_async_copy(g_send.at[s], g_recv.at[kind, chip], gr_sem.at[1]).start()

        shift = jnp.where(i % 2 == 1, 2 * RING - (i + 1) // 2, i // 2)
        origin = (z + shift) % RING
        pltpu.make_async_copy(w_ref.at[pl.ds(0, WIDTH)], weights.at[origin], w_sem.at[origin]).wait()
        block = ring[i].reshape(ROWS, WIDTH)
        pre[...] = pre[...] + jnp.dot(
            block, weights[origin], preferred_element_type=f32).reshape(GROUPS, GROUP, WIDTH)
        w_send[i] = lax.dot_general(
            block, gated_hid[...].reshape(ROWS, WIDTH), contract_rows, preferred_element_type=f32).astype(bf16)
        give(w_send.at[i], w_recv.at[chip], wg_send, wg_recv, 2 * origin + core)
        return c
    lax.fori_loop(0, RING, step, 0)

    ones = jnp.ones((8, WIDTH), bf16)
    for r in range(ROWS // RANK):
        groups = slice(r * GROUP, (r + 1) * GROUP)
        prod = pre[groups].reshape(RANK, WIDTH) * hid[groups].reshape(RANK, WIDTH).astype(f32)
        high = prod.astype(bf16)
        low = (prod - high.astype(f32)).astype(bf16)
        lanes = lax.dot_general(ones, high, contract_last, preferred_element_type=f32)
        lanes = lanes + lax.dot_general(ones, low, contract_last, preferred_element_type=f32)
        gate_part[:, r * RANK:(r + 1) * RANK] = lanes[0:1]
    me = 2 * t + core

    def send_gate(j, c):
        t2 = (t + j) % PEERS
        for other in range(2):
            remote(gate_part, gate_recv.at[me], gate_sem.at[0], gate_sem.at[1], 2 * chip + other, t2).start()
        return c
    lax.fori_loop(1, PEERS, send_gate, 0)
    remote(gate_part, gate_recv.at[me], gate_sem.at[0], gate_sem.at[1], partner, t).start()
    pltpu.make_async_copy(gate_part, gate_recv.at[me], gate_sem.at[1]).start()

    def slot_rows(slot):
        gate = recv_rid[slot][:, 0:1].astype(f32)
        return jnp.where(alive_ref[slot] > 0, gate * pre[place_ref[slot]], 0.0)

    def to_other(d):
        return remote(x_send.at[d], x_recv.at[d], x_ssem.at[d], x_rsem.at[d], partner, t)

    def expand(i, c):
        d = (chip + i) % CHIPS

        def one(j, c):
            x_send[d, j] = slot_rows((2 * d + 1 - core) * LEVELS + j).astype(bf16)
            return c
        lax.fori_loop(0, LEVELS, one, 0)
        to_other(d).start()
        return c
    lax.fori_loop(0, CHIPS, expand, 0)

    def give_back(i, c):
        d = (chip + i) % CHIPS
        wait_bytes(x_recv.at[d], x_rsem.at[d])

        def one(j, c):
            value = slot_rows((2 * d + core) * LEVELS + j) + x_recv[d, j].astype(f32)
            h_send[d, j] = value.astype(bf16)
            return c
        lax.fori_loop(0, LEVELS, one, 0)
        give(h_send.at[d], h_recv.at[chip], hr_sem.at[0], hr_sem.at[1], 2 * d + core)
        return c
    lax.fori_loop(0, CHIPS, give_back, 0)

    wait_bytes(gate_recv, gate_sem.at[1])
    total = jnp.sum(gate_recv[...], axis=0)
    spot = target_ref[core]
    pick = (lax.broadcasted_iota(jnp.int32, (ROWS, CHIPS * BLOCK), 0) == spot).astype(f32).astype(bf16)
    placed = jnp.zeros((8, CHIPS * BLOCK), f32)
    rest = total
    for _ in range(3):
        piece = rest.astype(bf16)
        rest = rest - piece.astype(f32)
        placed = placed + jnp.dot(jnp.broadcast_to(piece, (8, ROWS)), pick, preferred_element_type=f32)
    for d in range(CHIPS):
        gate_slots[d] = placed[0:1, d * BLOCK:(d + 1) * BLOCK]

    def send_slots(i, c):
        d = (chip + i) % CHIPS
        give(gate_slots.at[d], gate_back.at[chip], gate_sem.at[2], gate_sem.at[3], 2 * d + core)
        return c
    lax.fori_loop(0, CHIPS, send_slots, 0)

    wait_bytes(g_recv, gr_sem.at[1])
    ug_out[...] = jnp.sum(g_recv[0].astype(f32), axis=0)
    dg_out[...] = jnp.sum(g_recv[1].astype(f32), axis=0)
    wait_bytes(w_recv, wg_recv)

    def add_up(r, c):
        part = pl.ds(r * 64, 64)
        wg_out[part] = jnp.sum(w_recv[:, part].astype(f32), axis=0)
        return c
    lax.fori_loop(0, 8, add_up, 0)
    wait_bytes(h_recv, hr_sem.at[1])
    for d in range(CHIPS):
        hg_out[:, d] = h_recv[d].astype(f32)
    wait_bytes(gate_back, gate_sem.at[3])
    gg_out[...] = gate_back[...]

    wait_bytes(recv_rows.at[pl.ds(0, 15 * LEVELS)], in_sem.at[0])
    wait_bytes(recv_rid.at[pl.ds(0, 15 * LEVELS)], in_sem.at[2])
    wait_bytes(maps.at[pl.ds(0, 15)], in_sem.at[4])

    @pl.when(is_cot)
    def _():
        for h in range(2):
            to_across(h).wait_send()

    @pl.when(jnp.logical_not(is_cot))
    def _():
        to_partner().wait_send()
    for h in range(2):
        for slot in range(1, 7):
            to_right(ring.at[slot, half(h)], slot, h).wait_send()
        to_right(ring.at[7, half(h)], 7, h).wait_send()
    wait_bytes(part_recv.at[pl.ds(0, 15)], p_sem.at[0])
    wait_bytes(proj, p_sem.at[2])
    wait_bytes(g_send.at[pl.ds(0, 15)], gr_sem.at[0])
    wait_bytes(w_send.at[pl.ds(0, 7)], wg_send)
    for d in range(CHIPS):
        to_other(d).wait_send()
    wait_bytes(h_send.at[pl.ds(0, 7)], hr_sem.at[0])
    wait_bytes(gate_recv.at[pl.ds(0, 31)], gate_sem.at[0])
    wait_bytes(gate_slots.at[pl.ds(0, 7)], gate_sem.at[2])


def local(hidden, cotangent, router_gate, recursion_depth, live_counts, out_weight, adapter_down, adapter_up):
    blocks = live_counts // BLOCK
    finish = jnp.cumsum(blocks)
    begin = finish - blocks
    level = jnp.arange(LEVELS, dtype=jnp.int32)
    alive = level[None, :] < blocks[:, None]
    place = jnp.where(alive, begin[:, None] + level[None, :], 0)
    order = jnp.arange(GROUPS, dtype=jnp.int32)
    source = jnp.sum((finish[None, :] <= order[:, None]).astype(jnp.int32), axis=1)
    shard = jnp.arange(16, dtype=jnp.int32)
    first = jnp.sum(jnp.where(source[:, None] == shard[None, :], begin[None, :], 0), axis=1)
    pick = source * LEVELS + order - first
    inside = jnp.arange(GROUP, dtype=jnp.int32)
    target = jnp.where(alive[:, :, None], place[:, :, None] * GROUP + inside, -1)
    target = target.reshape(CHIPS, 2, LEVELS * GROUP).transpose(1, 0, 2)
    target = jnp.pad(target, ((0, 0), (0, 0), (0, BLOCK - LEVELS * GROUP)), constant_values=-1)
    target = target.reshape(2, 1, CHIPS * BLOCK).astype(jnp.int32)
    rider = jnp.where(
        jnp.arange(BLOCK)[None, :] < 64, router_gate[:, None], recursion_depth[:, None].astype(bf16)
    ).astype(bf16).reshape(LEVELS, CHIPS, GROUP, BLOCK)
    split = (LEVELS, CHIPS, GROUP, WIDTH)
    smem = pl.BlockSpec(memory_space=pltpu.SMEM)
    vmem = pl.BlockSpec(memory_space=pltpu.VMEM)
    out = pl.pallas_call(
        local_kernel,
        out_shape=(
            jax.ShapeDtypeStruct(split, f32),
            jax.ShapeDtypeStruct((CHIPS, 1, BLOCK), f32),
            jax.ShapeDtypeStruct((WIDTH, WIDTH), f32),
            jax.ShapeDtypeStruct((64, WIDTH), f32),
            jax.ShapeDtypeStruct((64, WIDTH), f32),
        ),
        in_specs=[smem, smem, smem, vmem, vmem, vmem, vmem, vmem, vmem, pl.BlockSpec(memory_space=pl.ANY)],
        out_specs=(vmem,) * 5,
        scratch_shapes=[
            pltpu.VMEM((96, GROUP, WIDTH), bf16),
            pltpu.VMEM((96, GROUP, BLOCK), bf16),
            pltpu.VMEM((GROUPS, GROUP, WIDTH), bf16),
            pltpu.VMEM((GROUPS, GROUP, BLOCK), bf16),
            pltpu.VMEM((GROUPS, GROUP, WIDTH), bf16),
            pltpu.VMEM((GROUPS, GROUP, WIDTH), bf16),
            pltpu.VMEM((RING, GROUPS, GROUP, WIDTH), bf16),
            pltpu.VMEM((RING, WIDTH, WIDTH), bf16),
            pltpu.VMEM((GROUPS, GROUP, WIDTH), f32),
            pltpu.VMEM((RING, WIDTH, WIDTH), bf16),
            pltpu.VMEM((CHIPS, WIDTH, WIDTH), bf16),
            pltpu.VMEM((16, 64, WIDTH), bf16),
            pltpu.VMEM((ROWS, RANK), bf16),
            pltpu.VMEM((PEERS, PART, RANK), bf16),
            pltpu.VMEM((PART, RANK), bf16),
            pltpu.VMEM((PEERS, PART, RANK), bf16),
            pltpu.VMEM((ROWS, NREC * RANK), bf16),
            pltpu.VMEM((16, 64, WIDTH), bf16),
            pltpu.VMEM((2, CHIPS, 64, WIDTH), bf16),
            pltpu.VMEM((CHIPS, LEVELS, GROUP, WIDTH), bf16),
            pltpu.VMEM((CHIPS, LEVELS, GROUP, WIDTH), bf16),
            pltpu.VMEM((CHIPS, LEVELS, GROUP, WIDTH), bf16),
            pltpu.VMEM((CHIPS, LEVELS, GROUP, WIDTH), bf16),
            pltpu.VMEM((1, ROWS), f32),
            pltpu.VMEM((32, 1, ROWS), f32),
            pltpu.VMEM((CHIPS, 1, BLOCK), f32),
            pltpu.VMEM((CHIPS, 1, BLOCK), f32),
            pltpu.SemaphoreType.DMA((6,)),
            pltpu.SemaphoreType.DMA((RING,)),
            pltpu.SemaphoreType.DMA((RING, 2)),
            pltpu.SemaphoreType.DMA((RING, 2)),
            pltpu.SemaphoreType.DMA((2,)),
            pltpu.SemaphoreType.DMA((4,)),
            pltpu.SemaphoreType.DMA,
            pltpu.SemaphoreType.DMA,
            pltpu.SemaphoreType.DMA((2,)),
            pltpu.SemaphoreType.DMA((CHIPS,)),
            pltpu.SemaphoreType.DMA((CHIPS,)),
            pltpu.SemaphoreType.DMA((2,)),
            pltpu.SemaphoreType.DMA((4,)),
        ],
        compiler_params=pltpu.CompilerParams(
            collective_id=0, has_side_effects=True, vmem_limit_bytes=VMEM_LIMIT
        ),
    )(
        pick, place.reshape(96), alive.reshape(96).astype(jnp.int32), target,
        cotangent.reshape(split), hidden.reshape(split), rider,
        adapter_up, adapter_down.T, out_weight,
    )
    hidden_grad, gate_back, weight_grad, down_grad, up_grad = out
    gate_grad = gate_back[:, 0, : LEVELS * GROUP].reshape(CHIPS, LEVELS, GROUP).transpose(1, 0, 2).reshape(-1)
    return hidden_grad.reshape(hidden.shape), gate_grad, weight_grad, down_grad, up_grad


def solution(mesh):
    in_specs = (
        P("seq", "tp"),
        P("seq", "tp"),
        P("seq"),
        P("seq"),
        P(),
        P(None, "tp"),
        P("tp", "seq"),
        P("seq", "tp"),
    )
    out_specs = (P("seq", "tp"), P("seq"), P("seq", "tp"), P("seq", "tp"), P("seq", "tp"))
    return jax.shard_map(local, mesh=mesh, in_specs=in_specs, out_specs=out_specs, check_vma=False)
```

```python
import functools

import jax
import jax.numpy as jnp
from jax import lax
from jax.experimental import pallas as pl
from jax.experimental.pallas import tpu as pltpu
from jax.sharding import PartitionSpec as P

NREC = 4
BLOCK = 128
GROUP = 16
CHIPS = 8
LEVELS = 6
GROUPS = 48
ROWS = GROUPS * GROUP
RING = 8
WIDTH = 512
HALF = WIDTH // 2
RANK = 256
PART = 48
PEERS = 16
PIECE = 64
VMEM_LIMIT = 60 * 1024 * 1024

contract_rows = (((0,), (0,)), ((), ()))
contract_last = (((1,), (1,)), ((), ()))
bf16 = jnp.bfloat16
f32 = jnp.float32


def local_kernel(
    pick, place, alive, cot_ref, hid_ref, rid_ref, up_ref, down_ref, w_ref,
    hg_out, gg_out, wg_out, dg_out, ug_out,
    recv_low, recv_high, recv_rid, slot_gate, slot_depth, gates, depths,
    rows, hid, gated_hid, ring, weights, pre,
    w_send, w_recv, sum_send, sum_recv, maps, part_send, part_recv, part_sum, proj, wide,
    g_send, g_recv, x_send, x_recv, h_send, h_recv,
    gate_part, gate_recv, gate_rows, gate_slots, gate_back,
    in_sem, w_sem, ring_send, ring_recv, hid_sem, p_sem, wg_send, wg_recv, sum_sem,
    gr_sem, x_ssem, x_rsem, hr_sem, gate_sem,
):
    s = lax.axis_index("seq")
    t = lax.axis_index("tp")
    core = s % 2
    chip = s // 2
    z = t // 2
    xl = t % 2
    is_cot = core == xl
    kind = (core + xl) % 2
    recv_rows = (recv_low, recv_high)

    def remote(src, dst, ssem, rsem, seq, tp):
        return pltpu.make_async_remote_copy(
            src_ref=src, dst_ref=dst, send_sem=ssem, recv_sem=rsem,
            device_id={"seq": seq, "tp": tp}, device_id_type=pl.DeviceIdType.MESH,
        )

    def wait_bytes(ref, sem):
        pltpu.make_async_copy(ref, ref, sem).wait()

    barrier = pltpu.get_barrier_semaphore()

    def greet_tp(i, c):
        for other in range(2):
            pl.semaphore_signal(barrier, inc=1, device_id={"seq": 2 * chip + other, "tp": (t + i) % 16},
                                device_id_type=pl.DeviceIdType.MESH)
        return c
    lax.fori_loop(1, 16, greet_tp, 0)

    def greet_seq(i, c):
        pl.semaphore_signal(barrier, inc=1, device_id={"seq": (s + i) % 16, "tp": t},
                            device_id_type=pl.DeviceIdType.MESH)
        return c
    lax.fori_loop(1, 16, greet_seq, 0)

    def load_weights(j, c):
        pltpu.make_async_copy(w_ref.at[2 * j + core], weights.at[j], w_sem.at[j]).start()
        return c
    lax.fori_loop(0, RING, load_weights, 0)
    pl.semaphore_wait(barrier, 45)

    def give(src, dst, sem_out, sem_in, seq):
        @pl.when(seq == s)
        def _():
            pltpu.make_async_copy(src, dst, sem_in).start()

        @pl.when(seq != s)
        def _():
            remote(src, dst, sem_out, sem_in, seq, t).start()

    my_slots = pl.ds(s * LEVELS, LEVELS)

    def half(h):
        return pl.ds(h * HALF, HALF)

    def send_first(h, i, c):
        d = (chip + i) % CHIPS
        give(cot_ref.at[:, d, :, half(h)], recv_rows[h].at[my_slots], in_sem.at[h], in_sem.at[6 + h], 2 * d + xl)
        return c
    for h in range(2):
        lax.fori_loop(0, CHIPS, functools.partial(send_first, h), 0)

    def send_rid(i, c):
        d = (chip + i) % CHIPS
        for other in range(2):
            give(rid_ref, recv_rid.at[s], in_sem.at[2], in_sem.at[3], 2 * d + other)
        return c
    lax.fori_loop(0, CHIPS, send_rid, 0)

    def send_second():
        def send_hid(i, c):
            d = (chip + i) % CHIPS
            for h in range(2):
                give(hid_ref.at[:, d, :, half(h)], recv_rows[h].at[my_slots], in_sem.at[h], in_sem.at[6 + h],
                     2 * d + 1 - xl)
            return c
        lax.fori_loop(0, CHIPS, send_hid, 0)

        def send_maps(i, c):
            d = (chip + i) % CHIPS
            give(up_ref, maps.at[s], in_sem.at[4], in_sem.at[5], 2 * d + xl)
            give(down_ref, maps.at[s], in_sem.at[4], in_sem.at[5], 2 * d + 1 - xl)
            return c
        lax.fori_loop(0, CHIPS, send_maps, 0)

    right = 2 * ((z + 1) % RING) + xl
    left = 2 * ((z + RING - 1) % RING) + xl
    across = 2 * z + 1 - xl
    partner = 2 * chip + 1 - core

    def to_right(src, slot, h):
        return remote(src, ring.at[slot, h], ring_send.at[slot, h], ring_recv.at[slot, h], s, right)

    def to_left(src, slot, h):
        return remote(src, ring.at[slot, h], ring_send.at[slot, h], ring_recv.at[slot, h], s, left)

    def to_across(h):
        return remote(ring.at[0, h], ring.at[0, h], ring_send.at[0, h], ring_recv.at[0, h], s, across)

    def to_partner():
        return remote(hid, hid, hid_sem.at[0], hid_sem.at[1], partner, t)

    def forward(i):
        for h in range(2):
            wait_bytes(ring.at[i, h], ring_recv.at[i, h])
            if i < 5 or h == 0:
                to_right(ring.at[i, h], i + 2, h).start()
            wait_bytes(ring.at[i + 1, h], ring_recv.at[i + 1, h])
            if i < 5:
                to_left(ring.at[i + 1, h], i + 3, h).start()
            elif h == 1:
                to_left(ring.at[6, h], 7, h).start()

    @pl.when(is_cot)
    def _():
        for h in range(2):
            wait_bytes(recv_rows[h], in_sem.at[6 + h])

            def pack(g, c):
                value = recv_rows[h][pick[g]]
                rows[g, :, h * HALF:(h + 1) * HALF] = value
                ring[0, h, g] = value
                return c
            lax.fori_loop(0, GROUPS, pack, 0, unroll=4)
            to_across(h).start()
            to_right(ring.at[0, h], 1, h).start()
            to_left(ring.at[0, h], 2, h).start()

    @pl.when(jnp.logical_not(is_cot))
    def _():
        for h in range(2):
            wait_bytes(ring.at[0, h], ring_recv.at[0, h])
            to_right(ring.at[0, h], 1, h).start()
            to_left(ring.at[0, h], 2, h).start()
    send_second()

    wait_bytes(recv_rid, in_sem.at[3])
    lane = lax.broadcasted_iota(jnp.int32, (GROUP, BLOCK), 1)
    row = lax.broadcasted_iota(jnp.int32, (GROUP, BLOCK), 0)
    chosen = (lane == chip * GROUP + row).astype(f32).astype(bf16)
    columns = lax.dot_general(chosen, recv_rid[...].reshape(16 * GROUP, BLOCK).astype(bf16), contract_last,
                              preferred_element_type=f32)
    for i in range(16):
        for j in range(LEVELS):
            at = i * GROUP + j
            slot_gate[i * LEVELS + j] = jnp.broadcast_to(columns[:, at:at + 1], (GROUP, BLOCK))
            slot_depth[i * LEVELS + j] = jnp.broadcast_to(columns[:, at + 8:at + 9], (GROUP, BLOCK))

    def pack_rid(g, c):
        gates[g] = slot_gate[pick[g]]
        depths[g] = slot_depth[pick[g]]
        return c
    lax.fori_loop(0, GROUPS, pack_rid, 0, unroll=4)
    pre[...] = jnp.zeros_like(pre)

    forward(1)

    @pl.when(jnp.logical_not(is_cot))
    def _():
        for h in range(2):
            wait_bytes(recv_rows[h], in_sem.at[6 + h])

            def pack(g, c):
                value = recv_rows[h][pick[g]]
                rows[g, :, h * HALF:(h + 1) * HALF] = value
                hid[g, :, h * HALF:(h + 1) * HALF] = value
                return c
            lax.fori_loop(0, GROUPS, pack, 0, unroll=4)
        to_partner().start()

    wait_bytes(maps, in_sem.at[5])

    def project(r, c):
        groups = pl.ds(r * GROUP, GROUP)
        x = rows[groups].reshape(RANK, WIDTH)
        y = lax.dot_general(x, maps[...].reshape(NREC * RANK, WIDTH), contract_last, preferred_element_type=f32)
        depth = depths[groups].reshape(RANK, BLOCK)[:, 0:1]
        total = jnp.zeros((RANK, RANK), f32)
        for d in range(NREC):
            total = total + jnp.where(depth == d + 1.0, y[:, d * RANK:(d + 1) * RANK], 0.0)
        part_send[pl.ds(r * RANK, RANK)] = total.astype(bf16)
        return c
    lax.fori_loop(0, ROWS // RANK, project, 0)

    def same_kind(t2):
        return 2 * chip + (core + xl + t2) % 2

    def send_part(i, c):
        t2 = (t + i) % PEERS
        remote(part_send.at[pl.ds(t2 * PART, PART)], part_recv.at[t], p_sem.at[0], p_sem.at[1],
               same_kind(t2), t2).start()
        return c
    lax.fori_loop(1, PEERS, send_part, 0)
    pltpu.make_async_copy(part_send.at[pl.ds(t * PART, PART)], part_recv.at[t], p_sem.at[1]).start()

    @pl.when(is_cot)
    def _():
        wait_bytes(hid, hid_sem.at[1])

    def apply_gate(g, c):
        gate = gates[g][:, 0:1]
        gated_hid[g] = (gate * hid[g].astype(f32)).astype(bf16)
        rows[g] = (gate * rows[g].astype(f32)).astype(bf16)
        return c
    lax.fori_loop(0, GROUPS, apply_gate, 0, unroll=4)

    def origin_of(i):
        shift = jnp.where(i % 2 == 1, 2 * RING - (i + 1) // 2, i // 2)
        return (z + shift) % RING

    def compute(i, c):
        origin = origin_of(i)
        pltpu.make_async_copy(w_ref.at[0], weights.at[origin], w_sem.at[origin]).wait()
        for h in range(2):
            w_send[i, h * 4:(h + 1) * 4] = lax.dot_general(
                ring[i, h].reshape(ROWS, HALF), gated_hid[...].reshape(ROWS, WIDTH), contract_rows,
                preferred_element_type=f32).astype(bf16).reshape(4, PIECE, WIDTH)

        give(w_send.at[i], w_recv.at[chip], wg_send, wg_recv.at[0], 2 * origin + core)
        term = jnp.dot(ring[i, 0].reshape(ROWS, HALF), weights[origin, 0], preferred_element_type=f32)
        term = term + jnp.dot(ring[i, 1].reshape(ROWS, HALF), weights[origin, 1], preferred_element_type=f32)
        pre[...] = pre[...] + term.reshape(GROUPS, GROUP, WIDTH)
        return c

    def run(i, c):
        @pl.when(i == 3)
        def _():
            forward(3)
            wait_bytes(part_recv, p_sem.at[1])
            part_sum[...] = jnp.sum(part_recv[...].astype(f32), axis=0).astype(bf16)

            def send_sum(j, c):
                t2 = (t + j) % PEERS
                remote(part_sum, proj.at[t], p_sem.at[2], p_sem.at[3],
                       4 * chip + 1 - same_kind(t2), t2).start()
                return c
            lax.fori_loop(0, PEERS, send_sum, 0)

        @pl.when(i == 5)
        def _():
            forward(5)

        @pl.when(i == RING - 1)
        def _():
            wait_bytes(proj, p_sem.at[3])
            flat = proj[...].reshape(ROWS, RANK)
            depth = depths[...].reshape(ROWS, BLOCK)[:, 0:1]
            for d in range(NREC):
                wide[:, d * RANK:(d + 1) * RANK] = jnp.where(
                    depth == d + 1.0, 0.5 * flat.astype(f32), 0.0).astype(bf16)

            @pl.when(jnp.logical_not(is_cot))
            def _():
                def add_adapter(r, c):
                    groups = pl.ds(r * GROUP, GROUP)
                    term = jnp.dot(wide[pl.ds(r * RANK, RANK)], maps[...].reshape(NREC * RANK, WIDTH),
                                   preferred_element_type=f32)
                    pre[groups] = pre[groups] + term.reshape(GROUP, GROUP, WIDTH)
                    return c
                lax.fori_loop(0, ROWS // RANK, add_adapter, 0)

            for q in range(NREC):
                grad = lax.dot_general(wide[:, q * RANK:(q + 1) * RANK], rows[...].reshape(ROWS, WIDTH),
                                       contract_rows, preferred_element_type=f32)
                g_send[q * 4:(q + 1) * 4] = grad.astype(bf16).reshape(4, PIECE, WIDTH)

            def send_grad(j, c):
                to = (s + j) % 16
                remote(g_send.at[to], g_recv.at[kind, chip], gr_sem.at[0], gr_sem.at[1], to, t).start()
                return c
            lax.fori_loop(1, 16, send_grad, 0)
            pltpu.make_async_copy(g_send.at[s], g_recv.at[kind, chip], gr_sem.at[1]).start()
            for h in range(2):
                wait_bytes(ring.at[RING - 1, h], ring_recv.at[RING - 1, h])

        compute(i, c)
        return c
    lax.fori_loop(0, RING, run, 0)

    ones = jnp.ones((8, WIDTH), bf16)
    for r in range(ROWS // RANK):
        groups = slice(r * GROUP, (r + 1) * GROUP)
        prod = pre[groups].reshape(RANK, WIDTH) * hid[groups].reshape(RANK, WIDTH).astype(f32)
        high = prod.astype(bf16)
        low = (prod - high.astype(f32)).astype(bf16)
        lanes = lax.dot_general(ones, high, contract_last, preferred_element_type=f32)
        lanes = lanes + lax.dot_general(ones, low, contract_last, preferred_element_type=f32)
        gate_part[:, r * RANK:(r + 1) * RANK] = lanes[0:1]
    me = 2 * t + core

    def send_gate(j, c):
        t2 = (t + j) % PEERS
        for other in range(2):
            remote(gate_part, gate_recv.at[me], gate_sem.at[0], gate_sem.at[1], 2 * chip + other, t2).start()
        return c
    lax.fori_loop(1, PEERS, send_gate, 0)
    remote(gate_part, gate_recv.at[me], gate_sem.at[0], gate_sem.at[1], partner, t).start()
    pltpu.make_async_copy(gate_part, gate_recv.at[me], gate_sem.at[1]).start()

    def slot_rows(slot):
        gate = slot_gate[slot][:, 0:1]
        return jnp.where(alive[slot] > 0, gate * pre[place[slot]], 0.0)

    def to_other(d):
        return remote(x_send.at[d], x_recv.at[d], x_ssem.at[d], x_rsem.at[d], partner, t)

    def expand(i, c):
        d = (chip + i) % CHIPS
        for j in range(LEVELS):
            x_send[d, j] = slot_rows((2 * d + 1 - core) * LEVELS + j).astype(bf16)
        to_other(d).start()
        return c
    lax.fori_loop(0, CHIPS, expand, 0)

    def give_back(i, c):
        d = (chip + i) % CHIPS
        wait_bytes(x_recv.at[d], x_rsem.at[d])
        for j in range(LEVELS):
            value = slot_rows((2 * d + core) * LEVELS + j) + x_recv[d, j].astype(f32)
            h_send[d, j] = value.astype(bf16)
        give(h_send.at[d], h_recv.at[chip], hr_sem.at[0], hr_sem.at[1], 2 * d + core)
        return c
    lax.fori_loop(0, CHIPS, give_back, 0)

    wait_bytes(gate_recv, gate_sem.at[1])
    total = jnp.sum(gate_recv[...], axis=0)
    group_of = lax.shift_right_logical(lax.broadcasted_iota(jnp.int32, (GROUPS, ROWS), 1), 4)
    rest = jnp.where(group_of == lax.broadcasted_iota(jnp.int32, (GROUPS, ROWS), 0), total, 0.0)
    low_bits = jnp.bitwise_and(lax.broadcasted_iota(jnp.int32, (ROWS, BLOCK), 0), GROUP - 1)
    low_lane = jnp.bitwise_and(lax.broadcasted_iota(jnp.int32, (ROWS, BLOCK), 1), GROUP - 1)
    fold = (low_bits == low_lane).astype(f32).astype(bf16)
    folded = jnp.zeros((GROUPS, BLOCK), f32)
    for _ in range(3):
        piece = rest.astype(bf16)
        rest = rest - piece.astype(f32)
        folded = folded + jnp.dot(piece, fold, preferred_element_type=f32)
    for g in range(GROUPS):
        gate_rows[g] = folded[g:g + 1]
    mine = lax.shift_right_logical(lax.broadcasted_iota(jnp.int32, (1, BLOCK), 1), 4) == chip

    for d in range(CHIPS):
        lines = []
        for j in range(LEVELS):
            slot = (2 * d + core) * LEVELS + j
            value = jnp.where(alive[slot] > 0, gate_rows[place[slot]], 0.0)
            lines.append(jnp.where(mine, value, 0.0))
        gate_slots[d] = jnp.concatenate(lines + [jnp.zeros((2, BLOCK), f32)], axis=0)

    def give_slots(i, c):
        d = (chip + i) % CHIPS
        give(gate_slots.at[d], gate_back.at[chip], gate_sem.at[2], gate_sem.at[3], 2 * d + core)
        return c
    lax.fori_loop(0, CHIPS, give_slots, 0)

    wait_bytes(g_recv, gr_sem.at[1])
    ug_out[...] = jnp.sum(g_recv[0].astype(f32), axis=0)
    dg_out[...] = jnp.sum(g_recv[1].astype(f32), axis=0)
    wait_bytes(h_recv, hr_sem.at[1])
    hg_out[...] = h_recv[...]
    wait_bytes(w_recv, wg_recv.at[0])
    for d in range(CHIPS):
        wg_out[d * PIECE:(d + 1) * PIECE] = jnp.sum(w_recv[:, d].astype(f32), axis=0)
    wait_bytes(gate_back, gate_sem.at[3])
    gg_out[...] = jnp.sum(gate_back[...], axis=0)

    for h in range(2):
        wait_bytes(recv_rows[h].at[pl.ds(0, 15 * LEVELS)], in_sem.at[h])
    wait_bytes(recv_rid.at[pl.ds(0, 15)], in_sem.at[2])
    wait_bytes(maps.at[pl.ds(0, 15)], in_sem.at[4])

    @pl.when(is_cot)
    def _():
        for h in range(2):
            to_across(h).wait_send()

    @pl.when(jnp.logical_not(is_cot))
    def _():
        to_partner().wait_send()
    for h in range(2):
        for slot in range(1, 7):
            to_right(ring.at[slot, h], slot, h).wait_send()
        to_right(ring.at[7, h], 7, h).wait_send()
    wait_bytes(part_recv.at[pl.ds(0, 15)], p_sem.at[0])
    wait_bytes(proj, p_sem.at[2])
    wait_bytes(g_send.at[pl.ds(0, 15)], gr_sem.at[0])
    wait_bytes(w_send.at[pl.ds(0, 7)], wg_send)
    for d in range(CHIPS):
        to_other(d).wait_send()
    wait_bytes(h_send.at[pl.ds(0, 7)], hr_sem.at[0])
    wait_bytes(gate_recv.at[pl.ds(0, 31)], gate_sem.at[0])
    wait_bytes(gate_slots.at[pl.ds(0, 7)], gate_sem.at[2])


def local(hidden, cotangent, router_gate, recursion_depth, live_counts, out_weight, adapter_down, adapter_up):
    rider = jnp.stack([router_gate.astype(f32), recursion_depth.astype(f32)]).reshape(2, LEVELS, BLOCK)
    rider = jnp.pad(rider, ((0, 0), (0, 2), (0, 0))).reshape(16, BLOCK)
    split = (LEVELS, CHIPS, GROUP, WIDTH)
    blocks = live_counts // BLOCK
    finish = jnp.cumsum(blocks)
    begin = finish - blocks
    level = jnp.arange(LEVELS, dtype=jnp.int32)
    alive = level[None, :] < blocks[:, None]
    place = jnp.where(alive, begin[:, None] + level[None, :], 0)
    order = jnp.arange(GROUPS, dtype=jnp.int32)
    past = finish[None, :] <= order[:, None]
    source = jnp.sum(past.astype(jnp.int32), axis=1)
    first = jnp.max(jnp.where(past, finish[None, :], 0), axis=1)
    pick = source * LEVELS + order - first
    vmem = pl.BlockSpec(memory_space=pltpu.VMEM)
    grouped = (GROUPS, GROUP, WIDTH)
    slots = (CHIPS, LEVELS, GROUP, WIDTH)
    dma = pltpu.SemaphoreType.DMA
    out = pl.pallas_call(
        local_kernel,
        out_shape=(
            jax.ShapeDtypeStruct(slots, bf16),
            jax.ShapeDtypeStruct((8, BLOCK), f32),
            jax.ShapeDtypeStruct((WIDTH, WIDTH), f32),
            jax.ShapeDtypeStruct((PIECE, WIDTH), f32),
            jax.ShapeDtypeStruct((PIECE, WIDTH), f32),
        ),
        in_specs=[pl.BlockSpec(memory_space=pltpu.SMEM)] * 3 + [vmem] * 5 + [pl.BlockSpec(memory_space=pl.ANY)],
        out_specs=(vmem,) * 5,
        scratch_shapes=[
            pltpu.VMEM((96, GROUP, HALF), bf16),
            pltpu.VMEM((96, GROUP, HALF), bf16),
            pltpu.VMEM((16, 16, BLOCK), f32),
            pltpu.VMEM((96, GROUP, BLOCK), f32),
            pltpu.VMEM((96, GROUP, BLOCK), f32),
            pltpu.VMEM((GROUPS, GROUP, BLOCK), f32),
            pltpu.VMEM((GROUPS, GROUP, BLOCK), f32),
            pltpu.VMEM(grouped, bf16),
            pltpu.VMEM(grouped, bf16),
            pltpu.VMEM(grouped, bf16),
            pltpu.VMEM((RING, 2, GROUPS, GROUP, HALF), bf16),
            pltpu.VMEM((RING, 2, HALF, WIDTH), bf16),
            pltpu.VMEM(grouped, f32),
            pltpu.VMEM((RING, CHIPS, PIECE, WIDTH), bf16),
            pltpu.VMEM((RING, CHIPS, PIECE, WIDTH), bf16),
            pltpu.VMEM((RING, PIECE, WIDTH), bf16),
            pltpu.VMEM((CHIPS, PIECE, WIDTH), bf16),
            pltpu.VMEM((16, PIECE, WIDTH), bf16),
            pltpu.VMEM((ROWS, RANK), bf16),
            pltpu.VMEM((PEERS, PART, RANK), bf16),
            pltpu.VMEM((PART, RANK), bf16),
            pltpu.VMEM((PEERS, PART, RANK), bf16),
            pltpu.VMEM((ROWS, NREC * RANK), bf16),
            pltpu.VMEM((16, PIECE, WIDTH), bf16),
            pltpu.VMEM((2, CHIPS, PIECE, WIDTH), bf16),
            pltpu.VMEM(slots, bf16),
            pltpu.VMEM(slots, bf16),
            pltpu.VMEM(slots, bf16),
            pltpu.VMEM(slots, bf16),
            pltpu.VMEM((1, ROWS), f32),
            pltpu.VMEM((32, 1, ROWS), f32),
            pltpu.VMEM((GROUPS, 1, BLOCK), f32),
            pltpu.VMEM((CHIPS, 8, BLOCK), f32),
            pltpu.VMEM((CHIPS, 8, BLOCK), f32),
            dma((8,)),
            dma((RING,)),
            dma((RING, 2)),
            dma((RING, 2)),
            dma((2,)),
            dma((4,)),
            dma,
            dma((RING,)),
            dma((2,)),
            dma((2,)),
            dma((CHIPS,)),
            dma((CHIPS,)),
            dma((2,)),
            dma((4,)),
        ],
        compiler_params=pltpu.CompilerParams(
            collective_id=0, has_side_effects=True, vmem_limit_bytes=VMEM_LIMIT
        ),
    )(
        pick, place.reshape(96), alive.reshape(96).astype(jnp.int32), cotangent.reshape(split), hidden.reshape(split), rider,
        adapter_up, adapter_down.T, out_weight.reshape(PEERS, 2, HALF, WIDTH),
    )
    hidden_grad, gate_back, weight_grad, down_grad, up_grad = out
    hidden_grad = hidden_grad.transpose(1, 0, 2, 3).reshape(hidden.shape).astype(f32)
    return hidden_grad, gate_back[:LEVELS].reshape(-1), weight_grad, down_grad, up_grad


def solution(mesh):
    in_specs = (
        P("seq", "tp"),
        P("seq", "tp"),
        P("seq"),
        P("seq"),
        P(),
        P(None, "tp"),
        P("tp", "seq"),
        P("seq", "tp"),
    )
    out_specs = (P("seq", "tp"), P("seq"), P("seq", "tp"), P("seq", "tp"), P("seq", "tp"))
    return jax.shard_map(local, mesh=mesh, in_specs=in_specs, out_specs=out_specs, check_vma=False)
```

```python
import functools

import jax
import jax.numpy as jnp
from jax import lax
from jax.experimental import pallas as pl
from jax.experimental.pallas import tpu as pltpu
from jax.sharding import PartitionSpec as P

NREC = 4
BLOCK = 128
GROUP = 16
CHIPS = 8
LEVELS = 6
GROUPS = 48
ROWS = GROUPS * GROUP
RING = 8
WIDTH = 512
HALF = WIDTH // 2
RANK = 256
PART = 48
PEERS = 16
PIECE = 64
VMEM_LIMIT = 60 * 1024 * 1024

contract_rows = (((0,), (0,)), ((), ()))
contract_last = (((1,), (1,)), ((), ()))
bf16 = jnp.bfloat16
f32 = jnp.float32


def local_kernel(
    pick, place, alive, cot_ref, hid_ref, rid_ref, up_ref, down_ref, w_ref,
    hg_out, gg_out, wg_out, dg_out, ug_out,
    recv_low, recv_high, recv_rid, slot_gate, slot_depth, gates, depths,
    rows, hid, gated_hid, ring, weights, pre,
    w_send, w_recv, sum_send, sum_recv, maps, part_send, part_recv, part_sum, proj, wide,
    g_send, g_recv, x_send, x_recv, h_send, h_recv,
    gate_part, gate_recv, gate_rows, gate_slots, gate_back,
    in_sem, w_sem, ring_send, ring_recv, hid_sem, p_sem, wg_send, wg_recv, sum_sem,
    gr_sem, x_ssem, x_rsem, hr_sem, gate_sem,
):
    s = lax.axis_index("seq")
    t = lax.axis_index("tp")
    core = s % 2
    chip = s // 2
    z = t // 2
    xl = t % 2
    is_cot = core == xl
    kind = (core + xl) % 2
    recv_rows = (recv_low, recv_high)

    def remote(src, dst, ssem, rsem, seq, tp):
        return pltpu.make_async_remote_copy(
            src_ref=src, dst_ref=dst, send_sem=ssem, recv_sem=rsem,
            device_id={"seq": seq, "tp": tp}, device_id_type=pl.DeviceIdType.MESH,
        )

    def wait_bytes(ref, sem):
        pltpu.make_async_copy(ref, ref, sem).wait()

    barrier = pltpu.get_barrier_semaphore()

    def greet_tp(i, c):
        for other in range(2):
            pl.semaphore_signal(barrier, inc=1, device_id={"seq": 2 * chip + other, "tp": (t + i) % 16},
                                device_id_type=pl.DeviceIdType.MESH)
        return c
    lax.fori_loop(1, 16, greet_tp, 0)

    def greet_seq(i, c):
        pl.semaphore_signal(barrier, inc=1, device_id={"seq": (s + i) % 16, "tp": t},
                            device_id_type=pl.DeviceIdType.MESH)
        return c
    lax.fori_loop(1, 16, greet_seq, 0)

    def load_weights(j, c):
        pltpu.make_async_copy(w_ref.at[2 * j + core], weights.at[j], w_sem.at[j]).start()
        return c
    lax.fori_loop(0, RING, load_weights, 0)
    pl.semaphore_wait(barrier, 45)

    def give(src, dst, sem_out, sem_in, seq):
        @pl.when(seq == s)
        def _():
            pltpu.make_async_copy(src, dst, sem_in).start()

        @pl.when(seq != s)
        def _():
            remote(src, dst, sem_out, sem_in, seq, t).start()

    my_slots = pl.ds(s * LEVELS, LEVELS)

    def half(h):
        return pl.ds(h * HALF, HALF)

    def send_first(h, i, c):
        d = (chip + i) % CHIPS
        give(cot_ref.at[:, d, :, half(h)], recv_rows[h].at[my_slots], in_sem.at[h], in_sem.at[6 + h], 2 * d + xl)
        return c
    for h in range(2):
        lax.fori_loop(0, CHIPS, functools.partial(send_first, h), 0)

    def send_rid(i, c):
        d = (chip + i) % CHIPS
        for other in range(2):
            give(rid_ref, recv_rid.at[s], in_sem.at[2], in_sem.at[3], 2 * d + other)
        return c
    lax.fori_loop(0, CHIPS, send_rid, 0)

    def send_second():
        def send_hid(i, c):
            d = (chip + i) % CHIPS
            for h in range(2):
                give(hid_ref.at[:, d, :, half(h)], recv_rows[h].at[my_slots], in_sem.at[h], in_sem.at[6 + h],
                     2 * d + 1 - xl)
            return c
        lax.fori_loop(0, CHIPS, send_hid, 0)

        def send_maps(i, c):
            d = (chip + i) % CHIPS
            give(up_ref, maps.at[s], in_sem.at[4], in_sem.at[5], 2 * d + xl)
            give(down_ref, maps.at[s], in_sem.at[4], in_sem.at[5], 2 * d + 1 - xl)
            return c
        lax.fori_loop(0, CHIPS, send_maps, 0)

    right = 2 * ((z + 1) % RING) + xl
    left = 2 * ((z + RING - 1) % RING) + xl
    across = 2 * z + 1 - xl
    partner = 2 * chip + 1 - core

    def to_right(src, slot, h):
        return remote(src, ring.at[slot, h], ring_send.at[slot, h], ring_recv.at[slot, h], s, right)

    def to_left(src, slot, h):
        return remote(src, ring.at[slot, h], ring_send.at[slot, h], ring_recv.at[slot, h], s, left)

    def to_across(h):
        return remote(ring.at[0, h], ring.at[0, h], ring_send.at[0, h], ring_recv.at[0, h], s, across)

    def to_partner():
        return remote(hid, hid, hid_sem.at[0], hid_sem.at[1], partner, t)

    def forward(i):
        for h in range(2):
            wait_bytes(ring.at[i, h], ring_recv.at[i, h])
            if i < 5 or h == 0:
                to_right(ring.at[i, h], i + 2, h).start()
            wait_bytes(ring.at[i + 1, h], ring_recv.at[i + 1, h])
            if i < 5:
                to_left(ring.at[i + 1, h], i + 3, h).start()
            elif h == 1:
                to_left(ring.at[6, h], 7, h).start()

    @pl.when(is_cot)
    def _():
        for h in range(2):
            wait_bytes(recv_rows[h], in_sem.at[6 + h])

            def pack(g, c):
                value = recv_rows[h][pick[g]]
                rows[g, :, h * HALF:(h + 1) * HALF] = value
                ring[0, h, g] = value
                return c
            lax.fori_loop(0, GROUPS, pack, 0, unroll=4)
            to_across(h).start()
            to_right(ring.at[0, h], 1, h).start()
            to_left(ring.at[0, h], 2, h).start()

    @pl.when(jnp.logical_not(is_cot))
    def _():
        for h in range(2):
            wait_bytes(ring.at[0, h], ring_recv.at[0, h])
            to_right(ring.at[0, h], 1, h).start()
            to_left(ring.at[0, h], 2, h).start()
    send_second()

    wait_bytes(recv_rid, in_sem.at[3])
    lane = lax.broadcasted_iota(jnp.int32, (GROUP, BLOCK), 1)
    row = lax.broadcasted_iota(jnp.int32, (GROUP, BLOCK), 0)
    chosen = (lane == chip * GROUP + row).astype(f32).astype(bf16)
    columns = lax.dot_general(chosen, recv_rid[...].reshape(16 * GROUP, BLOCK).astype(bf16), contract_last,
                              preferred_element_type=f32)
    for i in range(16):
        for j in range(LEVELS):
            at = i * GROUP + j
            slot_gate[i * LEVELS + j] = jnp.broadcast_to(columns[:, at:at + 1], (GROUP, BLOCK))
            slot_depth[i * LEVELS + j] = jnp.broadcast_to(columns[:, at + 8:at + 9], (GROUP, BLOCK))

    def pack_rid(g, c):
        gates[g] = slot_gate[pick[g]]
        depths[g] = slot_depth[pick[g]]
        return c
    lax.fori_loop(0, GROUPS, pack_rid, 0, unroll=4)
    pre[...] = jnp.zeros_like(pre)

    forward(1)

    @pl.when(jnp.logical_not(is_cot))
    def _():
        for h in range(2):
            wait_bytes(recv_rows[h], in_sem.at[6 + h])

            def pack(g, c):
                value = recv_rows[h][pick[g]]
                rows[g, :, h * HALF:(h + 1) * HALF] = value
                hid[g, :, h * HALF:(h + 1) * HALF] = value
                return c
            lax.fori_loop(0, GROUPS, pack, 0, unroll=4)
        to_partner().start()

    wait_bytes(maps, in_sem.at[5])

    def project(r, c):
        groups = pl.ds(r * GROUP, GROUP)
        x = rows[groups].reshape(RANK, WIDTH)
        y = lax.dot_general(x, maps[...].reshape(NREC * RANK, WIDTH), contract_last, preferred_element_type=f32)
        depth = depths[groups].reshape(RANK, BLOCK)[:, 0:1]
        total = jnp.zeros((RANK, RANK), f32)
        for d in range(NREC):
            total = total + jnp.where(depth == d + 1.0, y[:, d * RANK:(d + 1) * RANK], 0.0)
        part_send[pl.ds(r * RANK, RANK)] = total.astype(bf16)
        return c
    lax.fori_loop(0, ROWS // RANK, project, 0)

    def same_kind(t2):
        return 2 * chip + (core + xl + t2) % 2

    def send_part(i, c):
        t2 = (t + i) % PEERS
        remote(part_send.at[pl.ds(t2 * PART, PART)], part_recv.at[t], p_sem.at[0], p_sem.at[1],
               same_kind(t2), t2).start()
        return c
    lax.fori_loop(1, PEERS, send_part, 0)
    pltpu.make_async_copy(part_send.at[pl.ds(t * PART, PART)], part_recv.at[t], p_sem.at[1]).start()

    @pl.when(is_cot)
    def _():
        wait_bytes(hid, hid_sem.at[1])

    def apply_gate(g, c):
        gate = gates[g][:, 0:1]
        gated_hid[g] = (gate * hid[g].astype(f32)).astype(bf16)
        rows[g] = (gate * rows[g].astype(f32)).astype(bf16)
        return c
    lax.fori_loop(0, GROUPS, apply_gate, 0, unroll=4)

    def origin_of(i):
        shift = jnp.where(i % 2 == 1, 2 * RING - (i + 1) // 2, i // 2)
        return (z + shift) % RING

    def compute(i, c):
        origin = origin_of(i)
        pltpu.make_async_copy(w_ref.at[0], weights.at[origin], w_sem.at[origin]).wait()
        for h in range(2):
            w_send[i, h * 4:(h + 1) * 4] = lax.dot_general(
                ring[i, h].reshape(ROWS, HALF), gated_hid[...].reshape(ROWS, WIDTH), contract_rows,
                preferred_element_type=f32).astype(bf16).reshape(4, PIECE, WIDTH)

        def scatter(j, c):
            d = (chip + j) % CHIPS
            give(w_send.at[i, d], w_recv.at[i, chip], wg_send, wg_recv.at[i], 2 * d + core)
            return c
        lax.fori_loop(0, CHIPS, scatter, 0)
        term = jnp.dot(ring[i, 0].reshape(ROWS, HALF), weights[origin, 0], preferred_element_type=f32)
        term = term + jnp.dot(ring[i, 1].reshape(ROWS, HALF), weights[origin, 1], preferred_element_type=f32)
        pre[...] = pre[...] + term.reshape(GROUPS, GROUP, WIDTH)
        return c

    def collect(i, c):
        wait_bytes(w_recv.at[i], wg_recv.at[i])
        sum_send[i] = jnp.sum(w_recv[i].astype(f32), axis=0).astype(bf16)
        give(sum_send.at[i], sum_recv.at[chip], sum_sem.at[0], sum_sem.at[1], 2 * origin_of(i) + core)
        return c

    def run(i, c):
        @pl.when(i == 3)
        def _():
            forward(3)
            wait_bytes(part_recv, p_sem.at[1])
            part_sum[...] = jnp.sum(part_recv[...].astype(f32), axis=0).astype(bf16)

            def send_sum(j, c):
                t2 = (t + j) % PEERS
                remote(part_sum, proj.at[t], p_sem.at[2], p_sem.at[3],
                       4 * chip + 1 - same_kind(t2), t2).start()
                return c
            lax.fori_loop(0, PEERS, send_sum, 0)

        @pl.when(i == 5)
        def _():
            forward(5)

        @pl.when(i == RING - 1)
        def _():
            wait_bytes(proj, p_sem.at[3])
            flat = proj[...].reshape(ROWS, RANK)
            depth = depths[...].reshape(ROWS, BLOCK)[:, 0:1]
            for d in range(NREC):
                wide[:, d * RANK:(d + 1) * RANK] = jnp.where(
                    depth == d + 1.0, 0.5 * flat.astype(f32), 0.0).astype(bf16)

            @pl.when(jnp.logical_not(is_cot))
            def _():
                def add_adapter(r, c):
                    groups = pl.ds(r * GROUP, GROUP)
                    term = jnp.dot(wide[pl.ds(r * RANK, RANK)], maps[...].reshape(NREC * RANK, WIDTH),
                                   preferred_element_type=f32)
                    pre[groups] = pre[groups] + term.reshape(GROUP, GROUP, WIDTH)
                    return c
                lax.fori_loop(0, ROWS // RANK, add_adapter, 0)

            for q in range(NREC):
                grad = lax.dot_general(wide[:, q * RANK:(q + 1) * RANK], rows[...].reshape(ROWS, WIDTH),
                                       contract_rows, preferred_element_type=f32)
                g_send[q * 4:(q + 1) * 4] = grad.astype(bf16).reshape(4, PIECE, WIDTH)

            def send_grad(j, c):
                to = (s + j) % 16
                remote(g_send.at[to], g_recv.at[kind, chip], gr_sem.at[0], gr_sem.at[1], to, t).start()
                return c
            lax.fori_loop(1, 16, send_grad, 0)
            pltpu.make_async_copy(g_send.at[s], g_recv.at[kind, chip], gr_sem.at[1]).start()
            for h in range(2):
                wait_bytes(ring.at[RING - 1, h], ring_recv.at[RING - 1, h])

        compute(i, c)

        @pl.when(i >= 4)
        def _():
            collect(i - 4, c)
        return c
    lax.fori_loop(0, RING, run, 0)

    ones = jnp.ones((8, WIDTH), bf16)
    for r in range(ROWS // RANK):
        groups = slice(r * GROUP, (r + 1) * GROUP)
        prod = pre[groups].reshape(RANK, WIDTH) * hid[groups].reshape(RANK, WIDTH).astype(f32)
        high = prod.astype(bf16)
        low = (prod - high.astype(f32)).astype(bf16)
        lanes = lax.dot_general(ones, high, contract_last, preferred_element_type=f32)
        lanes = lanes + lax.dot_general(ones, low, contract_last, preferred_element_type=f32)
        gate_part[:, r * RANK:(r + 1) * RANK] = lanes[0:1]
    me = 2 * t + core

    def send_gate(j, c):
        t2 = (t + j) % PEERS
        for other in range(2):
            remote(gate_part, gate_recv.at[me], gate_sem.at[0], gate_sem.at[1], 2 * chip + other, t2).start()
        return c
    lax.fori_loop(1, PEERS, send_gate, 0)
    remote(gate_part, gate_recv.at[me], gate_sem.at[0], gate_sem.at[1], partner, t).start()
    pltpu.make_async_copy(gate_part, gate_recv.at[me], gate_sem.at[1]).start()

    def slot_rows(slot):
        gate = slot_gate[slot][:, 0:1]
        return jnp.where(alive[slot] > 0, gate * pre[place[slot]], 0.0)

    def to_other(d):
        return remote(x_send.at[d], x_recv.at[d], x_ssem.at[d], x_rsem.at[d], partner, t)

    def expand(i, c):
        d = (chip + i) % CHIPS
        for j in range(LEVELS):
            x_send[d, j] = slot_rows((2 * d + 1 - core) * LEVELS + j).astype(bf16)
        to_other(d).start()
        return c
    lax.fori_loop(0, CHIPS, expand, 0)

    def give_back(i, c):
        d = (chip + i) % CHIPS
        wait_bytes(x_recv.at[d], x_rsem.at[d])
        for j in range(LEVELS):
            value = slot_rows((2 * d + core) * LEVELS + j) + x_recv[d, j].astype(f32)
            h_send[d, j] = value.astype(bf16)
        give(h_send.at[d], h_recv.at[chip], hr_sem.at[0], hr_sem.at[1], 2 * d + core)
        return c
    lax.fori_loop(0, CHIPS, give_back, 0)
    lax.fori_loop(4, RING, collect, 0)

    wait_bytes(gate_recv, gate_sem.at[1])
    total = jnp.sum(gate_recv[...], axis=0)
    group_of = lax.shift_right_logical(lax.broadcasted_iota(jnp.int32, (GROUPS, ROWS), 1), 4)
    rest = jnp.where(group_of == lax.broadcasted_iota(jnp.int32, (GROUPS, ROWS), 0), total, 0.0)
    low_bits = jnp.bitwise_and(lax.broadcasted_iota(jnp.int32, (ROWS, BLOCK), 0), GROUP - 1)
    low_lane = jnp.bitwise_and(lax.broadcasted_iota(jnp.int32, (ROWS, BLOCK), 1), GROUP - 1)
    fold = (low_bits == low_lane).astype(f32).astype(bf16)
    folded = jnp.zeros((GROUPS, BLOCK), f32)
    for _ in range(3):
        piece = rest.astype(bf16)
        rest = rest - piece.astype(f32)
        folded = folded + jnp.dot(piece, fold, preferred_element_type=f32)
    for g in range(GROUPS):
        gate_rows[g] = folded[g:g + 1]
    mine = lax.shift_right_logical(lax.broadcasted_iota(jnp.int32, (1, BLOCK), 1), 4) == chip

    for d in range(CHIPS):
        lines = []
        for j in range(LEVELS):
            slot = (2 * d + core) * LEVELS + j
            value = jnp.where(alive[slot] > 0, gate_rows[place[slot]], 0.0)
            lines.append(jnp.where(mine, value, 0.0))
        gate_slots[d] = jnp.concatenate(lines + [jnp.zeros((2, BLOCK), f32)], axis=0)

    def give_slots(i, c):
        d = (chip + i) % CHIPS
        give(gate_slots.at[d], gate_back.at[chip], gate_sem.at[2], gate_sem.at[3], 2 * d + core)
        return c
    lax.fori_loop(0, CHIPS, give_slots, 0)

    wait_bytes(g_recv, gr_sem.at[1])
    ug_out[...] = jnp.sum(g_recv[0].astype(f32), axis=0)
    dg_out[...] = jnp.sum(g_recv[1].astype(f32), axis=0)
    wait_bytes(h_recv, hr_sem.at[1])
    hg_out[...] = h_recv[...]
    wait_bytes(sum_recv, sum_sem.at[1])
    wg_out[...] = sum_recv[...].reshape(WIDTH, WIDTH).astype(f32)
    wait_bytes(gate_back, gate_sem.at[3])
    gg_out[...] = jnp.sum(gate_back[...], axis=0)

    for h in range(2):
        wait_bytes(recv_rows[h].at[pl.ds(0, 15 * LEVELS)], in_sem.at[h])
    wait_bytes(recv_rid.at[pl.ds(0, 15)], in_sem.at[2])
    wait_bytes(maps.at[pl.ds(0, 15)], in_sem.at[4])

    @pl.when(is_cot)
    def _():
        for h in range(2):
            to_across(h).wait_send()

    @pl.when(jnp.logical_not(is_cot))
    def _():
        to_partner().wait_send()
    for h in range(2):
        for slot in range(1, 7):
            to_right(ring.at[slot, h], slot, h).wait_send()
        to_right(ring.at[7, h], 7, h).wait_send()
    wait_bytes(part_recv.at[pl.ds(0, 15)], p_sem.at[0])
    wait_bytes(proj, p_sem.at[2])
    wait_bytes(g_send.at[pl.ds(0, 15)], gr_sem.at[0])
    wait_bytes(w_send.at[pl.ds(0, 7)], wg_send)
    wait_bytes(sum_send.at[pl.ds(0, 7)], sum_sem.at[0])
    for d in range(CHIPS):
        to_other(d).wait_send()
    wait_bytes(h_send.at[pl.ds(0, 7)], hr_sem.at[0])
    wait_bytes(gate_recv.at[pl.ds(0, 31)], gate_sem.at[0])
    wait_bytes(gate_slots.at[pl.ds(0, 7)], gate_sem.at[2])


def local(hidden, cotangent, router_gate, recursion_depth, live_counts, out_weight, adapter_down, adapter_up):
    rider = jnp.stack([router_gate.astype(f32), recursion_depth.astype(f32)]).reshape(2, LEVELS, BLOCK)
    rider = jnp.pad(rider, ((0, 0), (0, 2), (0, 0))).reshape(16, BLOCK)
    split = (LEVELS, CHIPS, GROUP, WIDTH)
    blocks = live_counts // BLOCK
    finish = jnp.cumsum(blocks)
    begin = finish - blocks
    level = jnp.arange(LEVELS, dtype=jnp.int32)
    alive = level[None, :] < blocks[:, None]
    place = jnp.where(alive, begin[:, None] + level[None, :], 0)
    order = jnp.arange(GROUPS, dtype=jnp.int32)
    past = finish[None, :] <= order[:, None]
    source = jnp.sum(past.astype(jnp.int32), axis=1)
    first = jnp.max(jnp.where(past, finish[None, :], 0), axis=1)
    pick = source * LEVELS + order - first
    vmem = pl.BlockSpec(memory_space=pltpu.VMEM)
    grouped = (GROUPS, GROUP, WIDTH)
    slots = (CHIPS, LEVELS, GROUP, WIDTH)
    dma = pltpu.SemaphoreType.DMA
    out = pl.pallas_call(
        local_kernel,
        out_shape=(
            jax.ShapeDtypeStruct(slots, bf16),
            jax.ShapeDtypeStruct((8, BLOCK), f32),
            jax.ShapeDtypeStruct((WIDTH, WIDTH), f32),
            jax.ShapeDtypeStruct((PIECE, WIDTH), f32),
            jax.ShapeDtypeStruct((PIECE, WIDTH), f32),
        ),
        in_specs=[pl.BlockSpec(memory_space=pltpu.SMEM)] * 3 + [vmem] * 5 + [pl.BlockSpec(memory_space=pl.ANY)],
        out_specs=(vmem,) * 5,
        scratch_shapes=[
            pltpu.VMEM((96, GROUP, HALF), bf16),
            pltpu.VMEM((96, GROUP, HALF), bf16),
            pltpu.VMEM((16, 16, BLOCK), f32),
            pltpu.VMEM((96, GROUP, BLOCK), f32),
            pltpu.VMEM((96, GROUP, BLOCK), f32),
            pltpu.VMEM((GROUPS, GROUP, BLOCK), f32),
            pltpu.VMEM((GROUPS, GROUP, BLOCK), f32),
            pltpu.VMEM(grouped, bf16),
            pltpu.VMEM(grouped, bf16),
            pltpu.VMEM(grouped, bf16),
            pltpu.VMEM((RING, 2, GROUPS, GROUP, HALF), bf16),
            pltpu.VMEM((RING, 2, HALF, WIDTH), bf16),
            pltpu.VMEM(grouped, f32),
            pltpu.VMEM((RING, CHIPS, PIECE, WIDTH), bf16),
            pltpu.VMEM((RING, CHIPS, PIECE, WIDTH), bf16),
            pltpu.VMEM((RING, PIECE, WIDTH), bf16),
            pltpu.VMEM((CHIPS, PIECE, WIDTH), bf16),
            pltpu.VMEM((16, PIECE, WIDTH), bf16),
            pltpu.VMEM((ROWS, RANK), bf16),
            pltpu.VMEM((PEERS, PART, RANK), bf16),
            pltpu.VMEM((PART, RANK), bf16),
            pltpu.VMEM((PEERS, PART, RANK), bf16),
            pltpu.VMEM((ROWS, NREC * RANK), bf16),
            pltpu.VMEM((16, PIECE, WIDTH), bf16),
            pltpu.VMEM((2, CHIPS, PIECE, WIDTH), bf16),
            pltpu.VMEM(slots, bf16),
            pltpu.VMEM(slots, bf16),
            pltpu.VMEM(slots, bf16),
            pltpu.VMEM(slots, bf16),
            pltpu.VMEM((1, ROWS), f32),
            pltpu.VMEM((32, 1, ROWS), f32),
            pltpu.VMEM((GROUPS, 1, BLOCK), f32),
            pltpu.VMEM((CHIPS, 8, BLOCK), f32),
            pltpu.VMEM((CHIPS, 8, BLOCK), f32),
            dma((8,)),
            dma((RING,)),
            dma((RING, 2)),
            dma((RING, 2)),
            dma((2,)),
            dma((4,)),
            dma,
            dma((RING,)),
            dma((2,)),
            dma((2,)),
            dma((CHIPS,)),
            dma((CHIPS,)),
            dma((2,)),
            dma((4,)),
        ],
        compiler_params=pltpu.CompilerParams(
            collective_id=0, has_side_effects=True, vmem_limit_bytes=VMEM_LIMIT
        ),
    )(
        pick, place.reshape(96), alive.reshape(96).astype(jnp.int32), cotangent.reshape(split), hidden.reshape(split), rider,
        adapter_up, adapter_down.T, out_weight.reshape(PEERS, 2, HALF, WIDTH),
    )
    hidden_grad, gate_back, weight_grad, down_grad, up_grad = out
    hidden_grad = hidden_grad.transpose(1, 0, 2, 3).reshape(hidden.shape).astype(f32)
    return hidden_grad, gate_back[:LEVELS].reshape(-1), weight_grad, down_grad, up_grad


def solution(mesh):
    in_specs = (
        P("seq", "tp"),
        P("seq", "tp"),
        P("seq"),
        P("seq"),
        P(),
        P(None, "tp"),
        P("tp", "seq"),
        P("seq", "tp"),
    )
    out_specs = (P("seq", "tp"), P("seq"), P("seq", "tp"), P("seq", "tp"), P("seq", "tp"))
    return jax.shard_map(local, mesh=mesh, in_specs=in_specs, out_specs=out_specs, check_vma=False)
```

```python
import functools

import jax
import jax.numpy as jnp
from jax import lax
from jax.experimental import pallas as pl
from jax.experimental.pallas import tpu as pltpu
from jax.sharding import PartitionSpec as P

NREC = 4
BLOCK = 128
GROUP = 16
CHIPS = 8
LEVELS = 6
GROUPS = 48
ROWS = GROUPS * GROUP
RING = 8
WIDTH = 512
HALF = WIDTH // 2
RANK = 256
PART = 48
PEERS = 16
PIECE = 64
VMEM_LIMIT = 60 * 1024 * 1024

contract_rows = (((0,), (0,)), ((), ()))
contract_last = (((1,), (1,)), ((), ()))
bf16 = jnp.bfloat16
f32 = jnp.float32


def local_kernel(
    pick, place, alive, cot_ref, hid_ref, rid_ref, up_ref, down_ref, w_ref,
    hg_out, gg_out, wg_out, dg_out, ug_out,
    recv_low, recv_high, recv_rid, slot_gate, slot_depth, gates, depths,
    rows, hid, gated_hid, ring, weights, pre,
    w_send, a_recv, b_send, b_recv, sum_send, sum_recv, maps, part_send, part_recv, part_sum, proj, wide,
    g_send, g_recv, x_send, x_recv, h_send, h_recv,
    gate_part, gate_recv, gate_rows, gate_slots, gate_back,
    in_sem, w_sem, ring_send, ring_recv, hid_sem, p_sem, wg_send, wg_recv, b_sem, sum_sem, map_sem,
    gr_sem, x_ssem, x_rsem, hr_sem, gate_sem,
):
    s = lax.axis_index("seq")
    t = lax.axis_index("tp")
    core = s % 2
    chip = s // 2
    z = t // 2
    xl = t % 2
    is_cot = core == xl
    kind = (core + xl) % 2
    x_at = chip // 4
    y_at = chip % 4
    recv_rows = (recv_low, recv_high)

    def remote(src, dst, ssem, rsem, seq, tp):
        return pltpu.make_async_remote_copy(
            src_ref=src, dst_ref=dst, send_sem=ssem, recv_sem=rsem,
            device_id={"seq": seq, "tp": tp}, device_id_type=pl.DeviceIdType.MESH,
        )

    def wait_bytes(ref, sem):
        pltpu.make_async_copy(ref, ref, sem).wait()

    barrier = pltpu.get_barrier_semaphore()

    def greet_tp(i, c):
        for other in range(2):
            pl.semaphore_signal(barrier, inc=1, device_id={"seq": 2 * chip + other, "tp": (t + i) % 16},
                                device_id_type=pl.DeviceIdType.MESH)
        return c
    lax.fori_loop(1, 16, greet_tp, 0)

    def greet_seq(i, c):
        pl.semaphore_signal(barrier, inc=1, device_id={"seq": (s + i) % 16, "tp": t},
                            device_id_type=pl.DeviceIdType.MESH)
        return c
    lax.fori_loop(1, 16, greet_seq, 0)

    def load_weights(j, c):
        pltpu.make_async_copy(w_ref.at[2 * j + core], weights.at[j], w_sem.at[j]).start()
        return c
    lax.fori_loop(0, RING, load_weights, 0)
    pl.semaphore_wait(barrier, 45)

    def give(src, dst, sem_out, sem_in, seq):
        @pl.when(seq == s)
        def _():
            pltpu.make_async_copy(src, dst, sem_in).start()

        @pl.when(seq != s)
        def _():
            remote(src, dst, sem_out, sem_in, seq, t).start()

    my_slots = pl.ds(s * LEVELS, LEVELS)

    def half(h):
        return pl.ds(h * HALF, HALF)

    def send_first(h, i, c):
        d = (chip + i) % CHIPS
        give(cot_ref.at[:, d, :, half(h)], recv_rows[h].at[my_slots], in_sem.at[h], in_sem.at[6 + h], 2 * d + xl)
        return c
    for h in range(2):
        lax.fori_loop(0, CHIPS, functools.partial(send_first, h), 0)

    def send_rid(i, c):
        d = (chip + i) % CHIPS
        for other in range(2):
            give(rid_ref, recv_rid.at[s], in_sem.at[2], in_sem.at[3], 2 * d + other)
        return c
    lax.fori_loop(0, CHIPS, send_rid, 0)

    def send_second():
        def send_hid(i, c):
            d = (chip + i) % CHIPS
            for h in range(2):
                give(hid_ref.at[:, d, :, half(h)], recv_rows[h].at[my_slots], in_sem.at[h], in_sem.at[6 + h],
                     2 * d + 1 - xl)
            return c
        lax.fori_loop(0, CHIPS, send_hid, 0)

        for x2 in range(2):
            d = 4 * ((x_at + x2) % 2) + y_at
            mine = maps.at[x_at, y_at, core]
            give(up_ref, mine, in_sem.at[4], in_sem.at[5], 2 * d + xl)
            give(down_ref, mine, in_sem.at[4], in_sem.at[5], 2 * d + 1 - xl)

    right = 2 * ((z + 1) % RING) + xl
    left = 2 * ((z + RING - 1) % RING) + xl
    across = 2 * z + 1 - xl
    partner = 2 * chip + 1 - core

    def to_right(src, slot, h):
        return remote(src, ring.at[slot, h], ring_send.at[slot, h], ring_recv.at[slot, h], s, right)

    def to_left(src, slot, h):
        return remote(src, ring.at[slot, h], ring_send.at[slot, h], ring_recv.at[slot, h], s, left)

    def to_across(h):
        return remote(ring.at[0, h], ring.at[0, h], ring_send.at[0, h], ring_recv.at[0, h], s, across)

    def to_partner():
        return remote(hid, hid, hid_sem.at[0], hid_sem.at[1], partner, t)

    def forward(i):
        for h in range(2):
            wait_bytes(ring.at[i, h], ring_recv.at[i, h])
            if i < 5 or h == 0:
                to_right(ring.at[i, h], i + 2, h).start()
            wait_bytes(ring.at[i + 1, h], ring_recv.at[i + 1, h])
            if i < 5:
                to_left(ring.at[i + 1, h], i + 3, h).start()
            elif h == 1:
                to_left(ring.at[6, h], 7, h).start()

    @pl.when(is_cot)
    def _():
        for h in range(2):
            wait_bytes(recv_rows[h], in_sem.at[6 + h])

            def pack(g, c):
                value = recv_rows[h][pick[g]]
                rows[g, :, h * HALF:(h + 1) * HALF] = value
                ring[0, h, g] = value
                return c
            lax.fori_loop(0, GROUPS, pack, 0, unroll=4)
            to_across(h).start()
            to_right(ring.at[0, h], 1, h).start()
            to_left(ring.at[0, h], 2, h).start()

    @pl.when(jnp.logical_not(is_cot))
    def _():
        for h in range(2):
            wait_bytes(ring.at[0, h], ring_recv.at[0, h])
            to_right(ring.at[0, h], 1, h).start()
            to_left(ring.at[0, h], 2, h).start()
    send_second()

    wait_bytes(recv_rid, in_sem.at[3])
    lane = lax.broadcasted_iota(jnp.int32, (GROUP, BLOCK), 1)
    row = lax.broadcasted_iota(jnp.int32, (GROUP, BLOCK), 0)
    chosen = (lane == chip * GROUP + row).astype(f32).astype(bf16)
    columns = lax.dot_general(chosen, recv_rid[...].reshape(16 * GROUP, BLOCK).astype(bf16), contract_last,
                              preferred_element_type=f32)
    for i in range(16):
        for j in range(LEVELS):
            at = i * GROUP + j
            slot_gate[i * LEVELS + j] = jnp.broadcast_to(columns[:, at:at + 1], (GROUP, BLOCK))
            slot_depth[i * LEVELS + j] = jnp.broadcast_to(columns[:, at + 8:at + 9], (GROUP, BLOCK))

    def pack_rid(g, c):
        gates[g] = slot_gate[pick[g]]
        depths[g] = slot_depth[pick[g]]
        return c
    lax.fori_loop(0, GROUPS, pack_rid, 0, unroll=4)
    pre[...] = jnp.zeros_like(pre)

    wait_bytes(maps.at[:, 0], in_sem.at[5])

    def to_column(i):
        d = 4 * x_at + (y_at + i) % 4
        return remote(maps.at[:, y_at], maps.at[:, y_at], map_sem.at[0], map_sem.at[1], 2 * d + core, t)
    for i in range(1, 4):
        to_column(i).start()
    forward(1)

    @pl.when(jnp.logical_not(is_cot))
    def _():
        for h in range(2):
            wait_bytes(recv_rows[h], in_sem.at[6 + h])

            def pack(g, c):
                value = recv_rows[h][pick[g]]
                rows[g, :, h * HALF:(h + 1) * HALF] = value
                hid[g, :, h * HALF:(h + 1) * HALF] = value
                return c
            lax.fori_loop(0, GROUPS, pack, 0, unroll=4)
        to_partner().start()

    wait_bytes(maps.at[:, pl.ds(0, 3)], map_sem.at[1])

    def project(r, c):
        groups = pl.ds(r * GROUP, GROUP)
        x = rows[groups].reshape(RANK, WIDTH)
        y = lax.dot_general(x, maps[...].reshape(NREC * RANK, WIDTH), contract_last, preferred_element_type=f32)
        depth = depths[groups].reshape(RANK, BLOCK)[:, 0:1]
        total = jnp.zeros((RANK, RANK), f32)
        for d in range(NREC):
            total = total + jnp.where(depth == d + 1.0, y[:, d * RANK:(d + 1) * RANK], 0.0)
        part_send[pl.ds(r * RANK, RANK)] = total.astype(bf16)
        return c
    lax.fori_loop(0, ROWS // RANK, project, 0)

    def same_kind(t2):
        return 2 * chip + (core + xl + t2) % 2

    def send_part(i, c):
        t2 = (t + i) % PEERS
        remote(part_send.at[pl.ds(t2 * PART, PART)], part_recv.at[t], p_sem.at[0], p_sem.at[1],
               same_kind(t2), t2).start()
        return c
    lax.fori_loop(1, PEERS, send_part, 0)
    pltpu.make_async_copy(part_send.at[pl.ds(t * PART, PART)], part_recv.at[t], p_sem.at[1]).start()

    @pl.when(is_cot)
    def _():
        wait_bytes(hid, hid_sem.at[1])

    def apply_gate(g, c):
        gate = gates[g][:, 0:1]
        gated_hid[g] = (gate * hid[g].astype(f32)).astype(bf16)
        rows[g] = (gate * rows[g].astype(f32)).astype(bf16)
        return c
    lax.fori_loop(0, GROUPS, apply_gate, 0, unroll=4)

    def origin_of(i):
        shift = jnp.where(i % 2 == 1, 2 * RING - (i + 1) // 2, i // 2)
        return (z + shift) % RING

    def compute(i, c):
        origin = origin_of(i)
        pltpu.make_async_copy(w_ref.at[0], weights.at[origin], w_sem.at[origin]).wait()
        for h in range(2):
            w_send[i, h] = lax.dot_general(
                ring[i, h].reshape(ROWS, HALF), gated_hid[...].reshape(ROWS, WIDTH), contract_rows,
                preferred_element_type=f32).astype(bf16).reshape(4, PIECE, WIDTH)

        @pl.when(i % 2 == 1)
        def _():
            remote(w_send.at[i, 1 - x_at], a_recv.at[i, 0], wg_send.at[0], wg_recv.at[i],
                   2 * (4 * (1 - x_at) + y_at) + core, t).start()

        @pl.when(i % 2 == 0)
        def _():
            def scatter(j, c):
                y2 = (y_at + j) % 4
                give(w_send.at[i, :, y2], a_recv.at[i, :, y_at], wg_send.at[0], wg_recv.at[i],
                     2 * (4 * x_at + y2) + core)
                return c
            lax.fori_loop(0, 4, scatter, 0)
        term = jnp.dot(ring[i, 0].reshape(ROWS, HALF), weights[origin, 0], preferred_element_type=f32)
        term = term + jnp.dot(ring[i, 1].reshape(ROWS, HALF), weights[origin, 1], preferred_element_type=f32)
        pre[...] = pre[...] + term.reshape(GROUPS, GROUP, WIDTH)
        return c

    def second(i, c):
        @pl.when(i % 2 == 1)
        def _():
            wait_bytes(a_recv.at[i, 0], wg_recv.at[i])
            b_send[i] = (w_send[i, x_at].astype(f32) + a_recv[i, 0].astype(f32)).astype(bf16)

            def scatter(j, c):
                y2 = (y_at + j) % 4
                give(b_send.at[i, y2], b_recv.at[i, y_at], wg_send.at[1], b_sem.at[i],
                     2 * (4 * x_at + y2) + core)
                return c
            lax.fori_loop(0, 4, scatter, 0)

        @pl.when(i % 2 == 0)
        def _():
            wait_bytes(a_recv.at[i], wg_recv.at[i])
            for x2 in range(2):
                b_send[i, x2] = jnp.sum(a_recv[i, x2].astype(f32), axis=0).astype(bf16)
            remote(b_send.at[i, 1 - x_at], b_recv.at[i, 0], wg_send.at[1], b_sem.at[i],
                   2 * (4 * (1 - x_at) + y_at) + core, t).start()
        return c

    def third(i, c):
        @pl.when(i % 2 == 1)
        def _():
            wait_bytes(b_recv.at[i], b_sem.at[i])
            sum_send[i] = jnp.sum(b_recv[i].astype(f32), axis=0).astype(bf16)

        @pl.when(i % 2 == 0)
        def _():
            wait_bytes(b_recv.at[i, 0], b_sem.at[i])
            sum_send[i] = (b_send[i, x_at].astype(f32) + b_recv[i, 0].astype(f32)).astype(bf16)
        give(sum_send.at[i], sum_recv.at[chip], sum_sem.at[0], sum_sem.at[1], 2 * origin_of(i) + core)
        return c

    def run(i, c):
        @pl.when(i == 3)
        def _():
            forward(3)
            wait_bytes(part_recv, p_sem.at[1])
            part_sum[...] = jnp.sum(part_recv[...].astype(f32), axis=0).astype(bf16)

            def send_sum(j, c):
                t2 = (t + j) % PEERS
                remote(part_sum, proj.at[t], p_sem.at[2], p_sem.at[3],
                       4 * chip + 1 - same_kind(t2), t2).start()
                return c
            lax.fori_loop(0, PEERS, send_sum, 0)

        @pl.when(i == 5)
        def _():
            forward(5)

        @pl.when(i == RING - 1)
        def _():
            wait_bytes(proj, p_sem.at[3])
            flat = proj[...].reshape(ROWS, RANK)
            depth = depths[...].reshape(ROWS, BLOCK)[:, 0:1]
            for d in range(NREC):
                wide[:, d * RANK:(d + 1) * RANK] = jnp.where(
                    depth == d + 1.0, 0.5 * flat.astype(f32), 0.0).astype(bf16)

            @pl.when(jnp.logical_not(is_cot))
            def _():
                def add_adapter(r, c):
                    groups = pl.ds(r * GROUP, GROUP)
                    term = jnp.dot(wide[pl.ds(r * RANK, RANK)], maps[...].reshape(NREC * RANK, WIDTH),
                                   preferred_element_type=f32)
                    pre[groups] = pre[groups] + term.reshape(GROUP, GROUP, WIDTH)
                    return c
                lax.fori_loop(0, ROWS // RANK, add_adapter, 0)

            for q in range(NREC):
                grad = lax.dot_general(wide[:, q * RANK:(q + 1) * RANK], rows[...].reshape(ROWS, WIDTH),
                                       contract_rows, preferred_element_type=f32)
                g_send[q * 4:(q + 1) * 4] = grad.astype(bf16).reshape(4, PIECE, WIDTH)

            def send_grad(j, c):
                to = (s + j) % 16
                remote(g_send.at[to], g_recv.at[kind, chip], gr_sem.at[0], gr_sem.at[1], to, t).start()
                return c
            lax.fori_loop(1, 16, send_grad, 0)
            pltpu.make_async_copy(g_send.at[s], g_recv.at[kind, chip], gr_sem.at[1]).start()
            lax.fori_loop(5, 7, second, 0)
            lax.fori_loop(2, 5, third, 0)
            for h in range(2):
                wait_bytes(ring.at[RING - 1, h], ring_recv.at[RING - 1, h])

        compute(i, c)

        @pl.when(i == 4)
        def _():
            lax.fori_loop(0, 2, second, 0)

        @pl.when(i == 6)
        def _():
            lax.fori_loop(2, 5, second, 0)
            lax.fori_loop(0, 2, third, 0)
        return c
    lax.fori_loop(0, RING, run, 0)

    ones = jnp.ones((8, WIDTH), bf16)
    for r in range(ROWS // RANK):
        groups = slice(r * GROUP, (r + 1) * GROUP)
        prod = pre[groups].reshape(RANK, WIDTH) * hid[groups].reshape(RANK, WIDTH).astype(f32)
        high = prod.astype(bf16)
        low = (prod - high.astype(f32)).astype(bf16)
        lanes = lax.dot_general(ones, high, contract_last, preferred_element_type=f32)
        lanes = lanes + lax.dot_general(ones, low, contract_last, preferred_element_type=f32)
        gate_part[:, r * RANK:(r + 1) * RANK] = lanes[0:1]
    me = 2 * t + core

    def send_gate(j, c):
        t2 = (t + j) % PEERS
        for other in range(2):
            remote(gate_part, gate_recv.at[me], gate_sem.at[0], gate_sem.at[1], 2 * chip + other, t2).start()
        return c
    lax.fori_loop(1, PEERS, send_gate, 0)
    remote(gate_part, gate_recv.at[me], gate_sem.at[0], gate_sem.at[1], partner, t).start()
    pltpu.make_async_copy(gate_part, gate_recv.at[me], gate_sem.at[1]).start()

    def slot_rows(slot):
        gate = slot_gate[slot][:, 0:1]
        return jnp.where(alive[slot] > 0, gate * pre[place[slot]], 0.0)

    def to_other(d):
        return remote(x_send.at[d], x_recv.at[d], x_ssem.at[d], x_rsem.at[d], partner, t)

    def expand(i, c):
        d = (chip + i) % CHIPS
        for j in range(LEVELS):
            x_send[d, j] = slot_rows((2 * d + 1 - core) * LEVELS + j).astype(bf16)
        to_other(d).start()
        return c
    lax.fori_loop(0, CHIPS, expand, 0)

    def give_back(i, c):
        d = (chip + i) % CHIPS
        wait_bytes(x_recv.at[d], x_rsem.at[d])
        for j in range(LEVELS):
            value = slot_rows((2 * d + core) * LEVELS + j) + x_recv[d, j].astype(f32)
            h_send[d, j] = value.astype(bf16)
        give(h_send.at[d], h_recv.at[chip], hr_sem.at[0], hr_sem.at[1], 2 * d + core)
        return c
    lax.fori_loop(0, CHIPS, give_back, 0)
    lax.fori_loop(5, 7, third, 0)
    second(RING - 1, 0)
    third(RING - 1, 0)

    wait_bytes(gate_recv, gate_sem.at[1])
    total = jnp.sum(gate_recv[...], axis=0)
    group_of = lax.shift_right_logical(lax.broadcasted_iota(jnp.int32, (GROUPS, ROWS), 1), 4)
    rest = jnp.where(group_of == lax.broadcasted_iota(jnp.int32, (GROUPS, ROWS), 0), total, 0.0)
    low_bits = jnp.bitwise_and(lax.broadcasted_iota(jnp.int32, (ROWS, BLOCK), 0), GROUP - 1)
    low_lane = jnp.bitwise_and(lax.broadcasted_iota(jnp.int32, (ROWS, BLOCK), 1), GROUP - 1)
    fold = (low_bits == low_lane).astype(f32).astype(bf16)
    folded = jnp.zeros((GROUPS, BLOCK), f32)
    for _ in range(3):
        piece = rest.astype(bf16)
        rest = rest - piece.astype(f32)
        folded = folded + jnp.dot(piece, fold, preferred_element_type=f32)
    for g in range(GROUPS):
        gate_rows[g] = folded[g:g + 1]
    mine = lax.shift_right_logical(lax.broadcasted_iota(jnp.int32, (1, BLOCK), 1), 4) == chip

    for d in range(CHIPS):
        lines = []
        for j in range(LEVELS):
            slot = (2 * d + core) * LEVELS + j
            value = jnp.where(alive[slot] > 0, gate_rows[place[slot]], 0.0)
            lines.append(jnp.where(mine, value, 0.0))
        gate_slots[d] = jnp.concatenate(lines + [jnp.zeros((2, BLOCK), f32)], axis=0)

    def give_slots(i, c):
        d = (chip + i) % CHIPS
        give(gate_slots.at[d], gate_back.at[chip], gate_sem.at[2], gate_sem.at[3], 2 * d + core)
        return c
    lax.fori_loop(0, CHIPS, give_slots, 0)

    wait_bytes(g_recv, gr_sem.at[1])
    ug_out[...] = jnp.sum(g_recv[0].astype(f32), axis=0)
    dg_out[...] = jnp.sum(g_recv[1].astype(f32), axis=0)
    wait_bytes(h_recv, hr_sem.at[1])
    hg_out[...] = h_recv[...]
    wait_bytes(sum_recv, sum_sem.at[1])
    wg_out[...] = sum_recv[...].reshape(WIDTH, WIDTH).astype(f32)
    wait_bytes(gate_back, gate_sem.at[3])
    gg_out[...] = jnp.sum(gate_back[...], axis=0)

    for h in range(2):
        wait_bytes(recv_rows[h].at[pl.ds(0, 15 * LEVELS)], in_sem.at[h])
    wait_bytes(recv_rid.at[pl.ds(0, 15)], in_sem.at[2])
    wait_bytes(maps.at[0, pl.ds(0, 3), 0], in_sem.at[4])
    wait_bytes(maps.at[:, pl.ds(0, 3)], map_sem.at[0])

    @pl.when(is_cot)
    def _():
        for h in range(2):
            to_across(h).wait_send()

    @pl.when(jnp.logical_not(is_cot))
    def _():
        to_partner().wait_send()
    for h in range(2):
        for slot in range(1, 7):
            to_right(ring.at[slot, h], slot, h).wait_send()
        to_right(ring.at[7, h], 7, h).wait_send()
    wait_bytes(part_recv.at[pl.ds(0, 15)], p_sem.at[0])
    wait_bytes(proj, p_sem.at[2])
    wait_bytes(g_send.at[pl.ds(0, 15)], gr_sem.at[0])
    wait_bytes(w_send.at[pl.ds(0, 5)], wg_send.at[0])
    wait_bytes(b_send.at[pl.ds(0, 4)], wg_send.at[1])
    wait_bytes(sum_send.at[pl.ds(0, 7)], sum_sem.at[0])
    for d in range(CHIPS):
        to_other(d).wait_send()
    wait_bytes(h_send.at[pl.ds(0, 7)], hr_sem.at[0])
    wait_bytes(gate_recv.at[pl.ds(0, 31)], gate_sem.at[0])
    wait_bytes(gate_slots.at[pl.ds(0, 7)], gate_sem.at[2])


def local(hidden, cotangent, router_gate, recursion_depth, live_counts, out_weight, adapter_down, adapter_up):
    rider = jnp.stack([router_gate.astype(f32), recursion_depth.astype(f32)]).reshape(2, LEVELS, BLOCK)
    rider = jnp.pad(rider, ((0, 0), (0, 2), (0, 0))).reshape(16, BLOCK)
    split = (LEVELS, CHIPS, GROUP, WIDTH)
    blocks = live_counts // BLOCK
    finish = jnp.cumsum(blocks)
    begin = finish - blocks
    level = jnp.arange(LEVELS, dtype=jnp.int32)
    alive = level[None, :] < blocks[:, None]
    place = jnp.where(alive, begin[:, None] + level[None, :], 0)
    order = jnp.arange(GROUPS, dtype=jnp.int32)
    past = finish[None, :] <= order[:, None]
    source = jnp.sum(past.astype(jnp.int32), axis=1)
    first = jnp.max(jnp.where(past, finish[None, :], 0), axis=1)
    pick = source * LEVELS + order - first
    vmem = pl.BlockSpec(memory_space=pltpu.VMEM)
    grouped = (GROUPS, GROUP, WIDTH)
    slots = (CHIPS, LEVELS, GROUP, WIDTH)
    dma = pltpu.SemaphoreType.DMA
    out = pl.pallas_call(
        local_kernel,
        out_shape=(
            jax.ShapeDtypeStruct(slots, bf16),
            jax.ShapeDtypeStruct((8, BLOCK), f32),
            jax.ShapeDtypeStruct((WIDTH, WIDTH), f32),
            jax.ShapeDtypeStruct((PIECE, WIDTH), f32),
            jax.ShapeDtypeStruct((PIECE, WIDTH), f32),
        ),
        in_specs=[pl.BlockSpec(memory_space=pltpu.SMEM)] * 3 + [vmem] * 5 + [pl.BlockSpec(memory_space=pl.ANY)],
        out_specs=(vmem,) * 5,
        scratch_shapes=[
            pltpu.VMEM((96, GROUP, HALF), bf16),
            pltpu.VMEM((96, GROUP, HALF), bf16),
            pltpu.VMEM((16, 16, BLOCK), f32),
            pltpu.VMEM((96, GROUP, BLOCK), f32),
            pltpu.VMEM((96, GROUP, BLOCK), f32),
            pltpu.VMEM((GROUPS, GROUP, BLOCK), f32),
            pltpu.VMEM((GROUPS, GROUP, BLOCK), f32),
            pltpu.VMEM(grouped, bf16),
            pltpu.VMEM(grouped, bf16),
            pltpu.VMEM(grouped, bf16),
            pltpu.VMEM((RING, 2, GROUPS, GROUP, HALF), bf16),
            pltpu.VMEM((RING, 2, HALF, WIDTH), bf16),
            pltpu.VMEM(grouped, f32),
            pltpu.VMEM((RING, 2, 4, PIECE, WIDTH), bf16),
            pltpu.VMEM((RING, 2, 4, PIECE, WIDTH), bf16),
            pltpu.VMEM((RING, 4, PIECE, WIDTH), bf16),
            pltpu.VMEM((RING, 4, PIECE, WIDTH), bf16),
            pltpu.VMEM((RING, PIECE, WIDTH), bf16),
            pltpu.VMEM((CHIPS, PIECE, WIDTH), bf16),
            pltpu.VMEM((2, 4, 2, PIECE, WIDTH), bf16),
            pltpu.VMEM((ROWS, RANK), bf16),
            pltpu.VMEM((PEERS, PART, RANK), bf16),
            pltpu.VMEM((PART, RANK), bf16),
            pltpu.VMEM((PEERS, PART, RANK), bf16),
            pltpu.VMEM((ROWS, NREC * RANK), bf16),
            pltpu.VMEM((16, PIECE, WIDTH), bf16),
            pltpu.VMEM((2, CHIPS, PIECE, WIDTH), bf16),
            pltpu.VMEM(slots, bf16),
            pltpu.VMEM(slots, bf16),
            pltpu.VMEM(slots, bf16),
            pltpu.VMEM(slots, bf16),
            pltpu.VMEM((1, ROWS), f32),
            pltpu.VMEM((32, 1, ROWS), f32),
            pltpu.VMEM((GROUPS, 1, BLOCK), f32),
            pltpu.VMEM((CHIPS, 8, BLOCK), f32),
            pltpu.VMEM((CHIPS, 8, BLOCK), f32),
            dma((8,)),
            dma((RING,)),
            dma((RING, 2)),
            dma((RING, 2)),
            dma((2,)),
            dma((4,)),
            dma((2,)),
            dma((RING,)),
            dma((RING,)),
            dma((2,)),
            dma((2,)),
            dma((2,)),
            dma((CHIPS,)),
            dma((CHIPS,)),
            dma((2,)),
            dma((4,)),
        ],
        compiler_params=pltpu.CompilerParams(
            collective_id=0, has_side_effects=True, vmem_limit_bytes=VMEM_LIMIT
        ),
    )(
        pick, place.reshape(96), alive.reshape(96).astype(jnp.int32), cotangent.reshape(split), hidden.reshape(split), rider,
        adapter_up, adapter_down.T, out_weight.reshape(PEERS, 2, HALF, WIDTH),
    )
    hidden_grad, gate_back, weight_grad, down_grad, up_grad = out
    hidden_grad = hidden_grad.transpose(1, 0, 2, 3).reshape(hidden.shape).astype(f32)
    return hidden_grad, gate_back[:LEVELS].reshape(-1), weight_grad, down_grad, up_grad


def solution(mesh):
    in_specs = (
        P("seq", "tp"),
        P("seq", "tp"),
        P("seq"),
        P("seq"),
        P(),
        P(None, "tp"),
        P("tp", "seq"),
        P("seq", "tp"),
    )
    out_specs = (P("seq", "tp"), P("seq"), P("seq", "tp"), P("seq", "tp"), P("seq", "tp"))
    return jax.shard_map(local, mesh=mesh, in_specs=in_specs, out_specs=out_specs, check_vma=False)
```

```python
import functools

import jax
import jax.numpy as jnp
from jax import lax
from jax.experimental import pallas as pl
from jax.experimental.pallas import tpu as pltpu
from jax.sharding import PartitionSpec as P

NREC = 4
BLOCK = 128
GROUP = 16
CHIPS = 8
LEVELS = 6
GROUPS = 48
ROWS = GROUPS * GROUP
RING = 8
WIDTH = 512
HALF = WIDTH // 2
RANK = 256
PART = 48
PEERS = 16
PIECE = 64
VMEM_LIMIT = 60 * 1024 * 1024

contract_rows = (((0,), (0,)), ((), ()))
contract_last = (((1,), (1,)), ((), ()))
bf16 = jnp.bfloat16
f32 = jnp.float32


def local_kernel(
    pick, place, cot_ref, hid_ref, gate_ref, depth_ref, up_ref, down_ref, w_ref,
    hg_out, gg_out, wg_out, dg_out, ug_out,
    recv_low, recv_high, rid_send, recv_rid, slot_gate, slot_depth, gates, depths,
    rows, hid, gated_hid, ring, weights, pre,
    w_send, a_recv, b_send, b_recv, sum_send, sum_recv, maps, part_send, part_recv, part_sum, proj, wide,
    g_send, g_recv, x_send, x_recv, h_send, h_recv,
    gate_part, gate_recv, gate_rows, gate_slots, gate_back,
    in_sem, w_sem, ring_send, ring_recv, hid_sem, p_sem, wg_send, wg_recv, b_sem, sum_sem, map_sem,
    gr_sem, x_ssem, x_rsem, hr_sem, gate_sem,
):
    s = lax.axis_index("seq")
    t = lax.axis_index("tp")
    core = s % 2
    chip = s // 2
    z = t // 2
    xl = t % 2
    is_cot = core == xl
    kind = (core + xl) % 2
    x_at = chip // 4
    y_at = chip % 4
    recv_rows = (recv_low, recv_high)

    def remote(src, dst, ssem, rsem, seq, tp):
        return pltpu.make_async_remote_copy(
            src_ref=src, dst_ref=dst, send_sem=ssem, recv_sem=rsem,
            device_id={"seq": seq, "tp": tp}, device_id_type=pl.DeviceIdType.MESH,
        )

    def wait_bytes(ref, sem):
        pltpu.make_async_copy(ref, ref, sem).wait()

    barrier = pltpu.get_barrier_semaphore()

    def greet_tp(i, c):
        for other in range(2):
            pl.semaphore_signal(barrier, inc=1, device_id={"seq": 2 * chip + other, "tp": (t + i) % 16},
                                device_id_type=pl.DeviceIdType.MESH)
        return c
    lax.fori_loop(1, 16, greet_tp, 0)

    def greet_seq(i, c):
        pl.semaphore_signal(barrier, inc=1, device_id={"seq": (s + i) % 16, "tp": t},
                            device_id_type=pl.DeviceIdType.MESH)
        return c
    lax.fori_loop(1, 16, greet_seq, 0)

    def load_weights(j, c):
        pltpu.make_async_copy(w_ref.at[2 * j + core], weights.at[j], w_sem.at[j]).start()
        return c
    lax.fori_loop(0, RING, load_weights, 0)
    pl.semaphore_wait(barrier, 45)

    def give(src, dst, sem_out, sem_in, seq):
        @pl.when(seq == s)
        def _():
            pltpu.make_async_copy(src, dst, sem_in).start()

        @pl.when(seq != s)
        def _():
            remote(src, dst, sem_out, sem_in, seq, t).start()

    my_slots = pl.ds(s * LEVELS, LEVELS)

    def half(h):
        return pl.ds(h * HALF, HALF)

    def send_first(h, i, c):
        d = (chip + i) % CHIPS
        give(cot_ref.at[:, d, :, half(h)], recv_rows[h].at[my_slots], in_sem.at[h], in_sem.at[6 + h], 2 * d + xl)
        return c
    for h in range(2):
        lax.fori_loop(0, CHIPS, functools.partial(send_first, h), 0)

    rid_send[...] = jnp.zeros_like(rid_send)
    rid_send[0:LEVELS] = gate_ref[...].astype(f32)
    rid_send[8:8 + LEVELS] = depth_ref[...].astype(f32)

    def send_rid(i, c):
        d = (chip + i) % CHIPS
        for other in range(2):
            give(rid_send, recv_rid.at[s], in_sem.at[2], in_sem.at[3], 2 * d + other)
        return c
    lax.fori_loop(0, CHIPS, send_rid, 0)

    def send_hid():
        def send(i, c):
            d = (chip + i) % CHIPS
            for h in range(2):
                give(hid_ref.at[:, d, :, half(h)], recv_rows[h].at[my_slots], in_sem.at[h], in_sem.at[6 + h],
                     2 * d + 1 - xl)
            return c
        lax.fori_loop(0, CHIPS, send, 0)

    for x2 in range(2):
        d = 4 * ((x_at + x2) % 2) + y_at
        mine = maps.at[x_at, y_at, core]
        give(up_ref, mine, in_sem.at[4], in_sem.at[5], 2 * d + xl)
        give(down_ref, mine, in_sem.at[4], in_sem.at[5], 2 * d + 1 - xl)

    def to_column(i):
        d = 4 * x_at + (y_at + i) % 4
        return remote(maps.at[:, y_at], maps.at[:, y_at], map_sem.at[0], map_sem.at[1], 2 * d + core, t)

    def pass_maps():
        wait_bytes(maps.at[:, 0], in_sem.at[5])
        for i in range(1, 4):
            to_column(i).start()

    right = 2 * ((z + 1) % RING) + xl
    left = 2 * ((z + RING - 1) % RING) + xl
    across = 2 * z + 1 - xl
    partner = 2 * chip + 1 - core

    def to_right(src, slot, h):
        return remote(src, ring.at[slot, h], ring_send.at[slot, h], ring_recv.at[slot, h], s, right)

    def to_left(src, slot, h):
        return remote(src, ring.at[slot, h], ring_send.at[slot, h], ring_recv.at[slot, h], s, left)

    def to_across(h):
        return remote(ring.at[0, h], ring.at[0, h], ring_send.at[0, h], ring_recv.at[0, h], s, across)

    def to_partner():
        return remote(hid, hid, hid_sem.at[0], hid_sem.at[1], partner, t)

    def forward(i):
        for h in range(2):
            wait_bytes(ring.at[i, h], ring_recv.at[i, h])
            if i < 5 or h == 0:
                to_right(ring.at[i, h], i + 2, h).start()
            wait_bytes(ring.at[i + 1, h], ring_recv.at[i + 1, h])
            if i < 5:
                to_left(ring.at[i + 1, h], i + 3, h).start()
            elif h == 1:
                to_left(ring.at[6, h], 7, h).start()

    @pl.when(is_cot)
    def _():
        for h in range(2):
            wait_bytes(recv_rows[h], in_sem.at[6 + h])

            def pack(g, c):
                value = recv_rows[h][pick[g]]
                rows[g, :, h * HALF:(h + 1) * HALF] = value
                ring[0, h, g] = value
                return c
            lax.fori_loop(0, GROUPS, pack, 0, unroll=4)
            to_across(h).start()
            to_right(ring.at[0, h], 1, h).start()
            to_left(ring.at[0, h], 2, h).start()
        pass_maps()

    @pl.when(jnp.logical_not(is_cot))
    def _():
        pass_maps()
        for h in range(2):
            wait_bytes(ring.at[0, h], ring_recv.at[0, h])
            to_right(ring.at[0, h], 1, h).start()
            to_left(ring.at[0, h], 2, h).start()
    send_hid()

    wait_bytes(recv_rid, in_sem.at[3])
    lane = lax.broadcasted_iota(jnp.int32, (GROUP, BLOCK), 1)
    row = lax.broadcasted_iota(jnp.int32, (GROUP, BLOCK), 0)
    chosen = (lane == chip * GROUP + row).astype(f32).astype(bf16)
    columns = lax.dot_general(chosen, recv_rid[...].reshape(16 * GROUP, BLOCK).astype(bf16), contract_last,
                              preferred_element_type=f32)
    for i in range(16):
        for j in range(LEVELS):
            at = i * GROUP + j
            slot_gate[i * LEVELS + j] = jnp.broadcast_to(columns[:, at:at + 1], (GROUP, BLOCK))
            slot_depth[i * LEVELS + j] = jnp.broadcast_to(columns[:, at + 8:at + 9], (GROUP, BLOCK))

    def pack_rid(g, c):
        gates[g] = slot_gate[pick[g]]
        depths[g] = slot_depth[pick[g]]
        return c
    lax.fori_loop(0, GROUPS, pack_rid, 0, unroll=4)
    pre[...] = jnp.zeros_like(pre)

    forward(1)

    @pl.when(jnp.logical_not(is_cot))
    def _():
        for h in range(2):
            wait_bytes(recv_rows[h], in_sem.at[6 + h])

            def pack(g, c):
                value = recv_rows[h][pick[g]]
                rows[g, :, h * HALF:(h + 1) * HALF] = value
                hid[g, :, h * HALF:(h + 1) * HALF] = value
                return c
            lax.fori_loop(0, GROUPS, pack, 0, unroll=4)
        to_partner().start()

    wait_bytes(maps.at[:, pl.ds(0, 3)], map_sem.at[1])

    def project(r, c):
        groups = pl.ds(r * GROUP, GROUP)
        x = rows[groups].reshape(RANK, WIDTH)
        y = lax.dot_general(x, maps[...].reshape(NREC * RANK, WIDTH), contract_last, preferred_element_type=f32)
        depth = depths[groups].reshape(RANK, BLOCK)[:, 0:1]
        total = jnp.zeros((RANK, RANK), f32)
        for d in range(NREC):
            total = total + jnp.where(depth == d + 1.0, y[:, d * RANK:(d + 1) * RANK], 0.0)
        part_send[pl.ds(r * RANK, RANK)] = total.astype(bf16)
        return c
    lax.fori_loop(0, ROWS // RANK, project, 0)

    def same_kind(t2):
        return 2 * chip + (core + xl + t2) % 2

    def send_part(i, c):
        t2 = (t + i) % PEERS
        remote(part_send.at[pl.ds(t2 * PART, PART)], part_recv.at[t], p_sem.at[0], p_sem.at[1],
               same_kind(t2), t2).start()
        return c
    lax.fori_loop(1, PEERS, send_part, 0)
    pltpu.make_async_copy(part_send.at[pl.ds(t * PART, PART)], part_recv.at[t], p_sem.at[1]).start()

    @pl.when(is_cot)
    def _():
        wait_bytes(hid, hid_sem.at[1])

    def apply_gate(g, c):
        gate = gates[g][:, 0:1]
        gated_hid[g] = (gate * hid[g].astype(f32)).astype(bf16)
        rows[g] = (gate * rows[g].astype(f32)).astype(bf16)
        return c
    lax.fori_loop(0, GROUPS, apply_gate, 0, unroll=4)

    def origin_of(i):
        shift = jnp.where(i % 2 == 1, 2 * RING - (i + 1) // 2, i // 2)
        return (z + shift) % RING

    def compute(i, c):
        origin = origin_of(i)
        pltpu.make_async_copy(w_ref.at[0], weights.at[origin], w_sem.at[origin]).wait()
        for h in range(2):
            w_send[i, h] = lax.dot_general(
                ring[i, h].reshape(ROWS, HALF), gated_hid[...].reshape(ROWS, WIDTH), contract_rows,
                preferred_element_type=f32).astype(bf16).reshape(4, PIECE, WIDTH)

        @pl.when(i % 2 == 1)
        def _():
            remote(w_send.at[i, 1 - x_at], a_recv.at[i, 0], wg_send.at[0], wg_recv.at[i],
                   2 * (4 * (1 - x_at) + y_at) + core, t).start()

        @pl.when(i % 2 == 0)
        def _():
            def scatter(j, c):
                y2 = (y_at + j) % 4
                give(w_send.at[i, :, y2], a_recv.at[i, :, y_at], wg_send.at[0], wg_recv.at[i],
                     2 * (4 * x_at + y2) + core)
                return c
            lax.fori_loop(0, 4, scatter, 0)
        term = jnp.dot(ring[i, 0].reshape(ROWS, HALF), weights[origin, 0], preferred_element_type=f32)
        term = term + jnp.dot(ring[i, 1].reshape(ROWS, HALF), weights[origin, 1], preferred_element_type=f32)
        pre[...] = pre[...] + term.reshape(GROUPS, GROUP, WIDTH)
        return c

    def second(i, c):
        @pl.when(i % 2 == 1)
        def _():
            wait_bytes(a_recv.at[i, 0], wg_recv.at[i])
            b_send[i] = (w_send[i, x_at].astype(f32) + a_recv[i, 0].astype(f32)).astype(bf16)

            def scatter(j, c):
                y2 = (y_at + j) % 4
                give(b_send.at[i, y2], b_recv.at[i, y_at], wg_send.at[1], b_sem.at[i],
                     2 * (4 * x_at + y2) + core)
                return c
            lax.fori_loop(0, 4, scatter, 0)

        @pl.when(i % 2 == 0)
        def _():
            wait_bytes(a_recv.at[i], wg_recv.at[i])
            for x2 in range(2):
                b_send[i, x2] = jnp.sum(a_recv[i, x2].astype(f32), axis=0).astype(bf16)
            remote(b_send.at[i, 1 - x_at], b_recv.at[i, 0], wg_send.at[1], b_sem.at[i],
                   2 * (4 * (1 - x_at) + y_at) + core, t).start()
        return c

    def third(i, c):
        @pl.when(i % 2 == 1)
        def _():
            wait_bytes(b_recv.at[i], b_sem.at[i])
            sum_send[i] = jnp.sum(b_recv[i].astype(f32), axis=0).astype(bf16)

        @pl.when(i % 2 == 0)
        def _():
            wait_bytes(b_recv.at[i, 0], b_sem.at[i])
            sum_send[i] = (b_send[i, x_at].astype(f32) + b_recv[i, 0].astype(f32)).astype(bf16)
        give(sum_send.at[i], sum_recv.at[chip], sum_sem.at[0], sum_sem.at[1], 2 * origin_of(i) + core)
        return c

    def run(i, c):
        @pl.when(i == 3)
        def _():
            forward(3)

        @pl.when(i == 5)
        def _():
            forward(5)

        @pl.when(i == RING - 1)
        def _():
            lax.fori_loop(5, 7, second, 0)
            lax.fori_loop(2, 5, third, 0)
            for h in range(2):
                wait_bytes(ring.at[RING - 1, h], ring_recv.at[RING - 1, h])

        compute(i, c)

        @pl.when(i == 4)
        def _():
            wait_bytes(part_recv, p_sem.at[1])
            part_sum[...] = jnp.sum(part_recv[...].astype(f32), axis=0).astype(bf16)

            def send_sum(j, c):
                t2 = (t + j) % PEERS
                remote(part_sum, proj.at[t], p_sem.at[2], p_sem.at[3],
                       4 * chip + 1 - same_kind(t2), t2).start()
                return c
            lax.fori_loop(0, PEERS, send_sum, 0)
            lax.fori_loop(0, 2, second, 0)

        @pl.when(i == 6)
        def _():
            lax.fori_loop(2, 5, second, 0)
            lax.fori_loop(0, 2, third, 0)
            wait_bytes(proj, p_sem.at[3])
            flat = proj[...].reshape(ROWS, RANK)
            depth = depths[...].reshape(ROWS, BLOCK)[:, 0:1]
            for d in range(NREC):
                wide[:, d * RANK:(d + 1) * RANK] = jnp.where(
                    depth == d + 1.0, 0.5 * flat.astype(f32), 0.0).astype(bf16)

            @pl.when(jnp.logical_not(is_cot))
            def _():
                def add_adapter(r, c):
                    groups = pl.ds(r * GROUP, GROUP)
                    term = jnp.dot(wide[pl.ds(r * RANK, RANK)], maps[...].reshape(NREC * RANK, WIDTH),
                                   preferred_element_type=f32)
                    pre[groups] = pre[groups] + term.reshape(GROUP, GROUP, WIDTH)
                    return c
                lax.fori_loop(0, ROWS // RANK, add_adapter, 0)

            for q in range(NREC):
                grad = lax.dot_general(wide[:, q * RANK:(q + 1) * RANK], rows[...].reshape(ROWS, WIDTH),
                                       contract_rows, preferred_element_type=f32)
                g_send[q * 4:(q + 1) * 4] = grad.astype(bf16).reshape(4, PIECE, WIDTH)

            def send_grad(j, c):
                to = (s + j) % 16
                remote(g_send.at[to], g_recv.at[kind, chip], gr_sem.at[0], gr_sem.at[1], to, t).start()
                return c
            lax.fori_loop(1, 16, send_grad, 0)
            pltpu.make_async_copy(g_send.at[s], g_recv.at[kind, chip], gr_sem.at[1]).start()
        return c
    lax.fori_loop(0, RING, run, 0)

    ones = jnp.ones((8, WIDTH), bf16)
    for r in range(ROWS // RANK):
        groups = slice(r * GROUP, (r + 1) * GROUP)
        prod = pre[groups].reshape(RANK, WIDTH) * hid[groups].reshape(RANK, WIDTH).astype(f32)
        high = prod.astype(bf16)
        low = (prod - high.astype(f32)).astype(bf16)
        lanes = lax.dot_general(ones, high, contract_last, preferred_element_type=f32)
        lanes = lanes + lax.dot_general(ones, low, contract_last, preferred_element_type=f32)
        gate_part[:, r * RANK:(r + 1) * RANK] = lanes[0:1]
    me = 2 * t + core

    def send_gate(j, c):
        t2 = (t + j) % PEERS
        for other in range(2):
            remote(gate_part, gate_recv.at[me], gate_sem.at[0], gate_sem.at[1], 2 * chip + other, t2).start()
        return c
    lax.fori_loop(1, PEERS, send_gate, 0)
    remote(gate_part, gate_recv.at[me], gate_sem.at[0], gate_sem.at[1], partner, t).start()
    pltpu.make_async_copy(gate_part, gate_recv.at[me], gate_sem.at[1]).start()

    def slot_rows(slot):
        gate = slot_gate[slot][:, 0:1]
        at = place[slot]
        return jnp.where(at >= 0, gate * pre[jnp.maximum(at, 0)], 0.0)

    def to_other(d):
        return remote(x_send.at[d], x_recv.at[d], x_ssem.at[d], x_rsem.at[d], partner, t)

    def expand(i, c):
        d = (chip + i) % CHIPS
        for j in range(LEVELS):
            x_send[d, j] = slot_rows((2 * d + 1 - core) * LEVELS + j).astype(bf16)
        to_other(d).start()
        return c
    lax.fori_loop(0, CHIPS, expand, 0)

    def give_back(i, c):
        d = (chip + i) % CHIPS
        wait_bytes(x_recv.at[d], x_rsem.at[d])
        for j in range(LEVELS):
            value = slot_rows((2 * d + core) * LEVELS + j) + x_recv[d, j].astype(f32)
            h_send[d, j] = value.astype(bf16)
        give(h_send.at[d], h_recv.at[chip], hr_sem.at[0], hr_sem.at[1], 2 * d + core)
        return c
    lax.fori_loop(0, CHIPS, give_back, 0)
    second(RING - 1, 0)
    lax.fori_loop(5, RING, third, 0)

    wait_bytes(gate_recv, gate_sem.at[1])
    total = jnp.sum(gate_recv[...], axis=0)
    group_of = lax.shift_right_logical(lax.broadcasted_iota(jnp.int32, (GROUPS, ROWS), 1), 4)
    rest = jnp.where(group_of == lax.broadcasted_iota(jnp.int32, (GROUPS, ROWS), 0), total, 0.0)
    low_bits = jnp.bitwise_and(lax.broadcasted_iota(jnp.int32, (ROWS, BLOCK), 0), GROUP - 1)
    low_lane = jnp.bitwise_and(lax.broadcasted_iota(jnp.int32, (ROWS, BLOCK), 1), GROUP - 1)
    fold = (low_bits == low_lane).astype(f32).astype(bf16)
    folded = jnp.zeros((GROUPS, BLOCK), f32)
    for _ in range(3):
        piece = rest.astype(bf16)
        rest = rest - piece.astype(f32)
        folded = folded + jnp.dot(piece, fold, preferred_element_type=f32)
    for g in range(GROUPS):
        gate_rows[g] = folded[g:g + 1]
    mine = lax.shift_right_logical(lax.broadcasted_iota(jnp.int32, (1, BLOCK), 1), 4) == chip

    for d in range(CHIPS):
        lines = []
        for j in range(LEVELS):
            slot = (2 * d + core) * LEVELS + j
            at = place[slot]
            value = jnp.where(at >= 0, gate_rows[jnp.maximum(at, 0)], 0.0)
            lines.append(jnp.where(mine, value, 0.0))
        gate_slots[d] = jnp.concatenate(lines + [jnp.zeros((2, BLOCK), f32)], axis=0)

    def give_slots(i, c):
        d = (chip + i) % CHIPS
        give(gate_slots.at[d], gate_back.at[chip], gate_sem.at[2], gate_sem.at[3], 2 * d + core)
        return c
    lax.fori_loop(0, CHIPS, give_slots, 0)

    wait_bytes(g_recv, gr_sem.at[1])
    ug_out[...] = jnp.sum(g_recv[0].astype(f32), axis=0)
    dg_out[...] = jnp.sum(g_recv[1].astype(f32), axis=0)
    wait_bytes(h_recv, hr_sem.at[1])
    for d in range(CHIPS):
        hg_out[:, d] = h_recv[d]
    wait_bytes(sum_recv, sum_sem.at[1])
    wg_out[...] = sum_recv[...].reshape(WIDTH, WIDTH)
    wait_bytes(gate_back, gate_sem.at[3])
    gg_out[...] = jnp.sum(gate_back[...], axis=0)

    for h in range(2):
        wait_bytes(recv_rows[h].at[pl.ds(0, 15 * LEVELS)], in_sem.at[h])
    wait_bytes(recv_rid.at[pl.ds(0, 15)], in_sem.at[2])
    wait_bytes(maps.at[0, pl.ds(0, 3), 0], in_sem.at[4])
    wait_bytes(maps.at[:, pl.ds(0, 3)], map_sem.at[0])

    @pl.when(is_cot)
    def _():
        for h in range(2):
            to_across(h).wait_send()

    @pl.when(jnp.logical_not(is_cot))
    def _():
        to_partner().wait_send()
    for h in range(2):
        for slot in range(1, 7):
            to_right(ring.at[slot, h], slot, h).wait_send()
        to_right(ring.at[7, h], 7, h).wait_send()
    wait_bytes(part_recv.at[pl.ds(0, 15)], p_sem.at[0])
    wait_bytes(proj, p_sem.at[2])
    wait_bytes(g_send.at[pl.ds(0, 15)], gr_sem.at[0])
    wait_bytes(w_send.at[pl.ds(0, 5)], wg_send.at[0])
    wait_bytes(b_send.at[pl.ds(0, 4)], wg_send.at[1])
    wait_bytes(sum_send.at[pl.ds(0, 7)], sum_sem.at[0])
    for d in range(CHIPS):
        to_other(d).wait_send()
    wait_bytes(h_send.at[pl.ds(0, 7)], hr_sem.at[0])
    wait_bytes(gate_recv.at[pl.ds(0, 31)], gate_sem.at[0])
    wait_bytes(gate_slots.at[pl.ds(0, 7)], gate_sem.at[2])


def local(hidden, cotangent, router_gate, recursion_depth, live_counts, out_weight, adapter_down, adapter_up):
    split = (LEVELS, CHIPS, GROUP, WIDTH)
    blocks = lax.shift_right_logical(live_counts, 7)
    slot = jnp.arange(96, dtype=jnp.int32)
    shard = jnp.arange(16, dtype=jnp.int32)
    owner = (slot // LEVELS)[:, None]
    before = jnp.sum(jnp.where(shard[None, :] < owner, blocks[None, :], 0), axis=1)
    own = jnp.sum(jnp.where(shard[None, :] == owner, blocks[None, :], 0), axis=1)
    place = jnp.where(slot % LEVELS < own, before + slot % LEVELS, -1)
    order = jnp.arange(GROUPS, dtype=jnp.int32)
    pick = jnp.sum(jnp.where(place[None, :] == order[:, None], slot[None, :], 0), axis=1)
    vmem = pl.BlockSpec(memory_space=pltpu.VMEM)
    grouped = (GROUPS, GROUP, WIDTH)
    slots = (CHIPS, LEVELS, GROUP, WIDTH)
    dma = pltpu.SemaphoreType.DMA
    out = pl.pallas_call(
        local_kernel,
        out_shape=(
            jax.ShapeDtypeStruct(split, bf16),
            jax.ShapeDtypeStruct((8, BLOCK), f32),
            jax.ShapeDtypeStruct((WIDTH, WIDTH), bf16),
            jax.ShapeDtypeStruct((PIECE, WIDTH), f32),
            jax.ShapeDtypeStruct((PIECE, WIDTH), f32),
        ),
        in_specs=[pl.BlockSpec(memory_space=pltpu.SMEM)] * 2 + [vmem] * 6 + [pl.BlockSpec(memory_space=pl.ANY)],
        out_specs=(vmem,) * 5,
        scratch_shapes=[
            pltpu.VMEM((96, GROUP, HALF), bf16),
            pltpu.VMEM((96, GROUP, HALF), bf16),
            pltpu.VMEM((16, BLOCK), f32),
            pltpu.VMEM((16, 16, BLOCK), f32),
            pltpu.VMEM((96, GROUP, BLOCK), f32),
            pltpu.VMEM((96, GROUP, BLOCK), f32),
            pltpu.VMEM((GROUPS, GROUP, BLOCK), f32),
            pltpu.VMEM((GROUPS, GROUP, BLOCK), f32),
            pltpu.VMEM(grouped, bf16),
            pltpu.VMEM(grouped, bf16),
            pltpu.VMEM(grouped, bf16),
            pltpu.VMEM((RING, 2, GROUPS, GROUP, HALF), bf16),
            pltpu.VMEM((RING, 2, HALF, WIDTH), bf16),
            pltpu.VMEM(grouped, f32),
            pltpu.VMEM((RING, 2, 4, PIECE, WIDTH), bf16),
            pltpu.VMEM((RING, 2, 4, PIECE, WIDTH), bf16),
            pltpu.VMEM((RING, 4, PIECE, WIDTH), bf16),
            pltpu.VMEM((RING, 4, PIECE, WIDTH), bf16),
            pltpu.VMEM((RING, PIECE, WIDTH), bf16),
            pltpu.VMEM((CHIPS, PIECE, WIDTH), bf16),
            pltpu.VMEM((2, 4, 2, PIECE, WIDTH), bf16),
            pltpu.VMEM((ROWS, RANK), bf16),
            pltpu.VMEM((PEERS, PART, RANK), bf16),
            pltpu.VMEM((PART, RANK), bf16),
            pltpu.VMEM((PEERS, PART, RANK), bf16),
            pltpu.VMEM((ROWS, NREC * RANK), bf16),
            pltpu.VMEM((16, PIECE, WIDTH), bf16),
            pltpu.VMEM((2, CHIPS, PIECE, WIDTH), bf16),
            pltpu.VMEM(slots, bf16),
            pltpu.VMEM(slots, bf16),
            pltpu.VMEM(slots, bf16),
            pltpu.VMEM(slots, bf16),
            pltpu.VMEM((1, ROWS), f32),
            pltpu.VMEM((32, 1, ROWS), f32),
            pltpu.VMEM((GROUPS, 1, BLOCK), f32),
            pltpu.VMEM((CHIPS, 8, BLOCK), f32),
            pltpu.VMEM((CHIPS, 8, BLOCK), f32),
            dma((8,)),
            dma((RING,)),
            dma((RING, 2)),
            dma((RING, 2)),
            dma((2,)),
            dma((4,)),
            dma((2,)),
            dma((RING,)),
            dma((RING,)),
            dma((2,)),
            dma((2,)),
            dma((2,)),
            dma((CHIPS,)),
            dma((CHIPS,)),
            dma((2,)),
            dma((4,)),
        ],
        compiler_params=pltpu.CompilerParams(
            collective_id=0, has_side_effects=True, vmem_limit_bytes=VMEM_LIMIT
        ),
    )(
        pick, place, cotangent.reshape(split), hidden.reshape(split),
        router_gate.reshape(LEVELS, BLOCK), recursion_depth.reshape(LEVELS, BLOCK),
        adapter_up, adapter_down.T, out_weight.reshape(PEERS, 2, HALF, WIDTH),
    )
    hidden_grad, gate_back, weight_grad, down_grad, up_grad = out
    hidden_grad = hidden_grad.reshape(hidden.shape).astype(f32)
    return hidden_grad, gate_back[:LEVELS].reshape(-1), weight_grad.astype(f32), down_grad, up_grad


def solution(mesh):
    in_specs = (
        P("seq", "tp"),
        P("seq", "tp"),
        P("seq"),
        P("seq"),
        P(),
        P(None, "tp"),
        P("tp", "seq"),
        P("seq", "tp"),
    )
    out_specs = (P("seq", "tp"), P("seq"), P("seq", "tp"), P("seq", "tp"), P("seq", "tp"))
    return jax.shard_map(local, mesh=mesh, in_specs=in_specs, out_specs=out_specs, check_vma=False)
```

```python
import functools

import jax
import jax.numpy as jnp
from jax import lax
from jax.experimental import pallas as pl
from jax.experimental.pallas import tpu as pltpu
from jax.sharding import PartitionSpec as P

NREC = 4
BLOCK = 128
GROUP = 16
CHIPS = 8
LEVELS = 6
GROUPS = 48
ROWS = GROUPS * GROUP
RING = 8
WIDTH = 512
HALF = WIDTH // 2
RANK = 256
PART = 48
PEERS = 16
PIECE = 64
VMEM_LIMIT = 60 * 1024 * 1024

contract_rows = (((0,), (0,)), ((), ()))
contract_last = (((1,), (1,)), ((), ()))
bf16 = jnp.bfloat16
f32 = jnp.float32


def local_kernel(
    pick, place, cot_ref, hid_ref, gate_ref, depth_ref, up_ref, down_ref, w_ref,
    hg_out, gg_out, wg_out, dg_out, ug_out,
    recv_low, recv_high, rid_send, recv_rid, slot_gate, slot_depth, gates, depths,
    rows, hid, gated_hid, ring, weights, pre,
    w_send, a_recv, b_send, b_recv, sum_send, sum_recv, maps, part_send, part_recv, part_sum, proj, wide,
    g_send, g_recv, x_send, x_recv, h_send, h_recv,
    gate_part, gate_recv, gate_rows, gate_slots, gate_back,
    in_sem, w_sem, ring_send, ring_recv, hid_sem, p_sem, wg_send, wg_recv, b_sem, sum_sem, map_sem,
    gr_sem, x_ssem, x_rsem, hr_sem, gate_sem,
):
    s = lax.axis_index("seq")
    t = lax.axis_index("tp")
    core = s % 2
    chip = s // 2
    z = t // 2
    xl = t % 2
    is_cot = core == xl
    kind = (core + xl) % 2
    x_at = chip // 4
    y_at = chip % 4
    recv_rows = (recv_low, recv_high)

    def remote(src, dst, ssem, rsem, seq, tp):
        return pltpu.make_async_remote_copy(
            src_ref=src, dst_ref=dst, send_sem=ssem, recv_sem=rsem,
            device_id={"seq": seq, "tp": tp}, device_id_type=pl.DeviceIdType.MESH,
        )

    def wait_bytes(ref, sem):
        pltpu.make_async_copy(ref, ref, sem).wait()

    barrier = pltpu.get_barrier_semaphore()

    def greet_tp(i, c):
        for other in range(2):
            pl.semaphore_signal(barrier, inc=1, device_id={"seq": 2 * chip + other, "tp": (t + i) % 16},
                                device_id_type=pl.DeviceIdType.MESH)
        return c
    lax.fori_loop(1, 16, greet_tp, 0)

    def greet_seq(i, c):
        pl.semaphore_signal(barrier, inc=1, device_id={"seq": (s + i) % 16, "tp": t},
                            device_id_type=pl.DeviceIdType.MESH)
        return c
    lax.fori_loop(1, 16, greet_seq, 0)

    def load_weights(j, c):
        pltpu.make_async_copy(w_ref.at[2 * j + core], weights.at[j], w_sem.at[j]).start()
        return c
    lax.fori_loop(0, RING, load_weights, 0)
    pl.semaphore_wait(barrier, 45)

    def give(src, dst, sem_out, sem_in, seq):
        @pl.when(seq == s)
        def _():
            pltpu.make_async_copy(src, dst, sem_in).start()

        @pl.when(seq != s)
        def _():
            remote(src, dst, sem_out, sem_in, seq, t).start()

    my_slots = pl.ds(s * LEVELS, LEVELS)

    def half(h):
        return pl.ds(h * HALF, HALF)

    def send_first(h, i, c):
        d = (chip + i) % CHIPS
        give(cot_ref.at[:, d, :, half(h)], recv_rows[h].at[my_slots], in_sem.at[h], in_sem.at[6 + h], 2 * d + xl)
        return c
    for h in range(2):
        lax.fori_loop(0, CHIPS, functools.partial(send_first, h), 0)

    rid_send[...] = jnp.zeros_like(rid_send)
    rid_send[0:LEVELS] = gate_ref[...].astype(f32)
    rid_send[8:8 + LEVELS] = depth_ref[...].astype(f32)

    def send_rid(i, c):
        d = (chip + i) % CHIPS
        for other in range(2):
            give(rid_send, recv_rid.at[s], in_sem.at[2], in_sem.at[3], 2 * d + other)
        return c
    lax.fori_loop(0, CHIPS, send_rid, 0)

    def send_hid():
        def send(i, c):
            d = (chip + i) % CHIPS
            for h in range(2):
                give(hid_ref.at[:, d, :, half(h)], recv_rows[h].at[my_slots], in_sem.at[h], in_sem.at[6 + h],
                     2 * d + 1 - xl)
            return c
        lax.fori_loop(0, CHIPS, send, 0)

    for x2 in range(2):
        d = 4 * ((x_at + x2) % 2) + y_at
        mine = maps.at[x_at, y_at, core]
        give(up_ref, mine, in_sem.at[4], in_sem.at[5], 2 * d + xl)
        give(down_ref, mine, in_sem.at[4], in_sem.at[5], 2 * d + 1 - xl)

    def to_column(i):
        d = 4 * x_at + (y_at + i) % 4
        return remote(maps.at[:, y_at], maps.at[:, y_at], map_sem.at[0], map_sem.at[1], 2 * d + core, t)

    def pass_maps():
        wait_bytes(maps.at[:, 0], in_sem.at[5])
        for i in range(1, 4):
            to_column(i).start()

    right = 2 * ((z + 1) % RING) + xl
    left = 2 * ((z + RING - 1) % RING) + xl
    across = 2 * z + 1 - xl
    partner = 2 * chip + 1 - core

    def to_right(src, slot, h):
        return remote(src, ring.at[slot, h], ring_send.at[slot, h], ring_recv.at[slot, h], s, right)

    def to_left(src, slot, h):
        return remote(src, ring.at[slot, h], ring_send.at[slot, h], ring_recv.at[slot, h], s, left)

    def to_across(h):
        return remote(ring.at[0, h], ring.at[0, h], ring_send.at[0, h], ring_recv.at[0, h], s, across)

    def to_partner():
        return remote(hid, hid, hid_sem.at[0], hid_sem.at[1], partner, t)

    def forward(i):
        for h in range(2):
            wait_bytes(ring.at[i, h], ring_recv.at[i, h])
            if i < 5 or h == 0:
                to_right(ring.at[i, h], i + 2, h).start()
            wait_bytes(ring.at[i + 1, h], ring_recv.at[i + 1, h])
            if i < 5:
                to_left(ring.at[i + 1, h], i + 3, h).start()
            elif h == 1:
                to_left(ring.at[6, h], 7, h).start()

    @pl.when(is_cot)
    def _():
        for h in range(2):
            wait_bytes(recv_rows[h], in_sem.at[6 + h])

            def pack(g, c):
                value = recv_rows[h][pick[g]]
                rows[g, :, h * HALF:(h + 1) * HALF] = value
                ring[0, h, g] = value
                return c
            lax.fori_loop(0, GROUPS, pack, 0, unroll=4)
            to_across(h).start()
            to_right(ring.at[0, h], 1, h).start()
            to_left(ring.at[0, h], 2, h).start()
        pass_maps()

    @pl.when(jnp.logical_not(is_cot))
    def _():
        pass_maps()
        for h in range(2):
            wait_bytes(ring.at[0, h], ring_recv.at[0, h])
            to_right(ring.at[0, h], 1, h).start()
            to_left(ring.at[0, h], 2, h).start()
    send_hid()

    wait_bytes(recv_rid, in_sem.at[3])
    lane = lax.broadcasted_iota(jnp.int32, (GROUP, BLOCK), 1)
    row = lax.broadcasted_iota(jnp.int32, (GROUP, BLOCK), 0)
    chosen = (lane == chip * GROUP + row).astype(f32).astype(bf16)
    columns = lax.dot_general(chosen, recv_rid[...].reshape(16 * GROUP, BLOCK).astype(bf16), contract_last,
                              preferred_element_type=f32)
    for i in range(16):
        for j in range(LEVELS):
            at = i * GROUP + j
            slot_gate[i * LEVELS + j] = jnp.broadcast_to(columns[:, at:at + 1], (GROUP, BLOCK))
            slot_depth[i * LEVELS + j] = jnp.broadcast_to(columns[:, at + 8:at + 9], (GROUP, BLOCK))

    def pack_rid(g, c):
        gates[g] = slot_gate[pick[g]]
        depths[g] = slot_depth[pick[g]]
        return c
    lax.fori_loop(0, GROUPS, pack_rid, 0, unroll=4)
    pre[...] = jnp.zeros_like(pre)

    forward(1)

    @pl.when(jnp.logical_not(is_cot))
    def _():
        for h in range(2):
            wait_bytes(recv_rows[h], in_sem.at[6 + h])

            def pack(g, c):
                value = recv_rows[h][pick[g]]
                rows[g, :, h * HALF:(h + 1) * HALF] = value
                hid[g, :, h * HALF:(h + 1) * HALF] = value
                return c
            lax.fori_loop(0, GROUPS, pack, 0, unroll=4)
        to_partner().start()

    wait_bytes(maps.at[:, pl.ds(0, 3)], map_sem.at[1])

    def project(r, c):
        groups = pl.ds(r * GROUP, GROUP)
        x = rows[groups].reshape(RANK, WIDTH)
        y = lax.dot_general(x, maps[...].reshape(NREC * RANK, WIDTH), contract_last, preferred_element_type=f32)
        depth = depths[groups].reshape(RANK, BLOCK)[:, 0:1]
        total = jnp.zeros((RANK, RANK), f32)
        for d in range(NREC):
            total = total + jnp.where(depth == d + 1.0, y[:, d * RANK:(d + 1) * RANK], 0.0)
        part_send[pl.ds(r * RANK, RANK)] = total.astype(bf16)
        return c
    lax.fori_loop(0, ROWS // RANK, project, 0)

    def same_kind(t2):
        return 2 * chip + (core + xl + t2) % 2

    def send_part(i, c):
        t2 = (t + i) % PEERS
        remote(part_send.at[pl.ds(t2 * PART, PART)], part_recv.at[t], p_sem.at[0], p_sem.at[1],
               same_kind(t2), t2).start()
        return c
    lax.fori_loop(1, PEERS, send_part, 0)
    pltpu.make_async_copy(part_send.at[pl.ds(t * PART, PART)], part_recv.at[t], p_sem.at[1]).start()

    @pl.when(is_cot)
    def _():
        wait_bytes(hid, hid_sem.at[1])

    def apply_gate(g, c):
        gate = gates[g][:, 0:1]
        gated_hid[g] = (gate * hid[g].astype(f32)).astype(bf16)
        rows[g] = (gate * rows[g].astype(f32)).astype(bf16)
        return c
    lax.fori_loop(0, GROUPS, apply_gate, 0, unroll=4)

    def origin_of(i):
        shift = jnp.where(i % 2 == 1, 2 * RING - (i + 1) // 2, i // 2)
        return (z + shift) % RING

    def compute(i, c):
        origin = origin_of(i)
        pltpu.make_async_copy(w_ref.at[0], weights.at[origin], w_sem.at[origin]).wait()
        for h in range(2):
            w_send[i, h] = lax.dot_general(
                ring[i, h].reshape(ROWS, HALF), gated_hid[...].reshape(ROWS, WIDTH), contract_rows,
                preferred_element_type=f32).astype(bf16).reshape(4, PIECE, WIDTH)

        @pl.when(i % 2 == 1)
        def _():
            remote(w_send.at[i, 1 - x_at], a_recv.at[i, 0], wg_send.at[0], wg_recv.at[i],
                   2 * (4 * (1 - x_at) + y_at) + core, t).start()

        @pl.when(i % 2 == 0)
        def _():
            def scatter(j, c):
                y2 = (y_at + j) % 4
                give(w_send.at[i, :, y2], a_recv.at[i, :, y_at], wg_send.at[0], wg_recv.at[i],
                     2 * (4 * x_at + y2) + core)
                return c
            lax.fori_loop(0, 4, scatter, 0)
        term = jnp.dot(ring[i, 0].reshape(ROWS, HALF), weights[origin, 0], preferred_element_type=f32)
        term = term + jnp.dot(ring[i, 1].reshape(ROWS, HALF), weights[origin, 1], preferred_element_type=f32)
        pre[...] = pre[...] + term.reshape(GROUPS, GROUP, WIDTH)
        return c

    def second(i, c):
        @pl.when(i % 2 == 1)
        def _():
            wait_bytes(a_recv.at[i, 0], wg_recv.at[i])
            b_send[i] = (w_send[i, x_at].astype(f32) + a_recv[i, 0].astype(f32)).astype(bf16)

            def scatter(j, c):
                y2 = (y_at + j) % 4
                give(b_send.at[i, y2], b_recv.at[i, y_at], wg_send.at[1], b_sem.at[i],
                     2 * (4 * x_at + y2) + core)
                return c
            lax.fori_loop(0, 4, scatter, 0)

        @pl.when(i % 2 == 0)
        def _():
            wait_bytes(a_recv.at[i], wg_recv.at[i])
            for x2 in range(2):
                b_send[i, x2] = jnp.sum(a_recv[i, x2].astype(f32), axis=0).astype(bf16)
            remote(b_send.at[i, 1 - x_at], b_recv.at[i, 0], wg_send.at[1], b_sem.at[i],
                   2 * (4 * (1 - x_at) + y_at) + core, t).start()
        return c

    def third(i, c):
        @pl.when(i % 2 == 1)
        def _():
            wait_bytes(b_recv.at[i], b_sem.at[i])
            sum_send[i] = jnp.sum(b_recv[i].astype(f32), axis=0).astype(bf16)

        @pl.when(i % 2 == 0)
        def _():
            wait_bytes(b_recv.at[i, 0], b_sem.at[i])
            sum_send[i] = (b_send[i, x_at].astype(f32) + b_recv[i, 0].astype(f32)).astype(bf16)
        give(sum_send.at[i], sum_recv.at[chip], sum_sem.at[0], sum_sem.at[1], 2 * origin_of(i) + core)
        return c

    def sum_parts():
        wait_bytes(part_recv, p_sem.at[1])
        part_sum[...] = jnp.sum(part_recv[...].astype(f32), axis=0).astype(bf16)

        def send_sum(j, c):
            t2 = (t + j) % PEERS
            remote(part_sum, proj.at[t], p_sem.at[2], p_sem.at[3],
                   4 * chip + 1 - same_kind(t2), t2).start()
            return c
        lax.fori_loop(0, PEERS, send_sum, 0)

    def run(i, c):
        @pl.when(i == 3)
        def _():
            forward(3)

        @pl.when(i == 5)
        def _():
            forward(5)

        @pl.when(i == RING - 1)
        def _():
            lax.fori_loop(5, 7, second, 0)
            lax.fori_loop(2, 5, third, 0)
            for h in range(2):
                wait_bytes(ring.at[RING - 1, h], ring_recv.at[RING - 1, h])

        compute(i, c)

        @pl.when(i == 4)
        def _():
            pl.when(jnp.logical_not(is_cot))(sum_parts)
            lax.fori_loop(0, 2, second, 0)

        @pl.when(i == 6)
        def _():
            lax.fori_loop(2, 5, second, 0)
            lax.fori_loop(0, 2, third, 0)
            wait_bytes(proj, p_sem.at[3])
            flat = proj[...].reshape(ROWS, RANK)
            depth = depths[...].reshape(ROWS, BLOCK)[:, 0:1]
            for d in range(NREC):
                wide[:, d * RANK:(d + 1) * RANK] = jnp.where(
                    depth == d + 1.0, 0.5 * flat.astype(f32), 0.0).astype(bf16)

            @pl.when(jnp.logical_not(is_cot))
            def _():
                def add_adapter(r, c):
                    groups = pl.ds(r * GROUP, GROUP)
                    term = jnp.dot(wide[pl.ds(r * RANK, RANK)], maps[...].reshape(NREC * RANK, WIDTH),
                                   preferred_element_type=f32)
                    pre[groups] = pre[groups] + term.reshape(GROUP, GROUP, WIDTH)
                    return c
                lax.fori_loop(0, ROWS // RANK, add_adapter, 0)

            for q in range(NREC):
                grad = lax.dot_general(wide[:, q * RANK:(q + 1) * RANK], rows[...].reshape(ROWS, WIDTH),
                                       contract_rows, preferred_element_type=f32)
                g_send[q * 4:(q + 1) * 4] = grad.astype(bf16).reshape(4, PIECE, WIDTH)

            def send_grad(j, c):
                to = (s + j) % 16
                remote(g_send.at[to], g_recv.at[kind, chip], gr_sem.at[0], gr_sem.at[1], to, t).start()
                return c
            lax.fori_loop(1, 16, send_grad, 0)
            pltpu.make_async_copy(g_send.at[s], g_recv.at[kind, chip], gr_sem.at[1]).start()
        return c
    pl.when(is_cot)(sum_parts)
    lax.fori_loop(0, RING, run, 0)

    ones = jnp.ones((8, WIDTH), bf16)
    for r in range(ROWS // RANK):
        groups = slice(r * GROUP, (r + 1) * GROUP)
        prod = pre[groups].reshape(RANK, WIDTH) * hid[groups].reshape(RANK, WIDTH).astype(f32)
        high = prod.astype(bf16)
        low = (prod - high.astype(f32)).astype(bf16)
        lanes = lax.dot_general(ones, high, contract_last, preferred_element_type=f32)
        lanes = lanes + lax.dot_general(ones, low, contract_last, preferred_element_type=f32)
        gate_part[:, r * RANK:(r + 1) * RANK] = lanes[0:1]
    me = 2 * t + core

    def send_gate(j, c):
        t2 = (t + j) % PEERS
        for other in range(2):
            remote(gate_part, gate_recv.at[me], gate_sem.at[0], gate_sem.at[1], 2 * chip + other, t2).start()
        return c
    lax.fori_loop(1, PEERS, send_gate, 0)
    remote(gate_part, gate_recv.at[me], gate_sem.at[0], gate_sem.at[1], partner, t).start()
    pltpu.make_async_copy(gate_part, gate_recv.at[me], gate_sem.at[1]).start()

    def slot_rows(slot):
        gate = slot_gate[slot][:, 0:1]
        at = place[slot]
        return jnp.where(at >= 0, gate * pre[jnp.maximum(at, 0)], 0.0)

    def to_other(d):
        return remote(x_send.at[d], x_recv.at[d], x_ssem.at[d], x_rsem.at[d], partner, t)

    def expand(i, c):
        d = (chip + i) % CHIPS
        for j in range(LEVELS):
            x_send[d, j] = slot_rows((2 * d + 1 - core) * LEVELS + j).astype(bf16)
        to_other(d).start()
        return c
    lax.fori_loop(0, CHIPS, expand, 0)

    def give_back(i, c):
        d = (chip + i) % CHIPS
        wait_bytes(x_recv.at[d], x_rsem.at[d])
        for j in range(LEVELS):
            value = slot_rows((2 * d + core) * LEVELS + j) + x_recv[d, j].astype(f32)
            h_send[d, j] = value.astype(bf16)
        give(h_send.at[d], h_recv.at[chip], hr_sem.at[0], hr_sem.at[1], 2 * d + core)
        return c
    lax.fori_loop(0, CHIPS, give_back, 0)
    lax.fori_loop(5, 7, third, 0)
    second(RING - 1, 0)
    wait_bytes(gate_recv, gate_sem.at[1])
    total = jnp.sum(gate_recv[...], axis=0)
    group_of = lax.shift_right_logical(lax.broadcasted_iota(jnp.int32, (GROUPS, ROWS), 1), 4)
    rest = jnp.where(group_of == lax.broadcasted_iota(jnp.int32, (GROUPS, ROWS), 0), total, 0.0)
    low_bits = jnp.bitwise_and(lax.broadcasted_iota(jnp.int32, (ROWS, BLOCK), 0), GROUP - 1)
    low_lane = jnp.bitwise_and(lax.broadcasted_iota(jnp.int32, (ROWS, BLOCK), 1), GROUP - 1)
    fold = (low_bits == low_lane).astype(f32).astype(bf16)
    folded = jnp.zeros((GROUPS, BLOCK), f32)
    for _ in range(3):
        piece = rest.astype(bf16)
        rest = rest - piece.astype(f32)
        folded = folded + jnp.dot(piece, fold, preferred_element_type=f32)
    for g in range(GROUPS):
        gate_rows[g] = folded[g:g + 1]
    mine = lax.shift_right_logical(lax.broadcasted_iota(jnp.int32, (1, BLOCK), 1), 4) == chip

    for d in range(CHIPS):
        lines = []
        for j in range(LEVELS):
            slot = (2 * d + core) * LEVELS + j
            at = place[slot]
            value = jnp.where(at >= 0, gate_rows[jnp.maximum(at, 0)], 0.0)
            lines.append(jnp.where(mine, value, 0.0))
        gate_slots[d] = jnp.concatenate(lines + [jnp.zeros((2, BLOCK), f32)], axis=0)

    def give_slots(i, c):
        d = (chip + i) % CHIPS
        give(gate_slots.at[d], gate_back.at[chip], gate_sem.at[2], gate_sem.at[3], 2 * d + core)
        return c
    lax.fori_loop(0, CHIPS, give_slots, 0)
    third(RING - 1, 0)

    wait_bytes(g_recv, gr_sem.at[1])
    ug_out[...] = jnp.sum(g_recv[0].astype(f32), axis=0)
    dg_out[...] = jnp.sum(g_recv[1].astype(f32), axis=0)
    wait_bytes(h_recv, hr_sem.at[1])
    for d in range(CHIPS):
        hg_out[:, d] = h_recv[d]
    wait_bytes(sum_recv, sum_sem.at[1])
    wg_out[...] = sum_recv[...].reshape(WIDTH, WIDTH)
    wait_bytes(gate_back, gate_sem.at[3])
    gg_out[...] = jnp.sum(gate_back[...], axis=0)

    for h in range(2):
        wait_bytes(recv_rows[h].at[pl.ds(0, 15 * LEVELS)], in_sem.at[h])
    wait_bytes(recv_rid.at[pl.ds(0, 15)], in_sem.at[2])
    wait_bytes(maps.at[0, pl.ds(0, 3), 0], in_sem.at[4])
    wait_bytes(maps.at[:, pl.ds(0, 3)], map_sem.at[0])

    @pl.when(is_cot)
    def _():
        for h in range(2):
            to_across(h).wait_send()

    @pl.when(jnp.logical_not(is_cot))
    def _():
        to_partner().wait_send()
    for h in range(2):
        for slot in range(1, 7):
            to_right(ring.at[slot, h], slot, h).wait_send()
        to_right(ring.at[7, h], 7, h).wait_send()
    wait_bytes(part_recv.at[pl.ds(0, 15)], p_sem.at[0])
    wait_bytes(proj, p_sem.at[2])
    wait_bytes(g_send.at[pl.ds(0, 15)], gr_sem.at[0])
    wait_bytes(w_send.at[pl.ds(0, 5)], wg_send.at[0])
    wait_bytes(b_send.at[pl.ds(0, 4)], wg_send.at[1])
    wait_bytes(sum_send.at[pl.ds(0, 7)], sum_sem.at[0])
    for d in range(CHIPS):
        to_other(d).wait_send()
    wait_bytes(h_send.at[pl.ds(0, 7)], hr_sem.at[0])
    wait_bytes(gate_recv.at[pl.ds(0, 31)], gate_sem.at[0])
    wait_bytes(gate_slots.at[pl.ds(0, 7)], gate_sem.at[2])


def local(hidden, cotangent, router_gate, recursion_depth, live_counts, out_weight, adapter_down, adapter_up):
    split = (LEVELS, CHIPS, GROUP, WIDTH)
    blocks = lax.shift_right_logical(live_counts, 7)
    slot = jnp.arange(96, dtype=jnp.int32)
    shard = jnp.arange(16, dtype=jnp.int32)
    owner = (slot // LEVELS)[:, None]
    before = jnp.sum(jnp.where(shard[None, :] < owner, blocks[None, :], 0), axis=1)
    own = jnp.sum(jnp.where(shard[None, :] == owner, blocks[None, :], 0), axis=1)
    place = jnp.where(slot % LEVELS < own, before + slot % LEVELS, -1)
    order = jnp.arange(GROUPS, dtype=jnp.int32)
    pick = jnp.sum(jnp.where(place[None, :] == order[:, None], slot[None, :], 0), axis=1)
    vmem = pl.BlockSpec(memory_space=pltpu.VMEM)
    grouped = (GROUPS, GROUP, WIDTH)
    slots = (CHIPS, LEVELS, GROUP, WIDTH)
    dma = pltpu.SemaphoreType.DMA
    out = pl.pallas_call(
        local_kernel,
        out_shape=(
            jax.ShapeDtypeStruct(split, bf16),
            jax.ShapeDtypeStruct((8, BLOCK), f32),
            jax.ShapeDtypeStruct((WIDTH, WIDTH), bf16),
            jax.ShapeDtypeStruct((PIECE, WIDTH), f32),
            jax.ShapeDtypeStruct((PIECE, WIDTH), f32),
        ),
        in_specs=[pl.BlockSpec(memory_space=pltpu.SMEM)] * 2 + [vmem] * 6 + [pl.BlockSpec(memory_space=pl.ANY)],
        out_specs=(vmem,) * 5,
        scratch_shapes=[
            pltpu.VMEM((96, GROUP, HALF), bf16),
            pltpu.VMEM((96, GROUP, HALF), bf16),
            pltpu.VMEM((16, BLOCK), f32),
            pltpu.VMEM((16, 16, BLOCK), f32),
            pltpu.VMEM((96, GROUP, BLOCK), f32),
            pltpu.VMEM((96, GROUP, BLOCK), f32),
            pltpu.VMEM((GROUPS, GROUP, BLOCK), f32),
            pltpu.VMEM((GROUPS, GROUP, BLOCK), f32),
            pltpu.VMEM(grouped, bf16),
            pltpu.VMEM(grouped, bf16),
            pltpu.VMEM(grouped, bf16),
            pltpu.VMEM((RING, 2, GROUPS, GROUP, HALF), bf16),
            pltpu.VMEM((RING, 2, HALF, WIDTH), bf16),
            pltpu.VMEM(grouped, f32),
            pltpu.VMEM((RING, 2, 4, PIECE, WIDTH), bf16),
            pltpu.VMEM((RING, 2, 4, PIECE, WIDTH), bf16),
            pltpu.VMEM((RING, 4, PIECE, WIDTH), bf16),
            pltpu.VMEM((RING, 4, PIECE, WIDTH), bf16),
            pltpu.VMEM((RING, PIECE, WIDTH), bf16),
            pltpu.VMEM((CHIPS, PIECE, WIDTH), bf16),
            pltpu.VMEM((2, 4, 2, PIECE, WIDTH), bf16),
            pltpu.VMEM((ROWS, RANK), bf16),
            pltpu.VMEM((PEERS, PART, RANK), bf16),
            pltpu.VMEM((PART, RANK), bf16),
            pltpu.VMEM((PEERS, PART, RANK), bf16),
            pltpu.VMEM((ROWS, NREC * RANK), bf16),
            pltpu.VMEM((16, PIECE, WIDTH), bf16),
            pltpu.VMEM((2, CHIPS, PIECE, WIDTH), bf16),
            pltpu.VMEM(slots, bf16),
            pltpu.VMEM(slots, bf16),
            pltpu.VMEM(slots, bf16),
            pltpu.VMEM(slots, bf16),
            pltpu.VMEM((1, ROWS), f32),
            pltpu.VMEM((32, 1, ROWS), f32),
            pltpu.VMEM((GROUPS, 1, BLOCK), f32),
            pltpu.VMEM((CHIPS, 8, BLOCK), f32),
            pltpu.VMEM((CHIPS, 8, BLOCK), f32),
            dma((8,)),
            dma((RING,)),
            dma((RING, 2)),
            dma((RING, 2)),
            dma((2,)),
            dma((4,)),
            dma((2,)),
            dma((RING,)),
            dma((RING,)),
            dma((2,)),
            dma((2,)),
            dma((2,)),
            dma((CHIPS,)),
            dma((CHIPS,)),
            dma((2,)),
            dma((4,)),
        ],
        compiler_params=pltpu.CompilerParams(
            collective_id=0, has_side_effects=True, vmem_limit_bytes=VMEM_LIMIT
        ),
    )(
        pick, place, cotangent.reshape(split), hidden.reshape(split),
        router_gate.reshape(LEVELS, BLOCK), recursion_depth.reshape(LEVELS, BLOCK),
        adapter_up, adapter_down.T, out_weight.reshape(PEERS, 2, HALF, WIDTH),
    )
    hidden_grad, gate_back, weight_grad, down_grad, up_grad = out
    hidden_grad = hidden_grad.reshape(hidden.shape).astype(f32)
    return hidden_grad, gate_back[:LEVELS].reshape(-1), weight_grad.astype(f32), down_grad, up_grad


def solution(mesh):
    in_specs = (
        P("seq", "tp"),
        P("seq", "tp"),
        P("seq"),
        P("seq"),
        P(),
        P(None, "tp"),
        P("tp", "seq"),
        P("seq", "tp"),
    )
    out_specs = (P("seq", "tp"), P("seq"), P("seq", "tp"), P("seq", "tp"), P("seq", "tp"))
    return jax.shard_map(local, mesh=mesh, in_specs=in_specs, out_specs=out_specs, check_vma=False)
```

```python
import functools

import jax
import jax.numpy as jnp
from jax import lax
from jax.experimental import pallas as pl
from jax.experimental.pallas import tpu as pltpu
from jax.sharding import PartitionSpec as P

NREC = 4
BLOCK = 128
GROUP = 16
CHIPS = 8
LEVELS = 6
GROUPS = 48
ROWS = GROUPS * GROUP
RING = 8
WIDTH = 512
HALF = WIDTH // 2
RANK = 256
PART = 48
PEERS = 16
PIECE = 64
VMEM_LIMIT = 60 * 1024 * 1024

contract_rows = (((0,), (0,)), ((), ()))
contract_last = (((1,), (1,)), ((), ()))
bf16 = jnp.bfloat16
f32 = jnp.float32


def local_kernel(
    pick, place, cot_ref, hid_ref, gate_ref, depth_ref, up_ref, down_ref, w_ref,
    hg_out, gg_out, wg_out, dg_out, ug_out,
    recv_low, recv_high, rid_send, recv_rid, slot_gate, slot_depth, gates, depths,
    rows, hid, gated_hid, ring, weights, pre,
    w_send, a_recv, b_send, b_recv, sum_send, sum_recv, maps, part_send, part_recv, part_sum, proj, wide,
    g_send, g_recv, x_send, x_recv, h_send, h_recv,
    gate_part, gate_recv, gate_rows, gate_slots, gate_back,
    in_sem, w_sem, ring_send, ring_recv, hid_sem, p_sem, wg_send, wg_recv, b_sem, sum_sem, map_sem,
    gr_sem, x_ssem, x_rsem, hr_sem, gate_sem,
):
    s = lax.axis_index("seq")
    t = lax.axis_index("tp")
    core = s % 2
    chip = s // 2
    z = t // 2
    xl = t % 2
    is_cot = core == xl
    kind = (core + xl) % 2
    x_at = chip // 4
    y_at = chip % 4
    recv_rows = (recv_low, recv_high)

    def remote(src, dst, ssem, rsem, seq, tp):
        return pltpu.make_async_remote_copy(
            src_ref=src, dst_ref=dst, send_sem=ssem, recv_sem=rsem,
            device_id={"seq": seq, "tp": tp}, device_id_type=pl.DeviceIdType.MESH,
        )

    def wait_bytes(ref, sem):
        pltpu.make_async_copy(ref, ref, sem).wait()

    barrier = pltpu.get_barrier_semaphore()

    def greet_tp(i, c):
        for other in range(2):
            pl.semaphore_signal(barrier, inc=1, device_id={"seq": 2 * chip + other, "tp": (t + i) % 16},
                                device_id_type=pl.DeviceIdType.MESH)
        return c
    lax.fori_loop(1, 16, greet_tp, 0)

    def greet_seq(i, c):
        pl.semaphore_signal(barrier, inc=1, device_id={"seq": (s + i) % 16, "tp": t},
                            device_id_type=pl.DeviceIdType.MESH)
        return c
    lax.fori_loop(1, 16, greet_seq, 0)

    def load_weights(j, c):
        pltpu.make_async_copy(w_ref.at[2 * j + core], weights.at[j], w_sem.at[j]).start()
        return c
    lax.fori_loop(0, RING, load_weights, 0)
    pl.semaphore_wait(barrier, 45)

    def give(src, dst, sem_out, sem_in, seq):
        @pl.when(seq == s)
        def _():
            pltpu.make_async_copy(src, dst, sem_in).start()

        @pl.when(seq != s)
        def _():
            remote(src, dst, sem_out, sem_in, seq, t).start()

    my_slots = pl.ds(s * LEVELS, LEVELS)

    def half(h):
        return pl.ds(h * HALF, HALF)

    def send_first(h, i, c):
        d = (chip + i) % CHIPS
        give(cot_ref.at[:, d, :, half(h)], recv_rows[h].at[my_slots], in_sem.at[h], in_sem.at[6 + h], 2 * d + xl)
        return c
    for h in range(2):
        lax.fori_loop(0, CHIPS, functools.partial(send_first, h), 0)

    rid_send[...] = jnp.zeros_like(rid_send)
    rid_send[0:LEVELS] = gate_ref[...].astype(f32)
    rid_send[8:8 + LEVELS] = depth_ref[...].astype(f32)

    def send_rid(i, c):
        d = (chip + i) % CHIPS
        for other in range(2):
            give(rid_send, recv_rid.at[s], in_sem.at[2], in_sem.at[3], 2 * d + other)
        return c
    lax.fori_loop(0, CHIPS, send_rid, 0)

    def send_hid():
        def send(i, c):
            d = (chip + i) % CHIPS
            for h in range(2):
                give(hid_ref.at[:, d, :, half(h)], recv_rows[h].at[my_slots], in_sem.at[h], in_sem.at[6 + h],
                     2 * d + 1 - xl)
            return c
        lax.fori_loop(0, CHIPS, send, 0)

    for x2 in range(2):
        d = 4 * ((x_at + x2) % 2) + y_at
        mine = maps.at[x_at, y_at, core]
        give(up_ref, mine, in_sem.at[4], in_sem.at[5], 2 * d + xl)
        give(down_ref, mine, in_sem.at[4], in_sem.at[5], 2 * d + 1 - xl)

    def to_column(i):
        d = 4 * x_at + (y_at + i) % 4
        return remote(maps.at[:, y_at], maps.at[:, y_at], map_sem.at[0], map_sem.at[1], 2 * d + core, t)

    def pass_maps():
        wait_bytes(maps.at[:, 0], in_sem.at[5])
        for i in range(1, 4):
            to_column(i).start()

    right = 2 * ((z + 1) % RING) + xl
    left = 2 * ((z + RING - 1) % RING) + xl
    across = 2 * z + 1 - xl
    partner = 2 * chip + 1 - core

    def to_right(src, slot, h):
        return remote(src, ring.at[slot, h], ring_send.at[slot, h], ring_recv.at[slot, h], s, right)

    def to_left(src, slot, h):
        return remote(src, ring.at[slot, h], ring_send.at[slot, h], ring_recv.at[slot, h], s, left)

    def to_across(h):
        return remote(ring.at[0, h], ring.at[0, h], ring_send.at[0, h], ring_recv.at[0, h], s, across)

    def to_partner():
        return remote(hid, hid, hid_sem.at[0], hid_sem.at[1], partner, t)

    def forward(i):
        for h in range(2):
            wait_bytes(ring.at[i, h], ring_recv.at[i, h])
            if i < 5 or h == 0:
                to_right(ring.at[i, h], i + 2, h).start()
            wait_bytes(ring.at[i + 1, h], ring_recv.at[i + 1, h])
            if i < 5:
                to_left(ring.at[i + 1, h], i + 3, h).start()
            elif h == 1:
                to_left(ring.at[6, h], 7, h).start()

    @pl.when(is_cot)
    def _():
        for h in range(2):
            wait_bytes(recv_rows[h], in_sem.at[6 + h])

            def pack(g, c):
                value = recv_rows[h][pick[g]]
                rows[g, :, h * HALF:(h + 1) * HALF] = value
                ring[0, h, g] = value
                return c
            lax.fori_loop(0, GROUPS, pack, 0, unroll=4)
            to_across(h).start()
            to_right(ring.at[0, h], 1, h).start()
            to_left(ring.at[0, h], 2, h).start()
        pass_maps()

    @pl.when(jnp.logical_not(is_cot))
    def _():
        pass_maps()
        for h in range(2):
            wait_bytes(ring.at[0, h], ring_recv.at[0, h])
            to_right(ring.at[0, h], 1, h).start()
            to_left(ring.at[0, h], 2, h).start()
    send_hid()

    wait_bytes(recv_rid, in_sem.at[3])
    lane = lax.broadcasted_iota(jnp.int32, (GROUP, BLOCK), 1)
    row = lax.broadcasted_iota(jnp.int32, (GROUP, BLOCK), 0)
    chosen = (lane == chip * GROUP + row).astype(f32).astype(bf16)
    columns = lax.dot_general(chosen, recv_rid[...].reshape(16 * GROUP, BLOCK).astype(bf16), contract_last,
                              preferred_element_type=f32)
    for i in range(16):
        for j in range(LEVELS):
            at = i * GROUP + j
            slot_gate[i * LEVELS + j] = jnp.broadcast_to(columns[:, at:at + 1], (GROUP, BLOCK))
            slot_depth[i * LEVELS + j] = jnp.broadcast_to(columns[:, at + 8:at + 9], (GROUP, BLOCK))

    def pack_rid(g, c):
        gates[g] = slot_gate[pick[g]]
        depths[g] = slot_depth[pick[g]]
        return c
    lax.fori_loop(0, GROUPS, pack_rid, 0, unroll=4)
    pre[...] = jnp.zeros_like(pre)

    forward(1)

    @pl.when(jnp.logical_not(is_cot))
    def _():
        for h in range(2):
            wait_bytes(recv_rows[h], in_sem.at[6 + h])

            def pack(g, c):
                value = recv_rows[h][pick[g]]
                rows[g, :, h * HALF:(h + 1) * HALF] = value
                hid[g, :, h * HALF:(h + 1) * HALF] = value
                return c
            lax.fori_loop(0, GROUPS, pack, 0, unroll=4)
        to_partner().start()

    wait_bytes(maps.at[:, pl.ds(0, 3)], map_sem.at[1])

    def project(r, c):
        groups = pl.ds(r * GROUP, GROUP)
        x = rows[groups].reshape(RANK, WIDTH)
        y = lax.dot_general(x, maps[...].reshape(NREC * RANK, WIDTH), contract_last, preferred_element_type=f32)
        depth = depths[groups].reshape(RANK, BLOCK)[:, 0:1]
        total = jnp.zeros((RANK, RANK), f32)
        for d in range(NREC):
            total = total + jnp.where(depth == d + 1.0, y[:, d * RANK:(d + 1) * RANK], 0.0)
        part_send[pl.ds(r * RANK, RANK)] = total.astype(bf16)
        return c
    lax.fori_loop(0, ROWS // RANK, project, 0)

    def same_kind(t2):
        return 2 * chip + (core + xl + t2) % 2

    def send_part(i, c):
        t2 = (t + i) % PEERS
        remote(part_send.at[pl.ds(t2 * PART, PART)], part_recv.at[t], p_sem.at[0], p_sem.at[1],
               same_kind(t2), t2).start()
        return c
    lax.fori_loop(1, PEERS, send_part, 0)
    pltpu.make_async_copy(part_send.at[pl.ds(t * PART, PART)], part_recv.at[t], p_sem.at[1]).start()

    @pl.when(is_cot)
    def _():
        wait_bytes(hid, hid_sem.at[1])

    def apply_gate(g, c):
        gate = gates[g][:, 0:1]
        gated_hid[g] = (gate * hid[g].astype(f32)).astype(bf16)
        rows[g] = (gate * rows[g].astype(f32)).astype(bf16)
        return c
    lax.fori_loop(0, GROUPS, apply_gate, 0, unroll=4)

    def origin_of(i):
        shift = jnp.where(i % 2 == 1, 2 * RING - (i + 1) // 2, i // 2)
        return (z + shift) % RING

    def compute(i, c):
        origin = origin_of(i)
        pltpu.make_async_copy(w_ref.at[0], weights.at[origin], w_sem.at[origin]).wait()
        for h in range(2):
            w_send[i, h] = lax.dot_general(
                ring[i, h].reshape(ROWS, HALF), gated_hid[...].reshape(ROWS, WIDTH), contract_rows,
                preferred_element_type=f32).astype(bf16).reshape(4, PIECE, WIDTH)

        @pl.when(i % 2 == 1)
        def _():
            remote(w_send.at[i, 1 - x_at], a_recv.at[i, 0], wg_send.at[0], wg_recv.at[i],
                   2 * (4 * (1 - x_at) + y_at) + core, t).start()

        @pl.when(i % 2 == 0)
        def _():
            def scatter(j, c):
                y2 = (y_at + j) % 4
                give(w_send.at[i, :, y2], a_recv.at[i, :, y_at], wg_send.at[0], wg_recv.at[i],
                     2 * (4 * x_at + y2) + core)
                return c
            lax.fori_loop(0, 4, scatter, 0)
        term = jnp.dot(ring[i, 0].reshape(ROWS, HALF), weights[origin, 0], preferred_element_type=f32)
        term = term + jnp.dot(ring[i, 1].reshape(ROWS, HALF), weights[origin, 1], preferred_element_type=f32)
        pre[...] = pre[...] + term.reshape(GROUPS, GROUP, WIDTH)
        return c

    def second(i, c):
        @pl.when(i % 2 == 1)
        def _():
            wait_bytes(a_recv.at[i, 0], wg_recv.at[i])
            b_send[i] = (w_send[i, x_at].astype(f32) + a_recv[i, 0].astype(f32)).astype(bf16)

            def scatter(j, c):
                y2 = (y_at + j) % 4
                give(b_send.at[i, y2], b_recv.at[i, y_at], wg_send.at[1], b_sem.at[i],
                     2 * (4 * x_at + y2) + core)
                return c
            lax.fori_loop(0, 4, scatter, 0)

        @pl.when(i % 2 == 0)
        def _():
            wait_bytes(a_recv.at[i], wg_recv.at[i])
            for x2 in range(2):
                b_send[i, x2] = jnp.sum(a_recv[i, x2].astype(f32), axis=0).astype(bf16)
            remote(b_send.at[i, 1 - x_at], b_recv.at[i, 0], wg_send.at[1], b_sem.at[i],
                   2 * (4 * (1 - x_at) + y_at) + core, t).start()
        return c

    def third(i, c):
        @pl.when(i % 2 == 1)
        def _():
            wait_bytes(b_recv.at[i], b_sem.at[i])
            sum_send[i] = jnp.sum(b_recv[i].astype(f32), axis=0).astype(bf16)

        @pl.when(i % 2 == 0)
        def _():
            wait_bytes(b_recv.at[i, 0], b_sem.at[i])
            sum_send[i] = (b_send[i, x_at].astype(f32) + b_recv[i, 0].astype(f32)).astype(bf16)
        give(sum_send.at[i], sum_recv.at[chip], sum_sem.at[0], sum_sem.at[1], 2 * origin_of(i) + core)
        return c

    def sum_parts():
        wait_bytes(part_recv, p_sem.at[1])
        part_sum[...] = jnp.sum(part_recv[...].astype(f32), axis=0).astype(bf16)

        def send_sum(j, c):
            t2 = (t + j) % PEERS
            remote(part_sum, proj.at[t], p_sem.at[2], p_sem.at[3],
                   4 * chip + 1 - same_kind(t2), t2).start()
            return c
        lax.fori_loop(0, PEERS, send_sum, 0)

    def grads():
        wait_bytes(proj, p_sem.at[3])
        flat = proj[...].reshape(ROWS, RANK)
        depth = depths[...].reshape(ROWS, BLOCK)[:, 0:1]
        for d in range(NREC):
            wide[:, d * RANK:(d + 1) * RANK] = jnp.where(
                depth == d + 1.0, 0.5 * flat.astype(f32), 0.0).astype(bf16)

        @pl.when(jnp.logical_not(is_cot))
        def _():
            def add_adapter(r, c):
                groups = pl.ds(r * GROUP, GROUP)
                term = jnp.dot(wide[pl.ds(r * RANK, RANK)], maps[...].reshape(NREC * RANK, WIDTH),
                               preferred_element_type=f32)
                pre[groups] = pre[groups] + term.reshape(GROUP, GROUP, WIDTH)
                return c
            lax.fori_loop(0, ROWS // RANK, add_adapter, 0)

        for q in range(NREC):
            grad = lax.dot_general(wide[:, q * RANK:(q + 1) * RANK], rows[...].reshape(ROWS, WIDTH),
                                   contract_rows, preferred_element_type=f32)
            g_send[q * 4:(q + 1) * 4] = grad.astype(bf16).reshape(4, PIECE, WIDTH)

        def send_grad(j, c):
            to = (s + j) % 16
            remote(g_send.at[to], g_recv.at[kind, chip], gr_sem.at[0], gr_sem.at[1], to, t).start()
            return c
        lax.fori_loop(1, 16, send_grad, 0)
        pltpu.make_async_copy(g_send.at[s], g_recv.at[kind, chip], gr_sem.at[1]).start()

    def run(i, c):
        @pl.when(i == 3)
        def _():
            forward(3)

        @pl.when(i == 5)
        def _():
            forward(5)

        @pl.when(i == RING - 1)
        def _():
            lax.fori_loop(5, 7, second, 0)
            lax.fori_loop(2, 5, third, 0)
            pl.when(is_cot)(grads)
            for h in range(2):
                wait_bytes(ring.at[RING - 1, h], ring_recv.at[RING - 1, h])

        compute(i, c)

        @pl.when(i == 4)
        def _():
            pl.when(jnp.logical_not(is_cot))(sum_parts)
            lax.fori_loop(0, 2, second, 0)
            pl.when(jnp.logical_not(is_cot))(grads)

        @pl.when(i == 6)
        def _():
            lax.fori_loop(2, 5, second, 0)
            lax.fori_loop(0, 2, third, 0)
        return c
    pl.when(is_cot)(sum_parts)
    lax.fori_loop(0, RING, run, 0)

    ones = jnp.ones((8, WIDTH), bf16)
    for r in range(ROWS // RANK):
        groups = slice(r * GROUP, (r + 1) * GROUP)
        prod = pre[groups].reshape(RANK, WIDTH) * hid[groups].reshape(RANK, WIDTH).astype(f32)
        high = prod.astype(bf16)
        low = (prod - high.astype(f32)).astype(bf16)
        lanes = lax.dot_general(ones, high, contract_last, preferred_element_type=f32)
        lanes = lanes + lax.dot_general(ones, low, contract_last, preferred_element_type=f32)
        gate_part[:, r * RANK:(r + 1) * RANK] = lanes[0:1]
    me = 2 * t + core

    def send_gate(j, c):
        t2 = (t + j) % PEERS
        for other in range(2):
            remote(gate_part, gate_recv.at[me], gate_sem.at[0], gate_sem.at[1], 2 * chip + other, t2).start()
        return c
    lax.fori_loop(1, PEERS, send_gate, 0)
    remote(gate_part, gate_recv.at[me], gate_sem.at[0], gate_sem.at[1], partner, t).start()
    pltpu.make_async_copy(gate_part, gate_recv.at[me], gate_sem.at[1]).start()

    def slot_rows(slot):
        gate = slot_gate[slot][:, 0:1]
        at = place[slot]
        return jnp.where(at >= 0, gate * pre[jnp.maximum(at, 0)], 0.0)

    def to_other(d):
        return remote(x_send.at[d], x_recv.at[d], x_ssem.at[d], x_rsem.at[d], partner, t)

    def expand(i, c):
        d = (chip + i) % CHIPS
        for j in range(LEVELS):
            x_send[d, j] = slot_rows((2 * d + 1 - core) * LEVELS + j).astype(bf16)
        to_other(d).start()
        return c
    lax.fori_loop(0, CHIPS, expand, 0)

    def give_back(i, c):
        d = (chip + i) % CHIPS
        wait_bytes(x_recv.at[d], x_rsem.at[d])
        for j in range(LEVELS):
            value = slot_rows((2 * d + core) * LEVELS + j) + x_recv[d, j].astype(f32)
            h_send[d, j] = value.astype(bf16)
        give(h_send.at[d], h_recv.at[chip], hr_sem.at[0], hr_sem.at[1], 2 * d + core)
        return c
    lax.fori_loop(0, CHIPS, give_back, 0)
    lax.fori_loop(5, 7, third, 0)
    second(RING - 1, 0)
    wait_bytes(gate_recv, gate_sem.at[1])
    total = jnp.sum(gate_recv[...], axis=0)
    group_of = lax.shift_right_logical(lax.broadcasted_iota(jnp.int32, (GROUPS, ROWS), 1), 4)
    rest = jnp.where(group_of == lax.broadcasted_iota(jnp.int32, (GROUPS, ROWS), 0), total, 0.0)
    low_bits = jnp.bitwise_and(lax.broadcasted_iota(jnp.int32, (ROWS, BLOCK), 0), GROUP - 1)
    low_lane = jnp.bitwise_and(lax.broadcasted_iota(jnp.int32, (ROWS, BLOCK), 1), GROUP - 1)
    fold = (low_bits == low_lane).astype(f32).astype(bf16)
    folded = jnp.zeros((GROUPS, BLOCK), f32)
    for _ in range(3):
        piece = rest.astype(bf16)
        rest = rest - piece.astype(f32)
        folded = folded + jnp.dot(piece, fold, preferred_element_type=f32)
    for g in range(GROUPS):
        gate_rows[g] = folded[g:g + 1]
    mine = lax.shift_right_logical(lax.broadcasted_iota(jnp.int32, (1, BLOCK), 1), 4) == chip

    for d in range(CHIPS):
        lines = []
        for j in range(LEVELS):
            slot = (2 * d + core) * LEVELS + j
            at = place[slot]
            value = jnp.where(at >= 0, gate_rows[jnp.maximum(at, 0)], 0.0)
            lines.append(jnp.where(mine, value, 0.0))
        gate_slots[d] = jnp.concatenate(lines + [jnp.zeros((2, BLOCK), f32)], axis=0)

    def give_slots(i, c):
        d = (chip + i) % CHIPS
        give(gate_slots.at[d], gate_back.at[chip], gate_sem.at[2], gate_sem.at[3], 2 * d + core)
        return c
    lax.fori_loop(0, CHIPS, give_slots, 0)
    third(RING - 1, 0)

    wait_bytes(g_recv, gr_sem.at[1])
    ug_out[...] = jnp.sum(g_recv[0].astype(f32), axis=0)
    dg_out[...] = jnp.sum(g_recv[1].astype(f32), axis=0)
    wait_bytes(h_recv, hr_sem.at[1])
    for d in range(CHIPS):
        hg_out[:, d] = h_recv[d]
    wait_bytes(sum_recv, sum_sem.at[1])
    wg_out[...] = sum_recv[...].reshape(WIDTH, WIDTH)
    wait_bytes(gate_back, gate_sem.at[3])
    gg_out[...] = jnp.sum(gate_back[...], axis=0)

    for h in range(2):
        wait_bytes(recv_rows[h].at[pl.ds(0, 15 * LEVELS)], in_sem.at[h])
    wait_bytes(recv_rid.at[pl.ds(0, 15)], in_sem.at[2])
    wait_bytes(maps.at[0, pl.ds(0, 3), 0], in_sem.at[4])
    wait_bytes(maps.at[:, pl.ds(0, 3)], map_sem.at[0])

    @pl.when(is_cot)
    def _():
        for h in range(2):
            to_across(h).wait_send()

    @pl.when(jnp.logical_not(is_cot))
    def _():
        to_partner().wait_send()
    for h in range(2):
        for slot in range(1, 7):
            to_right(ring.at[slot, h], slot, h).wait_send()
        to_right(ring.at[7, h], 7, h).wait_send()
    wait_bytes(part_recv.at[pl.ds(0, 15)], p_sem.at[0])
    wait_bytes(proj, p_sem.at[2])
    wait_bytes(g_send.at[pl.ds(0, 15)], gr_sem.at[0])
    wait_bytes(w_send.at[pl.ds(0, 5)], wg_send.at[0])
    wait_bytes(b_send.at[pl.ds(0, 4)], wg_send.at[1])
    wait_bytes(sum_send.at[pl.ds(0, 7)], sum_sem.at[0])
    for d in range(CHIPS):
        to_other(d).wait_send()
    wait_bytes(h_send.at[pl.ds(0, 7)], hr_sem.at[0])
    wait_bytes(gate_recv.at[pl.ds(0, 31)], gate_sem.at[0])
    wait_bytes(gate_slots.at[pl.ds(0, 7)], gate_sem.at[2])


def local(hidden, cotangent, router_gate, recursion_depth, live_counts, out_weight, adapter_down, adapter_up):
    split = (LEVELS, CHIPS, GROUP, WIDTH)
    blocks = lax.shift_right_logical(live_counts, 7)
    slot = jnp.arange(96, dtype=jnp.int32)
    shard = jnp.arange(16, dtype=jnp.int32)
    owner = (slot // LEVELS)[:, None]
    before = jnp.sum(jnp.where(shard[None, :] < owner, blocks[None, :], 0), axis=1)
    own = jnp.sum(jnp.where(shard[None, :] == owner, blocks[None, :], 0), axis=1)
    place = jnp.where(slot % LEVELS < own, before + slot % LEVELS, -1)
    order = jnp.arange(GROUPS, dtype=jnp.int32)
    pick = jnp.sum(jnp.where(place[None, :] == order[:, None], slot[None, :], 0), axis=1)
    vmem = pl.BlockSpec(memory_space=pltpu.VMEM)
    grouped = (GROUPS, GROUP, WIDTH)
    slots = (CHIPS, LEVELS, GROUP, WIDTH)
    dma = pltpu.SemaphoreType.DMA
    out = pl.pallas_call(
        local_kernel,
        out_shape=(
            jax.ShapeDtypeStruct(split, bf16),
            jax.ShapeDtypeStruct((8, BLOCK), f32),
            jax.ShapeDtypeStruct((WIDTH, WIDTH), bf16),
            jax.ShapeDtypeStruct((PIECE, WIDTH), f32),
            jax.ShapeDtypeStruct((PIECE, WIDTH), f32),
        ),
        in_specs=[pl.BlockSpec(memory_space=pltpu.SMEM)] * 2 + [vmem] * 6 + [pl.BlockSpec(memory_space=pl.ANY)],
        out_specs=(vmem,) * 5,
        scratch_shapes=[
            pltpu.VMEM((96, GROUP, HALF), bf16),
            pltpu.VMEM((96, GROUP, HALF), bf16),
            pltpu.VMEM((16, BLOCK), f32),
            pltpu.VMEM((16, 16, BLOCK), f32),
            pltpu.VMEM((96, GROUP, BLOCK), f32),
            pltpu.VMEM((96, GROUP, BLOCK), f32),
            pltpu.VMEM((GROUPS, GROUP, BLOCK), f32),
            pltpu.VMEM((GROUPS, GROUP, BLOCK), f32),
            pltpu.VMEM(grouped, bf16),
            pltpu.VMEM(grouped, bf16),
            pltpu.VMEM(grouped, bf16),
            pltpu.VMEM((RING, 2, GROUPS, GROUP, HALF), bf16),
            pltpu.VMEM((RING, 2, HALF, WIDTH), bf16),
            pltpu.VMEM(grouped, f32),
            pltpu.VMEM((RING, 2, 4, PIECE, WIDTH), bf16),
            pltpu.VMEM((RING, 2, 4, PIECE, WIDTH), bf16),
            pltpu.VMEM((RING, 4, PIECE, WIDTH), bf16),
            pltpu.VMEM((RING, 4, PIECE, WIDTH), bf16),
            pltpu.VMEM((RING, PIECE, WIDTH), bf16),
            pltpu.VMEM((CHIPS, PIECE, WIDTH), bf16),
            pltpu.VMEM((2, 4, 2, PIECE, WIDTH), bf16),
            pltpu.VMEM((ROWS, RANK), bf16),
            pltpu.VMEM((PEERS, PART, RANK), bf16),
            pltpu.VMEM((PART, RANK), bf16),
            pltpu.VMEM((PEERS, PART, RANK), bf16),
            pltpu.VMEM((ROWS, NREC * RANK), bf16),
            pltpu.VMEM((16, PIECE, WIDTH), bf16),
            pltpu.VMEM((2, CHIPS, PIECE, WIDTH), bf16),
            pltpu.VMEM(slots, bf16),
            pltpu.VMEM(slots, bf16),
            pltpu.VMEM(slots, bf16),
            pltpu.VMEM(slots, bf16),
            pltpu.VMEM((1, ROWS), f32),
            pltpu.VMEM((32, 1, ROWS), f32),
            pltpu.VMEM((GROUPS, 1, BLOCK), f32),
            pltpu.VMEM((CHIPS, 8, BLOCK), f32),
            pltpu.VMEM((CHIPS, 8, BLOCK), f32),
            dma((8,)),
            dma((RING,)),
            dma((RING, 2)),
            dma((RING, 2)),
            dma((2,)),
            dma((4,)),
            dma((2,)),
            dma((RING,)),
            dma((RING,)),
            dma((2,)),
            dma((2,)),
            dma((2,)),
            dma((CHIPS,)),
            dma((CHIPS,)),
            dma((2,)),
            dma((4,)),
        ],
        compiler_params=pltpu.CompilerParams(
            collective_id=0, has_side_effects=True, vmem_limit_bytes=VMEM_LIMIT
        ),
    )(
        pick, place, cotangent.reshape(split), hidden.reshape(split),
        router_gate.reshape(LEVELS, BLOCK), recursion_depth.reshape(LEVELS, BLOCK),
        adapter_up, adapter_down.T, out_weight.reshape(PEERS, 2, HALF, WIDTH),
    )
    hidden_grad, gate_back, weight_grad, down_grad, up_grad = out
    hidden_grad = hidden_grad.reshape(hidden.shape).astype(f32)
    return hidden_grad, gate_back[:LEVELS].reshape(-1), weight_grad.astype(f32), down_grad, up_grad


def solution(mesh):
    in_specs = (
        P("seq", "tp"),
        P("seq", "tp"),
        P("seq"),
        P("seq"),
        P(),
        P(None, "tp"),
        P("tp", "seq"),
        P("seq", "tp"),
    )
    out_specs = (P("seq", "tp"), P("seq"), P("seq", "tp"), P("seq", "tp"), P("seq", "tp"))
    return jax.shard_map(local, mesh=mesh, in_specs=in_specs, out_specs=out_specs, check_vma=False)
```

```python
import functools

import jax
import jax.numpy as jnp
from jax import lax
from jax.experimental import pallas as pl
from jax.experimental.pallas import tpu as pltpu
from jax.sharding import PartitionSpec as P

NREC = 4
BLOCK = 128
GROUP = 16
CHIPS = 8
LEVELS = 6
GROUPS = 48
ROWS = GROUPS * GROUP
RING = 8
WIDTH = 512
HALF = WIDTH // 2
RANK = 256
PART = 48
PEERS = 16
PIECE = 64
VMEM_LIMIT = 60 * 1024 * 1024

contract_rows = (((0,), (0,)), ((), ()))
contract_last = (((1,), (1,)), ((), ()))
bf16 = jnp.bfloat16
f32 = jnp.float32


def local_kernel(
    pick, place, cot_ref, hid_ref, gate_ref, depth_ref, up_ref, down_ref, w_ref,
    hg_out, gg_out, wg_out, dg_out, ug_out,
    recv_low, recv_high, rid_send, recv_rid, slot_gate, slot_depth, gates, depths,
    rows, hid, gated_hid, ring, weights, pre,
    w_send, a_recv, b_send, b_recv, sum_send, sum_recv, maps, part_send, part_recv, part_sum, proj, wide,
    g_send, g_recv, x_send, x_recv, h_send, h_recv,
    gate_part, gate_recv, gate_rows, gate_slots, gate_back,
    in_sem, w_sem, ring_send, ring_recv, hid_sem, p_sem, wg_send, wg_recv, b_sem, sum_sem, map_sem,
    gr_sem, x_ssem, x_rsem, hr_sem, gate_sem,
):
    s = lax.axis_index("seq")
    t = lax.axis_index("tp")
    core = s % 2
    chip = s // 2
    z = t // 2
    xl = t % 2
    is_cot = core == xl
    kind = (core + xl) % 2
    x_at = chip // 4
    y_at = chip % 4
    recv_rows = (recv_low, recv_high)

    def remote(src, dst, ssem, rsem, seq, tp):
        return pltpu.make_async_remote_copy(
            src_ref=src, dst_ref=dst, send_sem=ssem, recv_sem=rsem,
            device_id={"seq": seq, "tp": tp}, device_id_type=pl.DeviceIdType.MESH,
        )

    def wait_bytes(ref, sem):
        pltpu.make_async_copy(ref, ref, sem).wait()

    barrier = pltpu.get_barrier_semaphore()

    def greet_tp(i, c):
        for other in range(2):
            pl.semaphore_signal(barrier, inc=1, device_id={"seq": 2 * chip + other, "tp": (t + i) % 16},
                                device_id_type=pl.DeviceIdType.MESH)
        return c
    lax.fori_loop(1, 16, greet_tp, 0)

    def greet_seq(i, c):
        pl.semaphore_signal(barrier, inc=1, device_id={"seq": (s + i) % 16, "tp": t},
                            device_id_type=pl.DeviceIdType.MESH)
        return c
    lax.fori_loop(1, 16, greet_seq, 0)

    def load_weights(j, c):
        pltpu.make_async_copy(w_ref.at[2 * j + core], weights.at[j], w_sem.at[j]).start()
        return c
    lax.fori_loop(0, RING, load_weights, 0)
    pl.semaphore_wait(barrier, 45)

    def give(src, dst, sem_out, sem_in, seq):
        @pl.when(seq == s)
        def _():
            pltpu.make_async_copy(src, dst, sem_in).start()

        @pl.when(seq != s)
        def _():
            remote(src, dst, sem_out, sem_in, seq, t).start()

    my_slots = pl.ds(s * LEVELS, LEVELS)

    def half(h):
        return pl.ds(h * HALF, HALF)

    def send_first(h, i, c):
        d = (chip + i) % CHIPS
        give(cot_ref.at[:, d, :, half(h)], recv_rows[h].at[my_slots], in_sem.at[h], in_sem.at[6 + h], 2 * d + xl)
        return c
    for h in range(2):
        lax.fori_loop(0, CHIPS, functools.partial(send_first, h), 0)

    rid_send[...] = jnp.zeros_like(rid_send)
    rid_send[0:LEVELS] = gate_ref[...].astype(f32)
    rid_send[8:8 + LEVELS] = depth_ref[...].astype(f32)

    def send_rid(i, c):
        d = (chip + i) % CHIPS
        for other in range(2):
            give(rid_send, recv_rid.at[s], in_sem.at[2], in_sem.at[3], 2 * d + other)
        return c
    lax.fori_loop(0, CHIPS, send_rid, 0)

    def send_hid():
        def send(i, c):
            d = (chip + i) % CHIPS
            for h in range(2):
                give(hid_ref.at[:, d, :, half(h)], recv_rows[h].at[my_slots], in_sem.at[h], in_sem.at[6 + h],
                     2 * d + 1 - xl)
            return c
        lax.fori_loop(0, CHIPS, send, 0)

    for x2 in range(2):
        d = 4 * ((x_at + x2) % 2) + y_at
        mine = maps.at[x_at, y_at, core]
        give(up_ref, mine, in_sem.at[4], in_sem.at[5], 2 * d + xl)
        give(down_ref, mine, in_sem.at[4], in_sem.at[5], 2 * d + 1 - xl)

    def to_column(i):
        d = 4 * x_at + (y_at + i) % 4
        return remote(maps.at[:, y_at], maps.at[:, y_at], map_sem.at[0], map_sem.at[1], 2 * d + core, t)

    def pass_maps():
        wait_bytes(maps.at[:, 0], in_sem.at[5])
        for i in range(1, 4):
            to_column(i).start()

    right = 2 * ((z + 1) % RING) + xl
    left = 2 * ((z + RING - 1) % RING) + xl
    across = 2 * z + 1 - xl
    partner = 2 * chip + 1 - core

    def to_right(src, slot, h):
        return remote(src, ring.at[slot, h], ring_send.at[slot, h], ring_recv.at[slot, h], s, right)

    def to_left(src, slot, h):
        return remote(src, ring.at[slot, h], ring_send.at[slot, h], ring_recv.at[slot, h], s, left)

    def to_across(h):
        return remote(ring.at[0, h], ring.at[0, h], ring_send.at[0, h], ring_recv.at[0, h], s, across)

    def to_partner():
        return remote(hid, hid, hid_sem.at[0], hid_sem.at[1], partner, t)

    def forward(i):
        for h in range(2):
            wait_bytes(ring.at[i, h], ring_recv.at[i, h])
            if i < 5 or h == 0:
                to_right(ring.at[i, h], i + 2, h).start()
            wait_bytes(ring.at[i + 1, h], ring_recv.at[i + 1, h])
            if i < 5:
                to_left(ring.at[i + 1, h], i + 3, h).start()
            elif h == 1:
                to_left(ring.at[6, h], 7, h).start()

    @pl.when(is_cot)
    def _():
        for h in range(2):
            wait_bytes(recv_rows[h], in_sem.at[6 + h])

            def pack(g, c):
                value = recv_rows[h][pick[g]]
                rows[g, :, h * HALF:(h + 1) * HALF] = value
                ring[0, h, g] = value
                return c
            lax.fori_loop(0, GROUPS, pack, 0, unroll=4)
            to_across(h).start()
            to_right(ring.at[0, h], 1, h).start()
            to_left(ring.at[0, h], 2, h).start()
        pass_maps()

    @pl.when(jnp.logical_not(is_cot))
    def _():
        pass_maps()
        for h in range(2):
            wait_bytes(ring.at[0, h], ring_recv.at[0, h])
            to_right(ring.at[0, h], 1, h).start()
            to_left(ring.at[0, h], 2, h).start()
    send_hid()

    wait_bytes(recv_rid, in_sem.at[3])
    lane = lax.broadcasted_iota(jnp.int32, (GROUP, BLOCK), 1)
    row = lax.broadcasted_iota(jnp.int32, (GROUP, BLOCK), 0)
    chosen = (lane == chip * GROUP + row).astype(f32).astype(bf16)
    columns = lax.dot_general(chosen, recv_rid[...].reshape(16 * GROUP, BLOCK).astype(bf16), contract_last,
                              preferred_element_type=f32)
    for i in range(16):
        for j in range(LEVELS):
            at = i * GROUP + j
            slot_gate[i * LEVELS + j] = jnp.broadcast_to(columns[:, at:at + 1], (GROUP, BLOCK))
            slot_depth[i * LEVELS + j] = jnp.broadcast_to(columns[:, at + 8:at + 9], (GROUP, BLOCK))

    def pack_rid(g, c):
        gates[g] = slot_gate[pick[g]]
        depths[g] = slot_depth[pick[g]]
        return c
    lax.fori_loop(0, GROUPS, pack_rid, 0, unroll=4)
    pre[...] = jnp.zeros_like(pre)

    forward(1)

    @pl.when(jnp.logical_not(is_cot))
    def _():
        for h in range(2):
            wait_bytes(recv_rows[h], in_sem.at[6 + h])

            def pack(g, c):
                value = recv_rows[h][pick[g]]
                rows[g, :, h * HALF:(h + 1) * HALF] = value
                hid[g, :, h * HALF:(h + 1) * HALF] = value
                return c
            lax.fori_loop(0, GROUPS, pack, 0, unroll=4)
        to_partner().start()

    wait_bytes(maps.at[:, pl.ds(0, 3)], map_sem.at[1])

    def project(r, c):
        groups = pl.ds(r * GROUP, GROUP)
        x = rows[groups].reshape(RANK, WIDTH)
        y = lax.dot_general(x, maps[...].reshape(NREC * RANK, WIDTH), contract_last, preferred_element_type=f32)
        depth = depths[groups].reshape(RANK, BLOCK)[:, 0:1]
        total = jnp.zeros((RANK, RANK), f32)
        for d in range(NREC):
            total = total + jnp.where(depth == d + 1.0, y[:, d * RANK:(d + 1) * RANK], 0.0)
        part_send[pl.ds(r * RANK, RANK)] = total.astype(bf16)
        return c
    lax.fori_loop(0, ROWS // RANK, project, 0)

    def same_kind(t2):
        return 2 * chip + (core + xl + t2) % 2

    def send_part(i, c):
        t2 = (t + i) % PEERS
        remote(part_send.at[pl.ds(t2 * PART, PART)], part_recv.at[t], p_sem.at[0], p_sem.at[1],
               same_kind(t2), t2).start()
        return c
    lax.fori_loop(1, PEERS, send_part, 0)
    pltpu.make_async_copy(part_send.at[pl.ds(t * PART, PART)], part_recv.at[t], p_sem.at[1]).start()

    @pl.when(is_cot)
    def _():
        wait_bytes(hid, hid_sem.at[1])

    def apply_gate(g, c):
        gate = gates[g][:, 0:1]
        gated_hid[g] = (gate * hid[g].astype(f32)).astype(bf16)
        rows[g] = (gate * rows[g].astype(f32)).astype(bf16)
        return c
    lax.fori_loop(0, GROUPS, apply_gate, 0, unroll=4)

    def origin_of(i):
        shift = jnp.where(i % 2 == 1, 2 * RING - (i + 1) // 2, i // 2)
        return (z + shift) % RING

    def compute(i, c):
        origin = origin_of(i)
        pltpu.make_async_copy(w_ref.at[0], weights.at[origin], w_sem.at[origin]).wait()
        for h in range(2):
            w_send[i, h] = lax.dot_general(
                ring[i, h].reshape(ROWS, HALF), gated_hid[...].reshape(ROWS, WIDTH), contract_rows,
                preferred_element_type=f32).astype(bf16).reshape(4, PIECE, WIDTH)

        @pl.when(i % 2 == 1)
        def _():
            remote(w_send.at[i, 1 - x_at], a_recv.at[i, 0], wg_send.at[0], wg_recv.at[i],
                   2 * (4 * (1 - x_at) + y_at) + core, t).start()

        @pl.when(i % 2 == 0)
        def _():
            def scatter(j, c):
                y2 = (y_at + j) % 4
                give(w_send.at[i, :, y2], a_recv.at[i, :, y_at], wg_send.at[0], wg_recv.at[i],
                     2 * (4 * x_at + y2) + core)
                return c
            lax.fori_loop(0, 4, scatter, 0)
        term = jnp.dot(ring[i, 0].reshape(ROWS, HALF), weights[origin, 0], preferred_element_type=f32)
        term = term + jnp.dot(ring[i, 1].reshape(ROWS, HALF), weights[origin, 1], preferred_element_type=f32)
        pre[...] = pre[...] + term.reshape(GROUPS, GROUP, WIDTH)
        return c

    def second(i, c):
        @pl.when(i % 2 == 1)
        def _():
            wait_bytes(a_recv.at[i, 0], wg_recv.at[i])
            b_send[i] = (w_send[i, x_at].astype(f32) + a_recv[i, 0].astype(f32)).astype(bf16)

            def scatter(j, c):
                y2 = (y_at + j) % 4
                give(b_send.at[i, y2], b_recv.at[i, y_at], wg_send.at[1], b_sem.at[i],
                     2 * (4 * x_at + y2) + core)
                return c
            lax.fori_loop(0, 4, scatter, 0)

        @pl.when(i % 2 == 0)
        def _():
            wait_bytes(a_recv.at[i], wg_recv.at[i])
            for x2 in range(2):
                b_send[i, x2] = jnp.sum(a_recv[i, x2].astype(f32), axis=0).astype(bf16)
            remote(b_send.at[i, 1 - x_at], b_recv.at[i, 0], wg_send.at[1], b_sem.at[i],
                   2 * (4 * (1 - x_at) + y_at) + core, t).start()
        return c

    def third(i, c):
        @pl.when(i % 2 == 1)
        def _():
            wait_bytes(b_recv.at[i], b_sem.at[i])
            sum_send[i] = jnp.sum(b_recv[i].astype(f32), axis=0).astype(bf16)

        @pl.when(i % 2 == 0)
        def _():
            wait_bytes(b_recv.at[i, 0], b_sem.at[i])
            sum_send[i] = (b_send[i, x_at].astype(f32) + b_recv[i, 0].astype(f32)).astype(bf16)
        give(sum_send.at[i], sum_recv.at[chip], sum_sem.at[0], sum_sem.at[1], 2 * origin_of(i) + core)
        return c

    def sum_parts():
        wait_bytes(part_recv, p_sem.at[1])
        part_sum[...] = jnp.sum(part_recv[...].astype(f32), axis=0).astype(bf16)

        def send_sum(j, c):
            t2 = (t + j) % PEERS
            remote(part_sum, proj.at[t], p_sem.at[2], p_sem.at[3],
                   4 * chip + 1 - same_kind(t2), t2).start()
            return c
        lax.fori_loop(0, PEERS, send_sum, 0)

    def grads():
        wait_bytes(proj, p_sem.at[3])
        flat = proj[...].reshape(ROWS, RANK)
        depth = depths[...].reshape(ROWS, BLOCK)[:, 0:1]
        for d in range(NREC):
            wide[:, d * RANK:(d + 1) * RANK] = jnp.where(
                depth == d + 1.0, 0.5 * flat.astype(f32), 0.0).astype(bf16)

        @pl.when(jnp.logical_not(is_cot))
        def _():
            def add_adapter(r, c):
                groups = pl.ds(r * GROUP, GROUP)
                term = jnp.dot(wide[pl.ds(r * RANK, RANK)], maps[...].reshape(NREC * RANK, WIDTH),
                               preferred_element_type=f32)
                pre[groups] = pre[groups] + term.reshape(GROUP, GROUP, WIDTH)
                return c
            lax.fori_loop(0, ROWS // RANK, add_adapter, 0)

        for q in range(NREC):
            grad = lax.dot_general(wide[:, q * RANK:(q + 1) * RANK], rows[...].reshape(ROWS, WIDTH),
                                   contract_rows, preferred_element_type=f32)
            g_send[q * 4:(q + 1) * 4] = grad.astype(bf16).reshape(4, PIECE, WIDTH)

        def send_grad(j, c):
            to = (s + j) % 16
            remote(g_send.at[to], g_recv.at[kind, chip], gr_sem.at[0], gr_sem.at[1], to, t).start()
            return c
        lax.fori_loop(1, 16, send_grad, 0)
        pltpu.make_async_copy(g_send.at[s], g_recv.at[kind, chip], gr_sem.at[1]).start()

    def run(i, c):
        @pl.when(i == 3)
        def _():
            forward(3)

        @pl.when(i == 5)
        def _():
            forward(5)

        @pl.when(i == RING - 1)
        def _():
            lax.fori_loop(5, 7, second, 0)
            lax.fori_loop(2, 5, third, 0)
            for h in range(2):
                wait_bytes(ring.at[RING - 1, h], ring_recv.at[RING - 1, h])

        compute(i, c)

        @pl.when(i == RING - 1)
        def _():
            pl.when(is_cot)(grads)

        @pl.when(i == 4)
        def _():
            pl.when(jnp.logical_not(is_cot))(sum_parts)
            lax.fori_loop(0, 2, second, 0)
            pl.when(jnp.logical_not(is_cot))(grads)

        @pl.when(i == 6)
        def _():
            lax.fori_loop(2, 5, second, 0)
            lax.fori_loop(0, 2, third, 0)
        return c
    pl.when(is_cot)(sum_parts)
    lax.fori_loop(0, RING, run, 0)

    ones = jnp.ones((8, WIDTH), bf16)
    for r in range(ROWS // RANK):
        groups = slice(r * GROUP, (r + 1) * GROUP)
        prod = pre[groups].reshape(RANK, WIDTH) * hid[groups].reshape(RANK, WIDTH).astype(f32)
        high = prod.astype(bf16)
        low = (prod - high.astype(f32)).astype(bf16)
        lanes = lax.dot_general(ones, high, contract_last, preferred_element_type=f32)
        lanes = lanes + lax.dot_general(ones, low, contract_last, preferred_element_type=f32)
        gate_part[:, r * RANK:(r + 1) * RANK] = lanes[0:1]
    me = 2 * t + core

    def send_gate(j, c):
        t2 = (t + j) % PEERS
        for other in range(2):
            remote(gate_part, gate_recv.at[me], gate_sem.at[0], gate_sem.at[1], 2 * chip + other, t2).start()
        return c
    lax.fori_loop(1, PEERS, send_gate, 0)
    remote(gate_part, gate_recv.at[me], gate_sem.at[0], gate_sem.at[1], partner, t).start()
    pltpu.make_async_copy(gate_part, gate_recv.at[me], gate_sem.at[1]).start()

    def slot_rows(slot):
        gate = slot_gate[slot][:, 0:1]
        at = place[slot]
        return jnp.where(at >= 0, gate * pre[jnp.maximum(at, 0)], 0.0)

    def to_other(d):
        return remote(x_send.at[d], x_recv.at[d], x_ssem.at[d], x_rsem.at[d], partner, t)

    def expand(i, c):
        d = (chip + i) % CHIPS
        for j in range(LEVELS):
            x_send[d, j] = slot_rows((2 * d + 1 - core) * LEVELS + j).astype(bf16)
        to_other(d).start()
        return c
    lax.fori_loop(0, CHIPS, expand, 0)

    def give_back(i, c):
        d = (chip + i) % CHIPS
        wait_bytes(x_recv.at[d], x_rsem.at[d])
        for j in range(LEVELS):
            value = slot_rows((2 * d + core) * LEVELS + j) + x_recv[d, j].astype(f32)
            h_send[d, j] = value.astype(bf16)
        give(h_send.at[d], h_recv.at[chip], hr_sem.at[0], hr_sem.at[1], 2 * d + core)
        return c
    lax.fori_loop(0, CHIPS, give_back, 0)
    lax.fori_loop(5, 7, third, 0)
    second(RING - 1, 0)
    wait_bytes(gate_recv, gate_sem.at[1])
    total = jnp.sum(gate_recv[...], axis=0)
    group_of = lax.shift_right_logical(lax.broadcasted_iota(jnp.int32, (GROUPS, ROWS), 1), 4)
    rest = jnp.where(group_of == lax.broadcasted_iota(jnp.int32, (GROUPS, ROWS), 0), total, 0.0)
    low_bits = jnp.bitwise_and(lax.broadcasted_iota(jnp.int32, (ROWS, BLOCK), 0), GROUP - 1)
    low_lane = jnp.bitwise_and(lax.broadcasted_iota(jnp.int32, (ROWS, BLOCK), 1), GROUP - 1)
    fold = (low_bits == low_lane).astype(f32).astype(bf16)
    folded = jnp.zeros((GROUPS, BLOCK), f32)
    for _ in range(3):
        piece = rest.astype(bf16)
        rest = rest - piece.astype(f32)
        folded = folded + jnp.dot(piece, fold, preferred_element_type=f32)
    for g in range(GROUPS):
        gate_rows[g] = folded[g:g + 1]
    mine = lax.shift_right_logical(lax.broadcasted_iota(jnp.int32, (1, BLOCK), 1), 4) == chip

    for d in range(CHIPS):
        lines = []
        for j in range(LEVELS):
            slot = (2 * d + core) * LEVELS + j
            at = place[slot]
            value = jnp.where(at >= 0, gate_rows[jnp.maximum(at, 0)], 0.0)
            lines.append(jnp.where(mine, value, 0.0))
        gate_slots[d] = jnp.concatenate(lines + [jnp.zeros((2, BLOCK), f32)], axis=0)

    def give_slots(i, c):
        d = (chip + i) % CHIPS
        give(gate_slots.at[d], gate_back.at[chip], gate_sem.at[2], gate_sem.at[3], 2 * d + core)
        return c
    lax.fori_loop(0, CHIPS, give_slots, 0)
    third(RING - 1, 0)

    wait_bytes(g_recv, gr_sem.at[1])
    ug_out[...] = jnp.sum(g_recv[0].astype(f32), axis=0)
    dg_out[...] = jnp.sum(g_recv[1].astype(f32), axis=0)
    wait_bytes(h_recv, hr_sem.at[1])
    for d in range(CHIPS):
        hg_out[:, d] = h_recv[d]
    wait_bytes(sum_recv, sum_sem.at[1])
    wg_out[...] = sum_recv[...].reshape(WIDTH, WIDTH)
    wait_bytes(gate_back, gate_sem.at[3])
    gg_out[...] = jnp.sum(gate_back[...], axis=0)

    for h in range(2):
        wait_bytes(recv_rows[h].at[pl.ds(0, 15 * LEVELS)], in_sem.at[h])
    wait_bytes(recv_rid.at[pl.ds(0, 15)], in_sem.at[2])
    wait_bytes(maps.at[0, pl.ds(0, 3), 0], in_sem.at[4])
    wait_bytes(maps.at[:, pl.ds(0, 3)], map_sem.at[0])

    @pl.when(is_cot)
    def _():
        for h in range(2):
            to_across(h).wait_send()

    @pl.when(jnp.logical_not(is_cot))
    def _():
        to_partner().wait_send()
    for h in range(2):
        for slot in range(1, 7):
            to_right(ring.at[slot, h], slot, h).wait_send()
        to_right(ring.at[7, h], 7, h).wait_send()
    wait_bytes(part_recv.at[pl.ds(0, 15)], p_sem.at[0])
    wait_bytes(proj, p_sem.at[2])
    wait_bytes(g_send.at[pl.ds(0, 15)], gr_sem.at[0])
    wait_bytes(w_send.at[pl.ds(0, 5)], wg_send.at[0])
    wait_bytes(b_send.at[pl.ds(0, 4)], wg_send.at[1])
    wait_bytes(sum_send.at[pl.ds(0, 7)], sum_sem.at[0])
    for d in range(CHIPS):
        to_other(d).wait_send()
    wait_bytes(h_send.at[pl.ds(0, 7)], hr_sem.at[0])
    wait_bytes(gate_recv.at[pl.ds(0, 31)], gate_sem.at[0])
    wait_bytes(gate_slots.at[pl.ds(0, 7)], gate_sem.at[2])


def local(hidden, cotangent, router_gate, recursion_depth, live_counts, out_weight, adapter_down, adapter_up):
    split = (LEVELS, CHIPS, GROUP, WIDTH)
    blocks = lax.shift_right_logical(live_counts, 7)
    slot = jnp.arange(96, dtype=jnp.int32)
    shard = jnp.arange(16, dtype=jnp.int32)
    owner = (slot // LEVELS)[:, None]
    before = jnp.sum(jnp.where(shard[None, :] < owner, blocks[None, :], 0), axis=1)
    own = jnp.sum(jnp.where(shard[None, :] == owner, blocks[None, :], 0), axis=1)
    place = jnp.where(slot % LEVELS < own, before + slot % LEVELS, -1)
    order = jnp.arange(GROUPS, dtype=jnp.int32)
    pick = jnp.sum(jnp.where(place[None, :] == order[:, None], slot[None, :], 0), axis=1)
    vmem = pl.BlockSpec(memory_space=pltpu.VMEM)
    grouped = (GROUPS, GROUP, WIDTH)
    slots = (CHIPS, LEVELS, GROUP, WIDTH)
    dma = pltpu.SemaphoreType.DMA
    out = pl.pallas_call(
        local_kernel,
        out_shape=(
            jax.ShapeDtypeStruct(split, bf16),
            jax.ShapeDtypeStruct((8, BLOCK), f32),
            jax.ShapeDtypeStruct((WIDTH, WIDTH), bf16),
            jax.ShapeDtypeStruct((PIECE, WIDTH), f32),
            jax.ShapeDtypeStruct((PIECE, WIDTH), f32),
        ),
        in_specs=[pl.BlockSpec(memory_space=pltpu.SMEM)] * 2 + [vmem] * 6 + [pl.BlockSpec(memory_space=pl.ANY)],
        out_specs=(vmem,) * 5,
        scratch_shapes=[
            pltpu.VMEM((96, GROUP, HALF), bf16),
            pltpu.VMEM((96, GROUP, HALF), bf16),
            pltpu.VMEM((16, BLOCK), f32),
            pltpu.VMEM((16, 16, BLOCK), f32),
            pltpu.VMEM((96, GROUP, BLOCK), f32),
            pltpu.VMEM((96, GROUP, BLOCK), f32),
            pltpu.VMEM((GROUPS, GROUP, BLOCK), f32),
            pltpu.VMEM((GROUPS, GROUP, BLOCK), f32),
            pltpu.VMEM(grouped, bf16),
            pltpu.VMEM(grouped, bf16),
            pltpu.VMEM(grouped, bf16),
            pltpu.VMEM((RING, 2, GROUPS, GROUP, HALF), bf16),
            pltpu.VMEM((RING, 2, HALF, WIDTH), bf16),
            pltpu.VMEM(grouped, f32),
            pltpu.VMEM((RING, 2, 4, PIECE, WIDTH), bf16),
            pltpu.VMEM((RING, 2, 4, PIECE, WIDTH), bf16),
            pltpu.VMEM((RING, 4, PIECE, WIDTH), bf16),
            pltpu.VMEM((RING, 4, PIECE, WIDTH), bf16),
            pltpu.VMEM((RING, PIECE, WIDTH), bf16),
            pltpu.VMEM((CHIPS, PIECE, WIDTH), bf16),
            pltpu.VMEM((2, 4, 2, PIECE, WIDTH), bf16),
            pltpu.VMEM((ROWS, RANK), bf16),
            pltpu.VMEM((PEERS, PART, RANK), bf16),
            pltpu.VMEM((PART, RANK), bf16),
            pltpu.VMEM((PEERS, PART, RANK), bf16),
            pltpu.VMEM((ROWS, NREC * RANK), bf16),
            pltpu.VMEM((16, PIECE, WIDTH), bf16),
            pltpu.VMEM((2, CHIPS, PIECE, WIDTH), bf16),
            pltpu.VMEM(slots, bf16),
            pltpu.VMEM(slots, bf16),
            pltpu.VMEM(slots, bf16),
            pltpu.VMEM(slots, bf16),
            pltpu.VMEM((1, ROWS), f32),
            pltpu.VMEM((32, 1, ROWS), f32),
            pltpu.VMEM((GROUPS, 1, BLOCK), f32),
            pltpu.VMEM((CHIPS, 8, BLOCK), f32),
            pltpu.VMEM((CHIPS, 8, BLOCK), f32),
            dma((8,)),
            dma((RING,)),
            dma((RING, 2)),
            dma((RING, 2)),
            dma((2,)),
            dma((4,)),
            dma((2,)),
            dma((RING,)),
            dma((RING,)),
            dma((2,)),
            dma((2,)),
            dma((2,)),
            dma((CHIPS,)),
            dma((CHIPS,)),
            dma((2,)),
            dma((4,)),
        ],
        compiler_params=pltpu.CompilerParams(
            collective_id=0, has_side_effects=True, vmem_limit_bytes=VMEM_LIMIT
        ),
    )(
        pick, place, cotangent.reshape(split), hidden.reshape(split),
        router_gate.reshape(LEVELS, BLOCK), recursion_depth.reshape(LEVELS, BLOCK),
        adapter_up, adapter_down.T, out_weight.reshape(PEERS, 2, HALF, WIDTH),
    )
    hidden_grad, gate_back, weight_grad, down_grad, up_grad = out
    hidden_grad = hidden_grad.reshape(hidden.shape).astype(f32)
    return hidden_grad, gate_back[:LEVELS].reshape(-1), weight_grad.astype(f32), down_grad, up_grad


def solution(mesh):
    in_specs = (
        P("seq", "tp"),
        P("seq", "tp"),
        P("seq"),
        P("seq"),
        P(),
        P(None, "tp"),
        P("tp", "seq"),
        P("seq", "tp"),
    )
    out_specs = (P("seq", "tp"), P("seq"), P("seq", "tp"), P("seq", "tp"), P("seq", "tp"))
    return jax.shard_map(local, mesh=mesh, in_specs=in_specs, out_specs=out_specs, check_vma=False)
```
